32 devices in a mesh: row: 4 (over y, x), col: 8 (over z, core).
Axes of the slice: x: 2, y: 2, z: 4, core: 2. Of those that a mesh axis runs over, the one named last changes fastest.
Arguments:
- rhs: float32 [4, 8, 4608], P('row', 'col'), may hold values from -14 to 14
- friction: float32 [4, 8, 4608], P('row', 'col'), may hold values from 1 to 4
- kernel_tiles: bfloat16 [4, 8, 256, 128, 128], P('row', 'col'), may hold values from -0.1875 to 0.1875
- tile_scale: float32 [4, 8, 256], P('row', 'col'), may hold values from 0.5 to 2
- tile_row: int32 [4, 8, 256], P('row', 'col'), may hold values from 0 to 287, as said below
- tile_col: int32 [4, 8, 256], P('row', 'col'), may hold values from 0 to 143
- tile_counts: int32 [4, 8], P('row', 'col'), may hold values from 64 to 256, as said below
- precond_blocks: bfloat16 [4, 8, 24, 512, 512], P('row', 'col'), may hold values from -3 to 3, as said below
- fault_sizes: int32 [4, 8, 24], P('row', 'col'), may hold values from 1 to 512, 4608 in all within a row
Outputs:
- update: float32 [4, 8, 4608], P('row', 'col')
- residual: float32 [4, 8, 4608], P('row', 'col')
The draws below stay inside these ranges and needn't reach their ends.
Inputs may be any that keep to these rules, and one draw needn't show every extreme that they name: Row tile within the row group; in every block (r, c), over all 256 slots, at most 64 slots have the same tile_row // 36, and some value of it has exactly 64. `tile_counts`: slots at or beyond the count hold no kernel tile and are ignored; some block has 256 live slots and some 256 // 4. `fault_sizes`: the faults of each (r, c) cover its 4608 elements in order; each (r, c) has a fault of exactly 512 elements. `precond_blocks`: entries of a block outside its fault's size are ignored.
All inputs are finite; a program needn't handle non-finite values.
Results may differ from the reference program's by a relative error of at most 0.012.
Values may be sent and summed in bfloat16 or wider, within the bound.
No kernel may reach another device: no remote copies, remote signals or barrier semaphores. Data moves between devices by JAX's collectives and lax.ppermute only.
A program may use at most 64 MiB of HBM per device.

```python
import math
import jax
import jax.numpy as jnp
import numpy as np
from jax import lax

TILE = 128
FMAX = 512
ITERS = 3
EL_DEV = 4608
TILES_DEV = 256
FAULTS_DEV = 24
TR_GRP = 288
TC_GRP = 144
N_ROW = 4
N_COL = 8


def draw_rhs(key, part):
    draw_shape = (N_ROW, N_COL, EL_DEV)
    key_value, key_scale = jax.random.split(key)
    spread = jnp.exp(jax.random.uniform(key_scale, draw_shape, jnp.float32) * 2.302585) / 3.0
    values = jax.random.truncated_normal(key_value, -4.0, 4.0, draw_shape, jnp.float32)
    return values * spread


def draw_tile_counts(key, part):
    counts = jax.random.randint(key, (N_ROW * N_COL,), TILES_DEV // 4, TILES_DEV + 1)
    chosen = jax.random.permutation(jax.random.fold_in(key, 7), N_ROW * N_COL)
    counts = counts.at[chosen[0]].set(TILES_DEV).at[chosen[1]].set(TILES_DEV // 4)
    return counts.reshape(N_ROW, N_COL).astype(jnp.int32)


def draw_tile_row(key, part):
    seg_tiles = EL_DEV // TILE
    capacity = max(2, 2 * TILES_DEV // N_COL)

    def one_block(block_key):
        key_full, key_pick, key_order, key_local = jax.random.split(block_key, 4)
        full_owner = jax.random.randint(key_full, (), 0, N_COL)
        copies = jnp.arange((N_COL - 1) * capacity, dtype=jnp.int32) // capacity
        others = (full_owner + 1 + copies) % N_COL
        picked = jax.random.permutation(key_pick, others)[:TILES_DEV - capacity]
        owners = jnp.concatenate([jnp.full((capacity,), full_owner, jnp.int32), picked.astype(jnp.int32)])
        owners = jax.random.permutation(key_order, owners)
        local_tile = jax.random.randint(key_local, (TILES_DEV,), 0, seg_tiles)
        return (owners * seg_tiles + local_tile).astype(jnp.int32)
    block_keys = jax.random.split(jax.random.fold_in(key, 11), N_ROW * N_COL)
    return jax.vmap(one_block)(block_keys).reshape(N_ROW, N_COL, TILES_DEV).astype(jnp.int32)


def draw_precond_blocks(key, part):
    draw_shape = (N_ROW, N_COL, FAULTS_DEV, FMAX, FMAX)
    key_noise, key_diag = jax.random.split(key)
    noise_part = jax.random.normal(key_noise, draw_shape, jnp.float32)
    diagonal_part = 1.0 + 0.5 * jax.random.uniform(key_diag, (N_ROW, N_COL, FAULTS_DEV, FMAX), jnp.float32)
    places = lax.broadcasted_iota(jnp.int32, (FMAX, FMAX), 0) == lax.broadcasted_iota(jnp.int32, (FMAX, FMAX), 1)
    return jnp.where(places, diagonal_part[..., None], 0.4 / jnp.sqrt(1.0 * FMAX) * noise_part).astype(jnp.bfloat16)


def place_ends(values, rng, smallest, high):
    spot = [jax.random.randint(jax.random.fold_in(rng, axis), (), 0, length) for axis, length in enumerate(values.shape)]
    longest = values.shape.index(max(values.shape))
    beside = spot[:longest] + [(spot[longest] + 1) % values.shape[longest]] + spot[longest + 1:]
    return values.at[tuple(spot)].set(smallest).at[tuple(beside)].set(high)


def shard_levels(stream_key, extent, cuts, least, largest):
    loudness = 1.0
    for position, parts in cuts:
        steps = jax.random.uniform(jax.random.fold_in(jax.random.fold_in(stream_key, 6), position), (parts,), jnp.float32, least / len(cuts), largest / len(cuts))
        loudness = loudness * jnp.repeat(jnp.exp(steps), extent[position] // parts).reshape((-1,) + (1,) * (len(extent) - 1 - position))
    return loudness


def length_profile(count, total, bound, slope):
    portions = [(1 << 20) // math.isqrt(grade ** slope) + 1 for grade in range(2, count + 1)]
    rest, holding = total - bound - (count - 1), [1] * (count - 1)
    while rest > 0:
        free = [i for i in range(count - 1) if holding[i] < bound]
        whole, remaining = sum([portions[i] for i in free]), rest
        for i in free:
            addition = min(bound - holding[i], max(1, remaining * portions[i] // whole), rest)
            holding[i] = holding[i] + addition
            rest = rest - addition
    return np.array([bound] + holding)


def ragged(key, number_of, total, most, lean):
    if number_of == 2:
        one = jax.random.randint(key, (), max(1, total - most), min(most, total - 1) + 1)
        return jnp.stack([one, total - one])
    tallies = jnp.asarray(length_profile(number_of, total, most, lean), jnp.int32)
    twos = (number_of - 1) // 2
    source_of, receiver = tallies[1:1 + 2 * twos:2], tallies[2:2 + 2 * twos:2]
    slack = jnp.minimum(source_of - 1, most - receiver)
    passed = jax.random.randint(jax.random.fold_in(key, 1), (twos,), 0, 1 << 20) % (slack + 1)
    tallies = tallies.at[1:1 + 2 * twos:2].set(source_of - passed).at[2:2 + 2 * twos:2].set(receiver + passed)
    return tallies[jax.random.permutation(jax.random.fold_in(key, 2), number_of)]


def bell_draw(key, extent, width, bound, pieces=(), held_as=jnp.bfloat16):
    level = shard_levels(key, extent, pieces, -0.22, 0.18) if pieces else 1.0
    values = jax.random.normal(key, extent, jnp.float32) * width * level
    return jnp.minimum(jnp.maximum(values, -bound), bound).astype(held_as)


def setup_inputs(seed: int = 0) -> dict:
    arg_keys = jax.random.split(jax.random.key(seed), 10)
    rhs = draw_rhs(jax.random.fold_in(arg_keys[9], 71), 0)
    friction = jnp.clip(jnp.exp(math.log(4.0) - 1.3862944 * jax.random.uniform(arg_keys[1], (N_ROW, N_COL, EL_DEV), jnp.float32) ** shard_levels(arg_keys[1], (N_ROW, N_COL, EL_DEV), ((0, 4), (1, 8)), -0.2, 0.2)), 1.0, 4.0)
    kernel_tiles = bell_draw(arg_keys[2], (N_ROW, N_COL, TILES_DEV, TILE, TILE), (TILES_DEV * TILE * N_COL // TR_GRP) ** -0.5, 0.1875, ((0, 4), (1, 8)))
    tile_scale = jnp.clip(jnp.exp(math.log(2.0) - 1.3862944 * jax.random.uniform(arg_keys[3], (N_ROW, N_COL, TILES_DEV), jnp.float32) ** shard_levels(arg_keys[3], (N_ROW, N_COL, TILES_DEV), ((0, 4), (1, 8)), -0.2, 0.2)), 0.5, 2.0)
    tile_row = draw_tile_row(jax.random.fold_in(arg_keys[9], 71), 0)
    tile_col = place_ends(jax.random.randint(arg_keys[5], (N_ROW, N_COL, TILES_DEV), 0, TC_GRP), jax.random.fold_in(arg_keys[5], 1), 0, TC_GRP - 1).astype(jnp.int32)
    tile_counts = draw_tile_counts(jax.random.fold_in(arg_keys[9], 71), 0)
    precond_blocks = draw_precond_blocks(jax.random.fold_in(arg_keys[9], 71), 0)
    fault_sizes = jax.vmap(lambda own: ragged(own, FAULTS_DEV, EL_DEV, FMAX, 2))(jax.random.split(arg_keys[8], N_ROW * N_COL)).reshape((N_ROW, N_COL, FAULTS_DEV)).astype(jnp.int32)
    return {"rhs": rhs, "friction": friction, "kernel_tiles": kernel_tiles, "tile_scale": tile_scale, "tile_row": tile_row, "tile_col": tile_col, "tile_counts": tile_counts, "precond_blocks": precond_blocks, "fault_sizes": fault_sizes}


exact_mode = lax.Precision.HIGHEST

def stretch_precond(vector_stretch, fault_blocks, fault_len):
    fault_starts = (jnp.cumsum(fault_len) - fault_len).astype(jnp.int32)
    slot_place = jnp.arange(FMAX, dtype=jnp.int32)
    gather_spot = jnp.clip(fault_starts[:, None] + slot_place[None, :], 0, EL_DEV - 1).astype(jnp.int32)
    slot_live = slot_place[None, :] < fault_len[:, None]
    padded = jnp.where(slot_live, vector_stretch[gather_spot], jnp.zeros((), vector_stretch.dtype))
    result = jnp.einsum('fij,fj->fi', fault_blocks.astype(jnp.float32), padded.astype(jnp.float32))
    element_ids = jnp.arange(EL_DEV, dtype=jnp.int32)
    owner_fault = lax.optimization_barrier(jnp.sum((fault_starts[None, :] <= element_ids[:, None]).astype(jnp.int32), axis=1)).astype(jnp.int32) - 1
    flat_spot = (owner_fault * FMAX + element_ids - fault_starts[owner_fault]).astype(jnp.int32)
    return result.reshape(-1)[flat_spot]

def precondition(vector, precond_blocks, fault_sizes):
    flat_vector = vector.astype(jnp.bfloat16).reshape(N_ROW * N_COL, EL_DEV)
    flat_blocks = precond_blocks.reshape(N_ROW * N_COL, FAULTS_DEV, FMAX, FMAX)
    flat_sizes = fault_sizes.reshape(N_ROW * N_COL, FAULTS_DEV)
    output = lax.map(lambda item: stretch_precond(item[0], item[1], item[2]), (flat_vector, flat_blocks, flat_sizes))
    return output.reshape(N_ROW, N_COL, EL_DEV)

def kernel_apply(field, kernel_tiles, tile_scale, tile_row, tile_col, tile_counts):
    low_field = field.astype(jnp.bfloat16)

    def one_row(row_id):

        def one_col(row_total, col_id):
            column = lax.dynamic_index_in_dim(low_field, col_id, 1, keepdims=False)
            column_pieces = column.reshape(TC_GRP, TILE)[tile_col[row_id, col_id]]
            live_slots = (jnp.arange(TILES_DEV, dtype=jnp.int32) < tile_counts[row_id, col_id]).astype(jnp.float32)
            products = jnp.einsum('tij,tj->ti', kernel_tiles[row_id, col_id].astype(jnp.float32), column_pieces.astype(jnp.float32))
            products = products * (tile_scale[row_id, col_id] * live_slots)[:, None]
            return (row_total + jax.ops.segment_sum(products, tile_row[row_id, col_id], num_segments=TR_GRP), None)
        row_total, _ = lax.scan(one_col, jnp.zeros((TR_GRP, TILE), jnp.float32), jnp.arange(N_COL, dtype=jnp.int32))
        return row_total.reshape(N_COL, EL_DEV)
    return lax.map(one_row, jnp.arange(N_ROW, dtype=jnp.int32))

def reference(rhs, friction, kernel_tiles, tile_scale, tile_row, tile_col, tile_counts, precond_blocks, fault_sizes):

    def operator(field):
        return friction * field + kernel_apply(field, kernel_tiles, tile_scale, tile_row, tile_col, tile_counts)
    rhs_norm = jnp.sqrt(jnp.sum(rhs * rhs))
    krylov = [(rhs / rhs_norm).reshape(-1)]
    directions = []
    hessenberg = jnp.zeros((ITERS + 1, ITERS), jnp.float32)
    for step in range(ITERS):
        direction = precondition(krylov[step].reshape(N_ROW, N_COL, EL_DEV), precond_blocks, fault_sizes)
        directions.append(direction.reshape(-1))
        image = operator(direction).reshape(-1)
        basis_stack = jnp.stack(krylov)
        heights = jnp.dot(basis_stack, image, precision=exact_mode)
        image = image - jnp.dot(heights, basis_stack, precision=exact_mode)
        new_norm = jnp.sqrt(jnp.sum(image * image))
        hessenberg = hessenberg.at[:step + 1, step].set(heights).at[step + 1, step].set(new_norm)
        krylov.append(image / new_norm)
    gram_matrix = jnp.dot(hessenberg.T, hessenberg, precision=exact_mode)
    target = rhs_norm * hessenberg[0, :]
    lower_factor = jnp.linalg.cholesky(gram_matrix)
    weights_y = jax.scipy.linalg.cho_solve((lower_factor, True), target)
    update = jnp.dot(weights_y, jnp.stack(directions), precision=exact_mode).reshape(N_ROW, N_COL, EL_DEV)
    residual = rhs - operator(update)
    return (update, residual)
```

```python
import jax
import jax.numpy as jnp
from jax import lax
from jax.experimental import pallas as pl
from jax.experimental.pallas import tpu as pltpu
from jax.sharding import PartitionSpec as P

LANES = 128
F32 = jnp.float32
BF16 = jnp.bfloat16
VMEM = pl.BlockSpec(memory_space=pltpu.VMEM)
SMEM = pl.BlockSpec(memory_space=pltpu.SMEM)
ANY = pl.BlockSpec(memory_space=pl.ANY)
PARAMS = pltpu.CompilerParams(vmem_limit_bytes=48 << 20)


def dot_nt(left, right):
    return lax.dot_general(left, right, (((1,), (1,)), ((), ())), preferred_element_type=F32)


def split(value):
    high = value.astype(BF16)
    low = (value - high.astype(F32)).astype(BF16)
    return high, low


def total(value):
    return jnp.sum(jnp.sum(value, axis=0, keepdims=True), axis=1, keepdims=True)


def lane_row(values):
    lane = lax.broadcasted_iota(jnp.int32, (1, LANES), 1)
    row = jnp.zeros((1, LANES), F32)
    for place, value in enumerate(values):
        row = jnp.where(lane == place, value, row)
    return row


def pick(row, place):
    lane = lax.broadcasted_iota(jnp.int32, (1, LANES), 1)
    return jnp.sum(jnp.where(lane == place, row, 0.0), axis=1, keepdims=True)


def load_rows(ref, count):
    return jnp.concatenate(
        [ref[0, :, pl.ds(k * LANES, LANES)] for k in range(count)], axis=0
    )


def fault_scalars(sizes, faults):
    start = jnp.int32(0)
    scalars = []
    for f in range(faults):
        scalars.append((start // LANES, start % LANES, sizes[0, 0, f]))
        start = start + sizes[0, 0, f]
    return scalars


def precondition(scalars, blocks, field, windows, shifts, lens, stack, ready):
    faults = len(scalars)
    chunks = blocks.shape[1] // LANES
    rows = field.shape[0]
    lane = lax.broadcasted_iota(jnp.int32, (faults, LANES), 1)
    for f, (tile, shift, size) in enumerate(scalars):
        shifts[f : f + 1, :] = jnp.full((1, LANES), shift, jnp.int32)
        lens[f : f + 1, :] = jnp.full((1, LANES), size, jnp.int32)
        for k in range(chunks + 1):
            windows[k, f : f + 1, :] = field[pl.ds(tile + k, 1), :]
    shift = shifts[...]
    size = lens[...]
    bits = [((shift >> b) & 1) == 1 for b in range(7)]
    live = [lane + k * LANES < size for k in range(chunks)]
    parts = [windows[k] for k in range(chunks + 1)]
    for b in range(7):
        step = 1 << b
        rolled = [pltpu.roll(part, LANES - step, 1) for part in parts]
        moved = [
            jnp.where(lane < LANES - step, rolled[k], rolled[min(k + 1, chunks)])
            for k in range(chunks + 1)
        ]
        parts = [jnp.where(bits[b], new, old) for new, old in zip(moved, parts)]
    parts = [jnp.where(live[k], parts[k], 0.0) for k in range(chunks)]
    sub = lax.broadcasted_iota(jnp.int32, (8, LANES), 0)
    products = [[] for _ in range(chunks)]
    for group in range(faults // 8):
        pieces = []
        for k in range(chunks):
            high, low = split(parts[k][group * 8 : group * 8 + 8])
            pieces.append(jnp.concatenate([high, low], axis=0))
        left = jnp.concatenate(pieces, axis=1)
        found = [jnp.zeros((8, LANES), F32) for _ in range(chunks)]
        for place in range(8):
            f = group * 8 + place
            ready(f)
            result = dot_nt(left, blocks[f])
            result = result[:8] + result[8:]
            for k in range(chunks):
                found[k] = jnp.where(
                    sub == place, result[:, k * LANES : (k + 1) * LANES], found[k]
                )
        for k in range(chunks):
            products[k].append(found[k])
    parts = [
        jnp.where(live[k], jnp.concatenate(products[k], axis=0), 0.0) for k in range(chunks)
    ]
    parts.append(jnp.zeros((faults, LANES), F32))
    for b in range(7):
        step = 1 << b
        rolled = [pltpu.roll(part, step, 1) for part in parts]
        moved = [
            jnp.where(lane >= step, rolled[k], rolled[k - 1] if k else 0.0)
            for k in range(chunks + 1)
        ]
        parts = [jnp.where(bits[b], new, old) for new, old in zip(moved, parts)]
    count = faults * (chunks + 1)
    for k in range(chunks + 1):
        stack[k * faults : (k + 1) * faults, :] = parts[k]
    depth = stack.shape[0]
    if depth > count:
        stack[count:depth, :] = jnp.zeros((depth - count, LANES), F32)
    place = lax.broadcasted_iota(jnp.int32, (1, depth), 1)
    chunk = jnp.zeros((1, depth), jnp.int32)
    for k in range(1, chunks + 1):
        chunk = chunk + (place >= k * faults).astype(jnp.int32)
    local = place - chunk * faults
    target = jnp.full((1, depth), -1, jnp.int32)
    for f, (tile, _, _) in enumerate(scalars):
        target = jnp.where(local == f, tile + chunk, target)
    target = jnp.where(place < count, target, -1)
    chosen = (lax.broadcasted_iota(jnp.int32, (rows, depth), 0) == target).astype(BF16)
    high, low = split(stack[...])
    return jnp.dot(chosen, high, preferred_element_type=F32) + jnp.dot(
        chosen, low, preferred_element_type=F32
    )


def always(f):
    pass


def first_kernel(sizes, rhs, friction, blocks, send, blocks_out, field, windows, shifts, lens, stack, sems):
    faults, width = blocks.shape[2], blocks.shape[3]
    tiles = rhs.shape[2] // LANES
    scalars = fault_scalars(sizes, faults)
    copies = []
    for f, (_, _, size) in enumerate(scalars):
        need = pl.multiple_of((size + 15) // 16 * 16, 16)
        copy = pltpu.make_async_copy(
            blocks.at[0, 0, f, pl.ds(0, need)], blocks_out.at[f, pl.ds(0, need)], sems.at[f]
        )
        copy.start()
        copies.append(copy)
    value = load_rows(rhs, tiles)
    field[0:tiles, :] = value
    field[tiles:, :] = jnp.zeros((field.shape[0] - tiles, LANES), F32)
    out = precondition(
        scalars, blocks_out, field, windows, shifts, lens, stack, lambda f: copies[f].wait()
    )
    direction = out[0:tiles]
    scaled = load_rows(friction, tiles) * direction
    send[...] = jnp.zeros_like(send)
    send[0:tiles, :] = direction
    send[tiles : tiles + 1, :] = lane_row([total(value * value), total(value * scaled)])


def gathered(parts, tiles):
    whole = parts[0]
    for c in range(1, parts.shape[0]):
        whole = whole + parts[c]
    return whole[0:tiles], whole[tiles : tiles + 1]


def second_kernel(sizes, rhs, friction, sent, parts, blocks, send, image_out, basis_out, field, windows, shifts, lens, stack):
    tiles = rhs.shape[2] // LANES
    scalars = fault_scalars(sizes, blocks.shape[0])
    start = load_rows(rhs, tiles)
    diagonal = load_rows(friction, tiles)
    product, sums = gathered(parts, tiles)
    norm2 = pick(sums, 0)
    image = diagonal * sent[0:tiles, :] + product
    scale = lax.rsqrt(norm2)
    value = (image - pick(sums, 1) / norm2 * start) * scale
    image_out[...] = image
    basis_out[0:tiles, :] = value
    basis_out[tiles:, :] = jnp.broadcast_to(norm2, (basis_out.shape[0] - tiles, LANES))
    field[0:tiles, :] = value
    field[tiles:, :] = jnp.zeros((field.shape[0] - tiles, LANES), F32)
    direction = precondition(scalars, blocks, field, windows, shifts, lens, stack, always)[0:tiles]
    scaled = diagonal * direction
    send[...] = jnp.zeros_like(send)
    send[0:tiles, :] = direction
    send[tiles : tiles + 1, :] = lane_row(
        [
            total(value * value),
            total(start * value) * scale,
            total(start * scaled) * scale,
            total(value * scaled),
        ]
    )


def third_kernel(sizes, rhs, friction, sent, parts, basis, blocks, send, image_out, field, windows, shifts, lens, stack):
    tiles = rhs.shape[2] // LANES
    scalars = fault_scalars(sizes, blocks.shape[0])
    start = load_rows(rhs, tiles)
    diagonal = load_rows(friction, tiles)
    product, sums = gathered(parts, tiles)
    image = diagonal * sent[0:tiles, :] + product
    value = basis[0:tiles, :]
    scale = lax.rsqrt(basis[tiles : tiles + 1, 0:1])
    norm2, cross, along_start, along = [pick(sums, k) for k in range(4)]
    left = norm2 - cross * cross
    usable = left > 1e-5 * norm2
    along = jnp.where(usable, (along - cross * along_start) / jnp.where(usable, left, 1.0), 0.0)
    along_start = along_start - cross * along
    value = (image - along * value - (along_start * scale) * start) * lax.rsqrt(
        jnp.maximum(norm2, 1e-30)
    )
    image_out[...] = image
    field[0:tiles, :] = value
    field[tiles:, :] = jnp.zeros((field.shape[0] - tiles, LANES), F32)
    direction = precondition(scalars, blocks, field, windows, shifts, lens, stack, always)[0:tiles]
    send[...] = jnp.zeros_like(send)
    send[0:tiles, :] = direction


def fourth_kernel(rhs, friction, sent, parts, image0, image1, image_out, sums_out):
    tiles = rhs.shape[2] // LANES
    start = load_rows(rhs, tiles)
    product, _ = gathered(parts, tiles)
    image = load_rows(friction, tiles) * sent[0:tiles, :] + product
    image_out[...] = image
    images = [image0[...], image1[...], image]
    values = [total(images[i] * images[j]) for i in range(3) for j in range(i + 1)]
    values += [total(start * one) for one in images]
    sums_out[...] = jnp.broadcast_to(lane_row(values), sums_out.shape)


def last_kernel(sums, rhs, image0, image1, image2, sent0, sent1, sent2, update, residual):
    tiles = rhs.shape[2] // LANES
    row = jnp.sum(sums[...], axis=0, keepdims=True)
    entries = [pick(row, k) for k in range(9)]
    scale = [lax.rsqrt(jnp.maximum(entries[k], 1e-30)) for k in (0, 2, 5)]
    gram = {}
    place = 0
    for i in range(3):
        for j in range(i + 1):
            gram[i, j] = entries[place] * scale[i] * scale[j]
            place += 1
    goal = [entries[6 + i] * scale[i] for i in range(3)]
    low10 = gram[1, 0]
    low20 = gram[2, 0]
    pivot1 = 1.0 - low10 * low10
    keep1 = pivot1 > 1e-6
    inverse1 = jnp.where(keep1, 1.0 / jnp.where(keep1, pivot1, 1.0), 0.0)
    cross = gram[2, 1] - low20 * low10
    low21 = cross * inverse1
    pivot2 = 1.0 - low20 * low20 - cross * low21
    keep2 = pivot2 > 1e-6
    inverse2 = jnp.where(keep2, 1.0 / jnp.where(keep2, pivot2, 1.0), 0.0)
    part1 = goal[1] - low10 * goal[0]
    part2 = goal[2] - low20 * goal[0] - low21 * part1
    weight2 = part2 * inverse2
    weight1 = part1 * inverse1 - low21 * weight2
    weight0 = goal[0] - low10 * weight1 - low20 * weight2
    weights = [weight0 * scale[0], weight1 * scale[1], weight2 * scale[2]]
    start = load_rows(rhs, tiles)
    best = (
        weights[0] * sent0[0:tiles, :]
        + weights[1] * sent1[0:tiles, :]
        + weights[2] * sent2[0:tiles, :]
    )
    rest = start - weights[0] * image0[...] - weights[1] * image1[...] - weights[2] * image2[...]
    for k in range(tiles):
        update[0, :, pl.ds(k * LANES, LANES)] = best[k : k + 1]
        residual[0, :, pl.ds(k * LANES, LANES)] = rest[k : k + 1]


def tiles_kernel(spots, rows, weight, blocks, *refs):
    sent, (out, field, found, products) = refs[:-4], refs[-4:]
    slots = blocks.shape[0]
    count, height = out.shape[0], out.shape[1]
    tiles = height - 8 if height % 8 == 0 else height
    sums = None
    for k, one in enumerate(sent):
        field[k * height : (k + 1) * height, :] = one[...]
    for t in range(slots):
        found[t : t + 1, :] = field[pl.ds(spots[0, t], 1), :]
    sub = lax.broadcasted_iota(jnp.int32, (8, LANES), 0)
    blank = jnp.zeros((8, LANES), F32)
    for group in range(slots // 16):
        base = group * 16
        top = jnp.concatenate([found[base : base + 8, :], blank], axis=1)
        bottom = jnp.concatenate([blank, found[base + 8 : base + 16, :]], axis=1)
        left = jnp.concatenate([top, bottom], axis=0).astype(BF16)
        first, second = blank, blank
        for p in range(4):
            a, b = base + 2 * p, base + 2 * p + 1
            right = jnp.concatenate(
                [
                    jnp.concatenate([blocks[a], blocks[a + 8]], axis=1),
                    jnp.concatenate([blocks[b], blocks[b + 8]], axis=1),
                ],
                axis=0,
            )
            result = dot_nt(left, right)
            for spot, half in ((2 * p, slice(0, LANES)), (2 * p + 1, slice(LANES, 2 * LANES))):
                first = jnp.where(sub == spot, result[:8, half], first)
                second = jnp.where(sub == spot, result[8:, half], second)
        products[base : base + 8, :] = first
        products[base + 8 : base + 16, :] = second
    high, low = split(products[...])
    target = rows[...]
    chosen = jnp.where(
        lax.broadcasted_iota(jnp.int32, (count * height, slots), 0) == target, weight[...], 0.0
    )
    chosen_high, chosen_low = split(chosen)
    value = (
        jnp.dot(chosen_high, high, preferred_element_type=F32)
        + jnp.dot(chosen_low, high, preferred_element_type=F32)
        + jnp.dot(chosen_high, low, preferred_element_type=F32)
    )
    out[...] = value.reshape(count, height, LANES)


def scratch(shape, dtype=F32):
    return pltpu.VMEM(shape, dtype)


def local(
    rhs,
    friction,
    kernel_tiles,
    tile_scale,
    tile_row,
    tile_col,
    tile_counts,
    precond_blocks,
    fault_sizes,
):
    length = rhs.shape[2]
    slots = kernel_tiles.shape[2]
    faults, width = precond_blocks.shape[2], precond_blocks.shape[3]
    tiles = length // LANES
    height = (tiles + 8) // 8 * 8
    chunks = width // LANES
    row_count = lax.axis_size("row")
    col_count = lax.axis_size("col")
    my_row = lax.axis_index("row")
    paired = row_count & (row_count - 1) == 0
    rows = (tiles + chunks + 8) // 8 * 8
    depth = (faults * (chunks + 1) + LANES - 1) // LANES * LANES

    source = tile_col[0, 0] // tiles
    order = source ^ my_row if paired else (my_row - source) % row_count
    spots = (order * height + tile_col[0, 0] % tiles).reshape(1, slots)
    target = (tile_row[0, 0] // tiles * height + tile_row[0, 0] % tiles).reshape(1, slots)
    weight = jnp.where(
        jnp.arange(slots, dtype=jnp.int32) < tile_counts[0, 0], tile_scale[0, 0], 0.0
    ).reshape(1, slots)

    grid = jax.ShapeDtypeStruct((height, LANES), F32)
    plain = jax.ShapeDtypeStruct((tiles, LANES), F32)
    work = [
        scratch((rows, LANES)),
        scratch((chunks + 1, faults, LANES)),
        scratch((faults, LANES), jnp.int32),
        scratch((faults, LANES), jnp.int32),
        scratch((depth, LANES)),
    ]

    sent0, blocks = pl.pallas_call(
        first_kernel,
        out_shape=[grid, pltpu.VMEM((faults, width, width), BF16)],
        in_specs=[SMEM, VMEM, VMEM, ANY],
        out_specs=[VMEM, VMEM],
        scratch_shapes=work + [pltpu.SemaphoreType.DMA((faults,))],
        compiler_params=PARAMS,
        name="first",
    )(fault_sizes, rhs, friction, precond_blocks)

    near = pltpu.with_memory_space_constraint(
        kernel_tiles.reshape(slots, LANES, LANES), pltpu.VMEM
    )

    def apply_kernel(sent):
        got = [sent]
        for d in range(1, row_count):
            pairs = [(i, i ^ d if paired else (i + d) % row_count) for i in range(row_count)]
            got.append(lax.ppermute(sent, "row", pairs))
        sums = got[0][tiles]
        for one in got[1:]:
            sums = sums + one[tiles]
        parts = pl.pallas_call(
            tiles_kernel,
            out_shape=jax.ShapeDtypeStruct((col_count, height, LANES), F32),
            in_specs=[SMEM, VMEM, VMEM, VMEM] + [VMEM] * row_count,
            out_specs=VMEM,
            scratch_shapes=[
                scratch((row_count * height, LANES)),
                scratch((slots, LANES)),
                scratch((slots, LANES)),
            ],
            compiler_params=PARAMS,
            name="tiles",
        )(spots, target, weight, near, *got)
        parts = parts.at[:, tiles, :].set(sums)
        return lax.all_to_all(parts, "col", 0, 0, tiled=True)

    parts0 = apply_kernel(sent0)
    sent1, image0, basis = pl.pallas_call(
        second_kernel,
        out_shape=[grid, plain, grid],
        in_specs=[SMEM] + [VMEM] * 5,
        out_specs=[VMEM] * 3,
        scratch_shapes=work,
        compiler_params=PARAMS,
        name="second",
    )(fault_sizes, rhs, friction, sent0, parts0, blocks)
    parts1 = apply_kernel(sent1)
    sent2, image1 = pl.pallas_call(
        third_kernel,
        out_shape=[grid, plain],
        in_specs=[SMEM] + [VMEM] * 6,
        out_specs=[VMEM] * 2,
        scratch_shapes=work,
        compiler_params=PARAMS,
        name="third",
    )(fault_sizes, rhs, friction, sent1, parts1, basis, blocks)
    parts2 = apply_kernel(sent2)
    devices = row_count * col_count
    image2, sums = pl.pallas_call(
        fourth_kernel,
        out_shape=[plain, jax.ShapeDtypeStruct((devices, LANES), F32)],
        in_specs=[VMEM] * 6,
        out_specs=[VMEM] * 2,
        compiler_params=PARAMS,
        name="fourth",
    )(rhs, friction, sent2, parts2, image0, image1)
    sums = lax.all_to_all(sums, ("row", "col"), 0, 0, tiled=True)
    whole = jax.ShapeDtypeStruct((1, 1, length), F32)
    return pl.pallas_call(
        last_kernel,
        out_shape=[whole, whole],
        in_specs=[VMEM] * 8,
        out_specs=[VMEM] * 2,
        compiler_params=PARAMS,
        name="last",
    )(sums, rhs, image0, image1, image2, sent0, sent1, sent2)


def solution(mesh):
    return jax.shard_map(
        local,
        mesh=mesh,
        in_specs=(
            P("row", "col", None),
            P("row", "col", None),
            P("row", "col", None, None, None),
            P("row", "col", None),
            P("row", "col", None),
            P("row", "col", None),
            P("row", "col"),
            P("row", "col", None, None, None),
            P("row", "col", None),
        ),
        out_specs=(P("row", "col", None), P("row", "col", None)),
        check_vma=False,
    )
```

```python
import functools

import jax
import jax.numpy as jnp
from jax import lax
from jax.experimental import pallas as pl
from jax.experimental.pallas import tpu as pltpu
from jax.sharding import PartitionSpec as P

LANES = 128
UNROLL = 3
F32 = jnp.float32
BF16 = jnp.bfloat16
VMEM = pl.BlockSpec(memory_space=pltpu.VMEM)
SMEM = pl.BlockSpec(memory_space=pltpu.SMEM)
ANY = pl.BlockSpec(memory_space=pl.ANY)
PARAMS = pltpu.CompilerParams(vmem_limit_bytes=54 << 20)


def dot_nt(left, right):
    return lax.dot_general(left, right, (((1,), (1,)), ((), ())), preferred_element_type=F32)


def split(value):
    high = value.astype(BF16)
    low = (value - high.astype(F32)).astype(BF16)
    return high, low


def total(value):
    return jnp.sum(jnp.sum(value, axis=0, keepdims=True), axis=1, keepdims=True)


def lane_row(values):
    lane = lax.broadcasted_iota(jnp.int32, (1, LANES), 1)
    row = jnp.zeros((1, LANES), F32)
    for place, value in enumerate(values):
        row = jnp.where(lane == place, value, row)
    return row


def pick(row, place):
    lane = lax.broadcasted_iota(jnp.int32, (1, LANES), 1)
    return jnp.sum(jnp.where(lane == place, row, 0.0), axis=1, keepdims=True)


def load_rows(ref, count):
    return jnp.concatenate(
        [ref[0, :, pl.ds(k * LANES, LANES)] for k in range(count)], axis=0
    )


def fault_scalars(sizes, faults):
    start = jnp.int32(0)
    scalars = []
    for f in range(faults):
        scalars.append((start // LANES, start % LANES, sizes[0, 0, f]))
        start = start + sizes[0, 0, f]
    return scalars


def fetch(scalars, remote, blocks, sems):
    copies = []
    for f, (_, _, size) in enumerate(scalars):
        need = pl.multiple_of((size + 15) // 16 * 16, 16)
        copy = pltpu.make_async_copy(
            remote.at[0, 0, f, pl.ds(0, need)], blocks.at[f, pl.ds(0, need)], sems.at[f]
        )
        copy.start()
        copies.append(copy)
    return copies


def precondition(sizes, remote, field, work):
    blocks, windows, shifts, lens, stack, lefts, found, large, sems = work
    faults = remote.shape[2]
    chunks = blocks.shape[1] // LANES
    rows = field.shape[0]
    scalars = fault_scalars(sizes, faults)
    copies = fetch(scalars, remote, blocks, sems)
    lane = lax.broadcasted_iota(jnp.int32, (faults, LANES), 1)
    for f, (tile, shift, size) in enumerate(scalars):
        shifts[f : f + 1, :] = jnp.full((1, LANES), shift, jnp.int32)
        lens[f : f + 1, :] = jnp.full((1, LANES), size, jnp.int32)
        for k in range(chunks + 1):
            windows[k, f : f + 1, :] = field[pl.ds(tile + k, 1), :]
    shift = shifts[...]
    size = lens[...]
    bits = [((shift >> b) & 1) == 1 for b in range(7)]
    live = [lane + k * LANES < size for k in range(chunks)]
    parts = [windows[k] for k in range(chunks + 1)]
    for b in range(7):
        step = 1 << b
        rolled = [pltpu.roll(part, LANES - step, 1) for part in parts]
        moved = [
            jnp.where(lane < LANES - step, rolled[k], rolled[min(k + 1, chunks)])
            for k in range(chunks + 1)
        ]
        parts = [jnp.where(bits[b], new, old) for new, old in zip(moved, parts)]
    parts = [jnp.where(live[k], parts[k], 0.0) for k in range(chunks)]
    sub = lax.broadcasted_iota(jnp.int32, (8, LANES), 0)
    half = blocks.shape[1] // 2
    chunk_half = chunks // 2
    for group in range(faults // 8):
        pieces = []
        for k in range(chunks):
            high, low = split(parts[k][group * 8 : group * 8 + 8])
            pieces.append(jnp.concatenate([high, low], axis=0))
        left = jnp.concatenate(pieces, axis=1)
        lefts[group] = left
        sums = [jnp.zeros((8, LANES), F32) for _ in range(chunk_half)]
        for place in range(8):
            f = group * 8 + place
            copies[f].wait()
            result = dot_nt(left[:, :half], blocks[f, :half, :half])
            result = result[:8] + result[8:]
            for k in range(chunk_half):
                sums[k] = jnp.where(sub == place, result[:, k * LANES : (k + 1) * LANES], sums[k])
        for k in range(chunks):
            found[k, group] = sums[k] if k < chunk_half else jnp.zeros((8, LANES), F32)
    count = jnp.int32(0)
    for f, (_, _, size) in enumerate(scalars):
        large[count] = f
        count = count + (size > half).astype(jnp.int32)

    def rest(step, carry):
        for u in range(UNROLL):
            place = step * UNROLL + u
            f = large[jnp.minimum(place, count - 1)]
            group = f // 8
            left = lefts[group]
            above = dot_nt(left[:, half:], blocks[f, :half, half:])
            below = dot_nt(left, blocks[f, half:, :])
            above = above[:8] + above[8:]
            below = below[:8] + below[8:]
            mine = jnp.logical_and(sub == f % 8, place < count)
            for k in range(chunk_half):
                piece = slice(k * LANES, (k + 1) * LANES)
                found[k, group] += jnp.where(mine, above[:, piece], 0.0)
                found[chunk_half + k, group] += jnp.where(mine, below[:, piece], 0.0)
        return carry

    lax.fori_loop(0, (count + UNROLL - 1) // UNROLL, rest, 0)
    parts = [
        jnp.where(live[k], found[k].reshape(faults, LANES), 0.0) for k in range(chunks)
    ]
    parts.append(jnp.zeros((faults, LANES), F32))
    for b in range(7):
        step = 1 << b
        rolled = [pltpu.roll(part, step, 1) for part in parts]
        moved = [
            jnp.where(lane >= step, rolled[k], rolled[k - 1] if k else 0.0)
            for k in range(chunks + 1)
        ]
        parts = [jnp.where(bits[b], new, old) for new, old in zip(moved, parts)]
    count = faults * (chunks + 1)
    for k in range(chunks + 1):
        stack[k * faults : (k + 1) * faults, :] = parts[k]
    depth = stack.shape[0]
    if depth > count:
        stack[count:depth, :] = jnp.zeros((depth - count, LANES), F32)
    place = lax.broadcasted_iota(jnp.int32, (1, depth), 1)
    chunk = jnp.zeros((1, depth), jnp.int32)
    for k in range(1, chunks + 1):
        chunk = chunk + (place >= k * faults).astype(jnp.int32)
    local = place - chunk * faults
    target = jnp.full((1, depth), -1, jnp.int32)
    for f, (tile, _, _) in enumerate(scalars):
        target = jnp.where(local == f, tile + chunk, target)
    target = jnp.where(place < count, target, -1)
    chosen = (lax.broadcasted_iota(jnp.int32, (rows, depth), 0) == target).astype(BF16)
    high, low = split(stack[...])
    return jnp.dot(chosen, high, preferred_element_type=F32) + jnp.dot(
        chosen, low, preferred_element_type=F32
    )


def set_field(field, value):
    tiles = value.shape[0]
    field[0:tiles, :] = value
    field[tiles:, :] = jnp.zeros((field.shape[0] - tiles, LANES), F32)


def first_kernel(sizes, rhs, friction, blocks, send, field, *work):
    tiles = rhs.shape[2] // LANES
    value = load_rows(rhs, tiles)
    set_field(field, value)
    direction = precondition(sizes, blocks, field, work)[0:tiles]
    scaled = load_rows(friction, tiles) * direction
    send[...] = jnp.zeros_like(send)
    send[0:tiles, :] = direction
    send[tiles : tiles + 1, :] = lane_row([total(value * value), total(value * scaled)])


def gathered(parts, tiles):
    whole = parts[0][...]
    for part in parts[1:]:
        whole = whole + part[...]
    return whole[0:tiles], whole[tiles : tiles + 1]


def second_kernel(sizes, rhs, friction, blocks, sent, *refs):
    parts, (send, image_out, basis_out, field, *work) = refs[:-13], refs[-13:]
    tiles = rhs.shape[2] // LANES
    start = load_rows(rhs, tiles)
    diagonal = load_rows(friction, tiles)
    product, sums = gathered(parts, tiles)
    norm2 = pick(sums, 0)
    image = diagonal * sent[0:tiles, :] + product
    scale = lax.rsqrt(norm2)
    value = (image - pick(sums, 1) / norm2 * start) * scale
    image_out[...] = image
    basis_out[0:tiles, :] = value
    basis_out[tiles:, :] = jnp.broadcast_to(norm2, (basis_out.shape[0] - tiles, LANES))
    set_field(field, value)
    direction = precondition(sizes, blocks, field, work)[0:tiles]
    scaled = diagonal * direction
    send[...] = jnp.zeros_like(send)
    send[0:tiles, :] = direction
    send[tiles : tiles + 1, :] = lane_row(
        [
            total(value * value),
            total(start * value) * scale,
            total(start * scaled) * scale,
            total(value * scaled),
        ]
    )


def third_kernel(sizes, rhs, friction, blocks, sent, basis, *refs):
    parts, (send, image_out, field, *work) = refs[:-12], refs[-12:]
    tiles = rhs.shape[2] // LANES
    start = load_rows(rhs, tiles)
    diagonal = load_rows(friction, tiles)
    product, sums = gathered(parts, tiles)
    image = diagonal * sent[0:tiles, :] + product
    value = basis[0:tiles, :]
    scale = lax.rsqrt(basis[tiles : tiles + 1, 0:1])
    norm2, cross, along_start, along = [pick(sums, k) for k in range(4)]
    left = norm2 - cross * cross
    usable = left > 1e-5 * norm2
    along = jnp.where(usable, (along - cross * along_start) / jnp.where(usable, left, 1.0), 0.0)
    along_start = along_start - cross * along
    value = (image - along * value - (along_start * scale) * start) * lax.rsqrt(
        jnp.maximum(norm2, 1e-30)
    )
    image_out[...] = image
    set_field(field, value)
    direction = precondition(sizes, blocks, field, work)[0:tiles]
    send[...] = jnp.zeros_like(send)
    send[0:tiles, :] = direction


def fourth_kernel(rhs, friction, sent, image0, image1, *refs):
    parts, (image_out, sums_out) = refs[:-2], refs[-2:]
    tiles = rhs.shape[2] // LANES
    start = load_rows(rhs, tiles)
    product, _ = gathered(parts, tiles)
    image = load_rows(friction, tiles) * sent[0:tiles, :] + product
    image_out[...] = image
    images = [image0[...], image1[...], image]
    values = [total(images[i] * images[j]) for i in range(3) for j in range(i + 1)]
    values += [total(start * one) for one in images]
    sums_out[...] = jnp.broadcast_to(lane_row(values), sums_out.shape)


def last_kernel(sums, rhs, image0, image1, image2, sent0, sent1, sent2, update, residual):
    tiles = rhs.shape[2] // LANES
    row = jnp.sum(sums[...], axis=0, keepdims=True)
    entries = [pick(row, k) for k in range(9)]
    scale = [lax.rsqrt(jnp.maximum(entries[k], 1e-30)) for k in (0, 2, 5)]
    gram = {}
    place = 0
    for i in range(3):
        for j in range(i + 1):
            gram[i, j] = entries[place] * scale[i] * scale[j]
            place += 1
    goal = [entries[6 + i] * scale[i] for i in range(3)]
    low10 = gram[1, 0]
    low20 = gram[2, 0]
    pivot1 = 1.0 - low10 * low10
    keep1 = pivot1 > 1e-6
    inverse1 = jnp.where(keep1, 1.0 / jnp.where(keep1, pivot1, 1.0), 0.0)
    cross = gram[2, 1] - low20 * low10
    low21 = cross * inverse1
    pivot2 = 1.0 - low20 * low20 - cross * low21
    keep2 = pivot2 > 1e-6
    inverse2 = jnp.where(keep2, 1.0 / jnp.where(keep2, pivot2, 1.0), 0.0)
    part1 = goal[1] - low10 * goal[0]
    part2 = goal[2] - low20 * goal[0] - low21 * part1
    weight2 = part2 * inverse2
    weight1 = part1 * inverse1 - low21 * weight2
    weight0 = goal[0] - low10 * weight1 - low20 * weight2
    weights = [weight0 * scale[0], weight1 * scale[1], weight2 * scale[2]]
    start = load_rows(rhs, tiles)
    best = (
        weights[0] * sent0[0:tiles, :]
        + weights[1] * sent1[0:tiles, :]
        + weights[2] * sent2[0:tiles, :]
    )
    rest = start - weights[0] * image0[...] - weights[1] * image1[...] - weights[2] * image2[...]
    for k in range(tiles):
        update[0, :, pl.ds(k * LANES, LANES)] = best[k : k + 1]
        residual[0, :, pl.ds(k * LANES, LANES)] = rest[k : k + 1]


def tiles_kernel(tail, spots, rows, weight, remote, *refs):
    sent, (keep, give, blocks, field, found, products, sems) = refs[:-7], refs[-7:]
    slots = blocks.shape[0]
    far, height = keep.shape[0], keep.shape[1]
    groups = slots // 16
    copies = []
    for group in range(groups):
        copy = pltpu.make_async_copy(
            remote.at[0, 0, pl.ds(group * 16, 16)],
            blocks.at[pl.ds(group * 16, 16)],
            sems.at[group],
        )
        copy.start()
        copies.append(copy)
    for k, one in enumerate(sent):
        field[k * height : (k + 1) * height, :] = one[...]
    for t in range(slots):
        found[t : t + 1, :] = field[pl.ds(spots[0, t], 1), :]
    sub = lax.broadcasted_iota(jnp.int32, (8, LANES), 0)
    blank = jnp.zeros((8, LANES), F32)
    for group in range(groups):
        copies[group].wait()
        base = group * 16
        top = jnp.concatenate([found[base : base + 8, :], blank], axis=1)
        bottom = jnp.concatenate([blank, found[base + 8 : base + 16, :]], axis=1)
        left = jnp.concatenate([top, bottom], axis=0).astype(BF16)
        first, second = blank, blank
        for p in range(4):
            a, b = base + 2 * p, base + 2 * p + 1
            right = jnp.concatenate(
                [
                    jnp.concatenate([blocks[a], blocks[a + 8]], axis=1),
                    jnp.concatenate([blocks[b], blocks[b + 8]], axis=1),
                ],
                axis=0,
            )
            result = dot_nt(left, right)
            for spot, half in ((2 * p, slice(0, LANES)), (2 * p + 1, slice(LANES, 2 * LANES))):
                first = jnp.where(sub == spot, result[:8, half], first)
                second = jnp.where(sub == spot, result[8:, half], second)
        products[base : base + 8, :] = first
        products[base + 8 : base + 16, :] = second
    high, low = split(products[...])
    target = rows[...]
    chosen = jnp.where(
        lax.broadcasted_iota(jnp.int32, (2 * far * height, slots), 0) == target, weight[...], 0.0
    )
    chosen_high, chosen_low = split(chosen)
    value = (
        jnp.dot(chosen_high, high, preferred_element_type=F32)
        + jnp.dot(chosen_low, high, preferred_element_type=F32)
        + jnp.dot(chosen_high, low, preferred_element_type=F32)
    )
    keep[...] = value[: far * height].reshape(far, height, LANES)
    give[...] = value[far * height :].reshape(far, height, LANES)
    last = height - 8
    sums = sent[0][last:height, :]
    for one in sent[1:]:
        sums = sums + one[last:height, :]
    sums = jnp.where(lax.broadcasted_iota(jnp.int32, (8, LANES), 0) == tail, sums, 0.0)
    for k in range(far):
        keep[k, last:height, :] += sums
        give[k, last:height, :] += sums


def scratch(shape, dtype=F32):
    return pltpu.VMEM(shape, dtype)


def local(
    rhs,
    friction,
    kernel_tiles,
    tile_scale,
    tile_row,
    tile_col,
    tile_counts,
    precond_blocks,
    fault_sizes,
):
    length = rhs.shape[2]
    slots = kernel_tiles.shape[2]
    faults, width = precond_blocks.shape[2], precond_blocks.shape[3]
    tiles = length // LANES
    height = (tiles + 8) // 8 * 8
    chunks = width // LANES
    row_count = lax.axis_size("row")
    col_count = lax.axis_size("col")
    my_row = lax.axis_index("row")
    my_col = lax.axis_index("col")
    far = col_count // 2
    rows = (tiles + chunks + 8) // 8 * 8
    depth = (faults * (chunks + 1) + LANES - 1) // LANES * LANES

    place = tile_col[0, 0] // tiles ^ my_row
    spots = (place * height + tile_col[0, 0] % tiles).reshape(1, slots)
    place = tile_row[0, 0] // tiles ^ my_col
    place = place % 2 * far + place // 2
    target = (place * height + tile_row[0, 0] % tiles).reshape(1, slots)
    weight = jnp.where(
        jnp.arange(slots, dtype=jnp.int32) < tile_counts[0, 0], tile_scale[0, 0], 0.0
    ).reshape(1, slots)

    grid = jax.ShapeDtypeStruct((height, LANES), F32)
    plain = jax.ShapeDtypeStruct((tiles, LANES), F32)
    half_grid = jax.ShapeDtypeStruct((far, height, LANES), F32)
    work = [
        scratch((rows, LANES)),
        scratch((faults, width, width), BF16),
        scratch((chunks + 1, faults, LANES)),
        scratch((faults, LANES), jnp.int32),
        scratch((faults, LANES), jnp.int32),
        scratch((depth, LANES)),
        scratch((faults // 8, 16, width), BF16),
        scratch((chunks, faults // 8, 8, LANES)),
        pltpu.SMEM((faults + 1,), jnp.int32),
        pltpu.SemaphoreType.DMA((faults,)),
    ]

    def exchange(value, axis, distance):
        size = lax.axis_size(axis)
        return lax.ppermute(value, axis, [(i, i ^ distance) for i in range(size)])

    def apply_kernel(sent):
        got = [sent] + [exchange(sent, "row", d) for d in range(1, row_count)]
        keep, give = pl.pallas_call(
            functools.partial(tiles_kernel, tiles % 8),
            out_shape=[half_grid, half_grid],
            in_specs=[SMEM, VMEM, VMEM, ANY] + [VMEM] * row_count,
            out_specs=[VMEM] * 2,
            scratch_shapes=[
                scratch((slots, LANES, LANES), BF16),
                scratch((row_count * height, LANES)),
                scratch((slots, LANES)),
                scratch((slots, LANES)),
                pltpu.SemaphoreType.DMA((slots // 16,)),
            ],
            compiler_params=PARAMS,
            name="tiles",
        )(spots, target, weight, kernel_tiles, *got)
        both = keep + exchange(give, "col", 1)
        return [both[0]] + [exchange(both[d], "col", 2 * d) for d in range(1, far)]

    sent0 = pl.pallas_call(
        first_kernel,
        out_shape=grid,
        in_specs=[SMEM, VMEM, VMEM, ANY],
        out_specs=VMEM,
        scratch_shapes=work,
        compiler_params=PARAMS,
        name="first",
    )(fault_sizes, rhs, friction, precond_blocks)
    parts0 = apply_kernel(sent0)
    sent1, image0, basis = pl.pallas_call(
        second_kernel,
        out_shape=[grid, plain, grid],
        in_specs=[SMEM, VMEM, VMEM, ANY] + [VMEM] * (1 + far),
        out_specs=[VMEM] * 3,
        scratch_shapes=work,
        compiler_params=PARAMS,
        name="second",
    )(fault_sizes, rhs, friction, precond_blocks, sent0, *parts0)
    parts1 = apply_kernel(sent1)
    sent2, image1 = pl.pallas_call(
        third_kernel,
        out_shape=[grid, plain],
        in_specs=[SMEM, VMEM, VMEM, ANY] + [VMEM] * (2 + far),
        out_specs=[VMEM] * 2,
        scratch_shapes=work,
        compiler_params=PARAMS,
        name="third",
    )(fault_sizes, rhs, friction, precond_blocks, sent1, basis, *parts1)
    parts2 = apply_kernel(sent2)
    devices = row_count * col_count
    image2, sums = pl.pallas_call(
        fourth_kernel,
        out_shape=[plain, jax.ShapeDtypeStruct((devices, LANES), F32)],
        in_specs=[VMEM] * (5 + far),
        out_specs=[VMEM] * 2,
        compiler_params=PARAMS,
        name="fourth",
    )(rhs, friction, sent2, image0, image1, *parts2)
    sums = lax.all_to_all(sums, ("row", "col"), 0, 0, tiled=True)
    whole = jax.ShapeDtypeStruct((1, 1, length), F32)
    return pl.pallas_call(
        last_kernel,
        out_shape=[whole, whole],
        in_specs=[VMEM] * 8,
        out_specs=[VMEM] * 2,
        compiler_params=PARAMS,
        name="last",
    )(sums, rhs, image0, image1, image2, sent0, sent1, sent2)


def solution(mesh):
    return jax.shard_map(
        local,
        mesh=mesh,
        in_specs=(
            P("row", "col", None),
            P("row", "col", None),
            P("row", "col", None, None, None),
            P("row", "col", None),
            P("row", "col", None),
            P("row", "col", None),
            P("row", "col"),
            P("row", "col", None, None, None),
            P("row", "col", None),
        ),
        out_specs=(P("row", "col", None), P("row", "col", None)),
        check_vma=False,
    )
```

```python
import functools

import jax
import jax.numpy as jnp
from jax import lax
from jax.experimental import pallas as pl
from jax.experimental.pallas import tpu as pltpu
from jax.sharding import PartitionSpec as P

LANES = 128
UNROLL = 3
AHEAD = 6
F32 = jnp.float32
BF16 = jnp.bfloat16
VMEM = pl.BlockSpec(memory_space=pltpu.VMEM)
SMEM = pl.BlockSpec(memory_space=pltpu.SMEM)
HBM = pl.BlockSpec(memory_space=pltpu.HBM)
PARAMS = pltpu.CompilerParams(vmem_limit_bytes=24 << 20)


def dot_nt(left, right):
    return lax.dot_general(left, right, (((1,), (1,)), ((), ())), preferred_element_type=F32)


def split(value):
    high = value.astype(BF16)
    low = (value - high.astype(F32)).astype(BF16)
    return high, low


def total(value):
    return jnp.sum(jnp.sum(value, axis=0, keepdims=True), axis=1, keepdims=True)


def lane_row(values):
    lane = lax.broadcasted_iota(jnp.int32, (1, LANES), 1)
    row = jnp.zeros((1, LANES), F32)
    for place, value in enumerate(values):
        row = jnp.where(lane == place, value, row)
    return row


def pick(row, place):
    lane = lax.broadcasted_iota(jnp.int32, (1, LANES), 1)
    return jnp.sum(jnp.where(lane == place, row, 0.0), axis=1, keepdims=True)


def load_rows(ref, count):
    return jnp.concatenate(
        [ref[0, :, pl.ds(k * LANES, LANES)] for k in range(count)], axis=0
    )


def fault_scalars(sizes, faults):
    start = jnp.int32(0)
    scalars = []
    for f in range(faults):
        scalars.append((start // LANES, start % LANES, sizes[0, 0, f]))
        start = start + sizes[0, 0, f]
    return scalars


def fetch(scalars, remote, blocks, sems):
    copies = []
    for f, (_, _, size) in enumerate(scalars):
        need = pl.multiple_of((size + 15) // 16 * 16, 16)
        copy = pltpu.make_async_copy(
            remote.at[0, 0, f, pl.ds(0, need)], blocks.at[f, pl.ds(0, need)], sems.at[f]
        )
        copies.append(copy)
    for copy in copies[:AHEAD]:
        copy.start()
    return copies


def await_copy(copies, place):
    copies[place].wait()
    if place + AHEAD < len(copies):
        copies[place + AHEAD].start()


def precondition(sizes, remote, field, work, begin=None):
    blocks, windows, shifts, lens, stack, lefts, found, large, sems = work
    faults = remote.shape[2]
    chunks = blocks.shape[1] // LANES
    rows = field.shape[0]
    scalars = fault_scalars(sizes, faults)
    copies = fetch(scalars, remote, blocks, sems)
    if begin is not None:
        begin()
    lane = lax.broadcasted_iota(jnp.int32, (faults, LANES), 1)
    for f, (tile, shift, size) in enumerate(scalars):
        shifts[f : f + 1, :] = jnp.full((1, LANES), shift, jnp.int32)
        lens[f : f + 1, :] = jnp.full((1, LANES), size, jnp.int32)
        for k in range(chunks + 1):
            windows[k, f : f + 1, :] = field[pl.ds(tile + k, 1), :]
    shift = shifts[...]
    size = lens[...]
    bits = [((shift >> b) & 1) == 1 for b in range(7)]
    live = [lane + k * LANES < size for k in range(chunks)]
    parts = [windows[k] for k in range(chunks + 1)]
    for b in range(7):
        step = 1 << b
        rolled = [pltpu.roll(part, LANES - step, 1) for part in parts]
        moved = [
            jnp.where(lane < LANES - step, rolled[k], rolled[min(k + 1, chunks)])
            for k in range(chunks + 1)
        ]
        parts = [jnp.where(bits[b], new, old) for new, old in zip(moved, parts)]
    parts = [jnp.where(live[k], parts[k], 0.0) for k in range(chunks)]
    sub = lax.broadcasted_iota(jnp.int32, (8, LANES), 0)
    half = blocks.shape[1] // 2
    chunk_half = chunks // 2
    for group in range(faults // 8):
        pieces = []
        for k in range(chunks):
            high, low = split(parts[k][group * 8 : group * 8 + 8])
            pieces.append(jnp.concatenate([high, low], axis=0))
        left = jnp.concatenate(pieces, axis=1)
        lefts[group] = left
        sums = [jnp.zeros((8, LANES), F32) for _ in range(chunk_half)]
        for place in range(8):
            f = group * 8 + place
            await_copy(copies, f)
            result = dot_nt(left[:, :half], blocks[f, :half, :half])
            result = result[:8] + result[8:]
            for k in range(chunk_half):
                sums[k] = jnp.where(sub == place, result[:, k * LANES : (k + 1) * LANES], sums[k])
        for k in range(chunks):
            found[k, group] = sums[k] if k < chunk_half else jnp.zeros((8, LANES), F32)
    count = jnp.int32(0)
    for f, (_, _, size) in enumerate(scalars):
        large[count] = f
        count = count + (size > half).astype(jnp.int32)

    def rest(step, carry):
        for u in range(UNROLL):
            place = step * UNROLL + u
            f = large[jnp.minimum(place, count - 1)]
            group = f // 8
            left = lefts[group]
            above = dot_nt(left[:, half:], blocks[f, :half, half:])
            below = dot_nt(left, blocks[f, half:, :])
            above = above[:8] + above[8:]
            below = below[:8] + below[8:]
            mine = jnp.logical_and(sub == f % 8, place < count)
            for k in range(chunk_half):
                piece = slice(k * LANES, (k + 1) * LANES)
                found[k, group] += jnp.where(mine, above[:, piece], 0.0)
                found[chunk_half + k, group] += jnp.where(mine, below[:, piece], 0.0)
        return carry

    lax.fori_loop(0, (count + UNROLL - 1) // UNROLL, rest, 0)
    parts = [
        jnp.where(live[k], found[k].reshape(faults, LANES), 0.0) for k in range(chunks)
    ]
    parts.append(jnp.zeros((faults, LANES), F32))
    for b in range(7):
        step = 1 << b
        rolled = [pltpu.roll(part, step, 1) for part in parts]
        moved = [
            jnp.where(lane >= step, rolled[k], rolled[k - 1] if k else 0.0)
            for k in range(chunks + 1)
        ]
        parts = [jnp.where(bits[b], new, old) for new, old in zip(moved, parts)]
    count = faults * (chunks + 1)
    for k in range(chunks + 1):
        stack[k * faults : (k + 1) * faults, :] = parts[k]
    depth = stack.shape[0]
    if depth > count:
        stack[count:depth, :] = jnp.zeros((depth - count, LANES), F32)
    place = lax.broadcasted_iota(jnp.int32, (1, depth), 1)
    chunk = jnp.zeros((1, depth), jnp.int32)
    for k in range(1, chunks + 1):
        chunk = chunk + (place >= k * faults).astype(jnp.int32)
    local = place - chunk * faults
    target = jnp.full((1, depth), -1, jnp.int32)
    for f, (tile, _, _) in enumerate(scalars):
        target = jnp.where(local == f, tile + chunk, target)
    target = jnp.where(place < count, target, -1)
    chosen = (lax.broadcasted_iota(jnp.int32, (rows, depth), 0) == target).astype(BF16)
    high, low = split(stack[...])
    return jnp.dot(chosen, high, preferred_element_type=F32) + jnp.dot(
        chosen, low, preferred_element_type=F32
    )


def set_field(field, value):
    tiles = value.shape[0]
    field[0:tiles, :] = value
    field[tiles:, :] = jnp.zeros((field.shape[0] - tiles, LANES), F32)


def first_kernel(far_sizes, far_rhs, far_friction, blocks, send, sizes, rhs, friction, sems, field, *work):
    tiles = rhs.shape[2] // LANES
    pairs = [(far_sizes, sizes), (far_rhs, rhs), (far_friction, friction)]
    copies = [pltpu.make_async_copy(a, b, sems.at[i]) for i, (a, b) in enumerate(pairs)]
    for copy in copies:
        copy.start()
    copies[0].wait()

    def value_to_field():
        copies[1].wait()
        set_field(field, load_rows(rhs, tiles))

    direction = precondition(sizes, blocks, field, work, value_to_field)[0:tiles]
    copies[2].wait()
    value = field[0:tiles, :]
    scaled = load_rows(friction, tiles) * direction
    send[...] = jnp.zeros_like(send)
    send[0:tiles, :] = direction
    send[tiles : tiles + 1, :] = lane_row([total(value * value), total(value * scaled)])


def gathered(parts, tiles):
    whole = parts[0][...]
    for part in parts[1:]:
        whole = whole + part[...]
    return whole[0:tiles], whole[tiles : tiles + 1]


def second_kernel(sizes, rhs, friction, blocks, sent, *refs):
    parts, (send, image_out, basis_out, field, *work) = refs[:-13], refs[-13:]
    tiles = rhs.shape[2] // LANES
    start = load_rows(rhs, tiles)
    diagonal = load_rows(friction, tiles)
    product, sums = gathered(parts, tiles)
    norm2 = pick(sums, 0)
    image = diagonal * sent[0:tiles, :] + product
    scale = lax.rsqrt(norm2)
    value = (image - pick(sums, 1) / norm2 * start) * scale
    image_out[...] = image
    basis_out[0:tiles, :] = value
    basis_out[tiles:, :] = jnp.broadcast_to(norm2, (basis_out.shape[0] - tiles, LANES))
    set_field(field, value)
    direction = precondition(sizes, blocks, field, work)[0:tiles]
    scaled = diagonal * direction
    send[...] = jnp.zeros_like(send)
    send[0:tiles, :] = direction
    send[tiles : tiles + 1, :] = lane_row(
        [
            total(value * value),
            total(start * value) * scale,
            total(start * scaled) * scale,
            total(value * scaled),
        ]
    )


def third_kernel(sizes, rhs, friction, blocks, sent, basis, *refs):
    parts, (send, image_out, field, *work) = refs[:-12], refs[-12:]
    tiles = rhs.shape[2] // LANES
    start = load_rows(rhs, tiles)
    diagonal = load_rows(friction, tiles)
    product, sums = gathered(parts, tiles)
    image = diagonal * sent[0:tiles, :] + product
    value = basis[0:tiles, :]
    scale = lax.rsqrt(basis[tiles : tiles + 1, 0:1])
    norm2, cross, along_start, along = [pick(sums, k) for k in range(4)]
    left = norm2 - cross * cross
    usable = left > 1e-5 * norm2
    along = jnp.where(usable, (along - cross * along_start) / jnp.where(usable, left, 1.0), 0.0)
    along_start = along_start - cross * along
    value = (image - along * value - (along_start * scale) * start) * lax.rsqrt(
        jnp.maximum(norm2, 1e-30)
    )
    image_out[...] = image
    set_field(field, value)
    direction = precondition(sizes, blocks, field, work)[0:tiles]
    send[...] = jnp.zeros_like(send)
    send[0:tiles, :] = direction


def fourth_kernel(rhs, friction, sent, image0, image1, *refs):
    parts, (image_out, sums_out) = refs[:-2], refs[-2:]
    tiles = rhs.shape[2] // LANES
    start = load_rows(rhs, tiles)
    product, _ = gathered(parts, tiles)
    image = load_rows(friction, tiles) * sent[0:tiles, :] + product
    image_out[...] = image
    images = [image0[...], image1[...], image]
    values = [total(images[i] * images[j]) for i in range(3) for j in range(i + 1)]
    values += [total(start * one) for one in images]
    sums_out[...] = jnp.broadcast_to(lane_row(values), sums_out.shape)


def last_kernel(sums, rhs, image0, image1, image2, sent0, sent1, sent2, update, residual):
    tiles = rhs.shape[2] // LANES
    row = jnp.sum(sums[...], axis=0, keepdims=True)
    entries = [pick(row, k) for k in range(9)]
    scale = [lax.rsqrt(jnp.maximum(entries[k], 1e-30)) for k in (0, 2, 5)]
    gram = {}
    place = 0
    for i in range(3):
        for j in range(i + 1):
            gram[i, j] = entries[place] * scale[i] * scale[j]
            place += 1
    goal = [entries[6 + i] * scale[i] for i in range(3)]
    low10 = gram[1, 0]
    low20 = gram[2, 0]
    pivot1 = 1.0 - low10 * low10
    keep1 = pivot1 > 1e-6
    inverse1 = jnp.where(keep1, 1.0 / jnp.where(keep1, pivot1, 1.0), 0.0)
    cross = gram[2, 1] - low20 * low10
    low21 = cross * inverse1
    pivot2 = 1.0 - low20 * low20 - cross * low21
    keep2 = pivot2 > 1e-6
    inverse2 = jnp.where(keep2, 1.0 / jnp.where(keep2, pivot2, 1.0), 0.0)
    part1 = goal[1] - low10 * goal[0]
    part2 = goal[2] - low20 * goal[0] - low21 * part1
    weight2 = part2 * inverse2
    weight1 = part1 * inverse1 - low21 * weight2
    weight0 = goal[0] - low10 * weight1 - low20 * weight2
    weights = [weight0 * scale[0], weight1 * scale[1], weight2 * scale[2]]
    start = load_rows(rhs, tiles)
    best = (
        weights[0] * sent0[0:tiles, :]
        + weights[1] * sent1[0:tiles, :]
        + weights[2] * sent2[0:tiles, :]
    )
    rest = start - weights[0] * image0[...] - weights[1] * image1[...] - weights[2] * image2[...]
    for k in range(tiles):
        update[0, :, pl.ds(k * LANES, LANES)] = best[k : k + 1]
        residual[0, :, pl.ds(k * LANES, LANES)] = rest[k : k + 1]


def tiles_kernel(tail, spots, rows, weight, remote, *refs):
    sent, (keep, give, blocks, field, found, products, sems) = refs[:-7], refs[-7:]
    slots = blocks.shape[0]
    far, height = keep.shape[0], keep.shape[1]
    groups = slots // 16
    copies = []
    for group in range(groups):
        copy = pltpu.make_async_copy(
            remote.at[0, 0, pl.ds(group * 16, 16)],
            blocks.at[pl.ds(group * 16, 16)],
            sems.at[group],
        )
        copies.append(copy)
    for copy in copies[:AHEAD]:
        copy.start()
    for k, one in enumerate(sent):
        field[k * height : (k + 1) * height, :] = one[...]
    for t in range(slots):
        found[t : t + 1, :] = field[pl.ds(spots[0, t], 1), :]
    sub = lax.broadcasted_iota(jnp.int32, (8, LANES), 0)
    blank = jnp.zeros((8, LANES), F32)
    for group in range(groups):
        await_copy(copies, group)
        base = group * 16
        top = jnp.concatenate([found[base : base + 8, :], blank], axis=1)
        bottom = jnp.concatenate([blank, found[base + 8 : base + 16, :]], axis=1)
        left = jnp.concatenate([top, bottom], axis=0).astype(BF16)
        first, second = blank, blank
        for p in range(4):
            a, b = base + 2 * p, base + 2 * p + 1
            right = jnp.concatenate(
                [
                    jnp.concatenate([blocks[a], blocks[a + 8]], axis=1),
                    jnp.concatenate([blocks[b], blocks[b + 8]], axis=1),
                ],
                axis=0,
            )
            result = dot_nt(left, right)
            for spot, half in ((2 * p, slice(0, LANES)), (2 * p + 1, slice(LANES, 2 * LANES))):
                first = jnp.where(sub == spot, result[:8, half], first)
                second = jnp.where(sub == spot, result[8:, half], second)
        products[base : base + 8, :] = first
        products[base + 8 : base + 16, :] = second
    high, low = split(products[...])
    target = rows[...]
    chosen = jnp.where(
        lax.broadcasted_iota(jnp.int32, (2 * far * height, slots), 0) == target, weight[...], 0.0
    )
    chosen_high, chosen_low = split(chosen)
    value = (
        jnp.dot(chosen_high, high, preferred_element_type=F32)
        + jnp.dot(chosen_low, high, preferred_element_type=F32)
        + jnp.dot(chosen_high, low, preferred_element_type=F32)
    )
    keep[...] = value[: far * height].reshape(far, height, LANES)
    give[...] = value[far * height :].reshape(far, height, LANES)
    last = height - 8
    sums = sent[0][last:height, :]
    for one in sent[1:]:
        sums = sums + one[last:height, :]
    sums = jnp.where(lax.broadcasted_iota(jnp.int32, (8, LANES), 0) == tail, sums, 0.0)
    for k in range(far):
        keep[k, last:height, :] += sums
        give[k, last:height, :] += sums


def scratch(shape, dtype=F32):
    return pltpu.VMEM(shape, dtype)


def local(
    rhs,
    friction,
    kernel_tiles,
    tile_scale,
    tile_row,
    tile_col,
    tile_counts,
    precond_blocks,
    fault_sizes,
):
    length = rhs.shape[2]
    slots = kernel_tiles.shape[2]
    faults, width = precond_blocks.shape[2], precond_blocks.shape[3]
    tiles = length // LANES
    height = (tiles + 8) // 8 * 8
    chunks = width // LANES
    row_count = lax.axis_size("row")
    col_count = lax.axis_size("col")
    my_row = lax.axis_index("row")
    my_col = lax.axis_index("col")
    far = col_count // 2
    rows = (tiles + chunks + 8) // 8 * 8
    depth = (faults * (chunks + 1) + LANES - 1) // LANES * LANES

    place = tile_col[0, 0] // tiles ^ my_row
    spots = (place * height + tile_col[0, 0] % tiles).reshape(1, slots)
    place = tile_row[0, 0] // tiles ^ my_col
    place = place % 2 * far + place // 2
    target = (place * height + tile_row[0, 0] % tiles).reshape(1, slots)
    weight = jnp.where(
        jnp.arange(slots, dtype=jnp.int32) < tile_counts[0, 0], tile_scale[0, 0], 0.0
    ).reshape(1, slots)

    kernel_tiles = pltpu.with_memory_space_constraint(kernel_tiles, pltpu.HBM)
    precond_blocks = pltpu.with_memory_space_constraint(precond_blocks, pltpu.HBM)
    grid = jax.ShapeDtypeStruct((height, LANES), F32)
    plain = jax.ShapeDtypeStruct((tiles, LANES), F32)
    half_grid = jax.ShapeDtypeStruct((far, height, LANES), F32)
    work = [
        scratch((rows, LANES)),
        scratch((faults, width, width), BF16),
        scratch((chunks + 1, faults, LANES)),
        scratch((faults, LANES), jnp.int32),
        scratch((faults, LANES), jnp.int32),
        scratch((depth, LANES)),
        scratch((faults // 8, 16, width), BF16),
        scratch((chunks, faults // 8, 8, LANES)),
        pltpu.SMEM((faults + 1,), jnp.int32),
        pltpu.SemaphoreType.DMA((faults,)),
    ]

    def exchange(value, axis, distance):
        size = lax.axis_size(axis)
        return lax.ppermute(value, axis, [(i, i ^ distance) for i in range(size)])

    def apply_kernel(sent):
        got = [sent] + [exchange(sent, "row", d) for d in range(1, row_count)]
        keep, give = pl.pallas_call(
            functools.partial(tiles_kernel, tiles % 8),
            out_shape=[half_grid, half_grid],
            in_specs=[SMEM, VMEM, VMEM, HBM] + [VMEM] * row_count,
            out_specs=[VMEM] * 2,
            scratch_shapes=[
                scratch((slots, LANES, LANES), BF16),
                scratch((row_count * height, LANES)),
                scratch((slots, LANES)),
                scratch((slots, LANES)),
                pltpu.SemaphoreType.DMA((slots // 16,)),
            ],
            compiler_params=PARAMS,
            name="tiles",
        )(spots, target, weight, kernel_tiles, *got)
        both = keep + exchange(give, "col", 1)
        return [both[0]] + [exchange(both[d], "col", 2 * d) for d in range(1, far)]

    sent0 = pl.pallas_call(
        first_kernel,
        out_shape=grid,
        in_specs=[HBM] * 4,
        out_specs=VMEM,
        scratch_shapes=[
            pltpu.SMEM(fault_sizes.shape, jnp.int32),
            scratch(rhs.shape),
            scratch(friction.shape),
            pltpu.SemaphoreType.DMA((3,)),
        ]
        + work,
        compiler_params=PARAMS,
        name="first",
    )(*[pltpu.with_memory_space_constraint(a, pltpu.HBM) for a in (fault_sizes, rhs, friction)], precond_blocks)
    parts0 = apply_kernel(sent0)
    sent1, image0, basis = pl.pallas_call(
        second_kernel,
        out_shape=[grid, plain, grid],
        in_specs=[SMEM, VMEM, VMEM, HBM] + [VMEM] * (1 + far),
        out_specs=[VMEM] * 3,
        scratch_shapes=work,
        compiler_params=PARAMS,
        name="second",
    )(fault_sizes, rhs, friction, precond_blocks, sent0, *parts0)
    parts1 = apply_kernel(sent1)
    sent2, image1 = pl.pallas_call(
        third_kernel,
        out_shape=[grid, plain],
        in_specs=[SMEM, VMEM, VMEM, HBM] + [VMEM] * (2 + far),
        out_specs=[VMEM] * 2,
        scratch_shapes=work,
        compiler_params=PARAMS,
        name="third",
    )(fault_sizes, rhs, friction, precond_blocks, sent1, basis, *parts1)
    parts2 = apply_kernel(sent2)
    devices = row_count * col_count
    image2, sums = pl.pallas_call(
        fourth_kernel,
        out_shape=[plain, jax.ShapeDtypeStruct((devices, LANES), F32)],
        in_specs=[VMEM] * (5 + far),
        out_specs=[VMEM] * 2,
        compiler_params=PARAMS,
        name="fourth",
    )(rhs, friction, sent2, image0, image1, *parts2)
    sums = lax.all_to_all(sums, ("row", "col"), 0, 0, tiled=True)
    whole = jax.ShapeDtypeStruct((1, 1, length), F32)
    return pl.pallas_call(
        last_kernel,
        out_shape=[whole, whole],
        in_specs=[VMEM] * 8,
        out_specs=[VMEM] * 2,
        compiler_params=PARAMS,
        name="last",
    )(sums, rhs, image0, image1, image2, sent0, sent1, sent2)


def solution(mesh):
    return jax.shard_map(
        local,
        mesh=mesh,
        in_specs=(
            P("row", "col", None),
            P("row", "col", None),
            P("row", "col", None, None, None),
            P("row", "col", None),
            P("row", "col", None),
            P("row", "col", None),
            P("row", "col"),
            P("row", "col", None, None, None),
            P("row", "col", None),
        ),
        out_specs=(P("row", "col", None), P("row", "col", None)),
        check_vma=False,
    )
```

```python
import functools

import jax
import jax.numpy as jnp
from jax import lax
from jax.experimental import pallas as pl
from jax.experimental.pallas import tpu as pltpu
from jax.sharding import PartitionSpec as P

LANES = 128
UNROLL = 3
F32 = jnp.float32
BF16 = jnp.bfloat16
VMEM = pl.BlockSpec(memory_space=pltpu.VMEM)
SMEM = pl.BlockSpec(memory_space=pltpu.SMEM)
HBM = pl.BlockSpec(memory_space=pltpu.HBM)
PARAMS = pltpu.CompilerParams(vmem_limit_bytes=6 << 20)


def dot_nt(left, right):
    return lax.dot_general(left, right, (((1,), (1,)), ((), ())), preferred_element_type=F32)


def split(value):
    high = value.astype(BF16)
    low = (value - high.astype(F32)).astype(BF16)
    return high, low


def total(value):
    return jnp.sum(jnp.sum(value, axis=0, keepdims=True), axis=1, keepdims=True)


def lane_row(values):
    lane = lax.broadcasted_iota(jnp.int32, (1, LANES), 1)
    row = jnp.zeros((1, LANES), F32)
    for place, value in enumerate(values):
        row = jnp.where(lane == place, value, row)
    return row


def pick(row, place):
    lane = lax.broadcasted_iota(jnp.int32, (1, LANES), 1)
    return jnp.sum(jnp.where(lane == place, row, 0.0), axis=1, keepdims=True)


def load_rows(ref, count):
    return jnp.concatenate(
        [ref[0, :, pl.ds(k * LANES, LANES)] for k in range(count)], axis=0
    )


def fault_scalars(sizes, faults):
    start = jnp.int32(0)
    scalars = []
    for f in range(faults):
        scalars.append((start // LANES, start % LANES, sizes[0, 0, f]))
        start = start + sizes[0, 0, f]
    return scalars


def quarters(remote, blocks, sems, f, which):
    half = blocks.shape[1] // 2
    near, far = pl.ds(0, half), pl.ds(half, half)
    return [
        pltpu.make_async_copy(
            remote.at[(0, 0, f) + part], blocks.at[(f,) + part], sems.at[place, f]
        )
        for place, part in list(enumerate([(near, near), (near, far), (far,)]))[which]
    ]


def fetch(scalars, remote, blocks, sems):
    half = blocks.shape[1] // 2
    for f in range(len(scalars)):
        quarters(remote, blocks, sems, f, slice(0, 1))[0].start()
    for f, (_, _, size) in enumerate(scalars):

        @pl.when(size > half)
        def _():
            for copy in quarters(remote, blocks, sems, f, slice(1, 3)):
                copy.start()


def precondition(sizes, remote, field, work, begin=None):
    windows, shifts, lens, stack, lefts, found, large = work[:7]
    local = len(work) == 7
    blocks, sems = (remote, None) if local else work[7:]
    faults = blocks.shape[0]
    chunks = blocks.shape[1] // LANES
    rows = field.shape[0]
    scalars = fault_scalars(sizes, faults)
    if not local:
        fetch(scalars, remote, blocks, sems)
    if begin is not None:
        begin()
    lane = lax.broadcasted_iota(jnp.int32, (faults, LANES), 1)
    for f, (tile, shift, size) in enumerate(scalars):
        shifts[f : f + 1, :] = jnp.full((1, LANES), shift, jnp.int32)
        lens[f : f + 1, :] = jnp.full((1, LANES), size, jnp.int32)
        for k in range(chunks + 1):
            windows[k, f : f + 1, :] = field[pl.ds(tile + k, 1), :]
    shift = shifts[...]
    size = lens[...]
    bits = [((shift >> b) & 1) == 1 for b in range(7)]
    live = [lane + k * LANES < size for k in range(chunks)]
    parts = [windows[k] for k in range(chunks + 1)]
    for b in range(7):
        step = 1 << b
        rolled = [pltpu.roll(part, LANES - step, 1) for part in parts]
        moved = [
            jnp.where(lane < LANES - step, rolled[k], rolled[min(k + 1, chunks)])
            for k in range(chunks + 1)
        ]
        parts = [jnp.where(bits[b], new, old) for new, old in zip(moved, parts)]
    parts = [jnp.where(live[k], parts[k], 0.0) for k in range(chunks)]
    sub = lax.broadcasted_iota(jnp.int32, (8, LANES), 0)
    half = blocks.shape[1] // 2
    chunk_half = chunks // 2
    for group in range(faults // 8):
        pieces = []
        for k in range(chunks):
            high, low = split(parts[k][group * 8 : group * 8 + 8])
            pieces.append(jnp.concatenate([high, low], axis=0))
        left = jnp.concatenate(pieces, axis=1)
        lefts[group] = left
        sums = [jnp.zeros((8, LANES), F32) for _ in range(chunk_half)]
        for place in range(8):
            f = group * 8 + place
            if not local:
                quarters(remote, blocks, sems, f, slice(0, 1))[0].wait()
            result = dot_nt(left[:, :half], blocks[f, :half, :half])
            result = result[:8] + result[8:]
            for k in range(chunk_half):
                sums[k] = jnp.where(sub == place, result[:, k * LANES : (k + 1) * LANES], sums[k])
        for k in range(chunks):
            found[k, group] = sums[k] if k < chunk_half else jnp.zeros((8, LANES), F32)
    count = jnp.int32(0)
    for f, (_, _, size) in enumerate(scalars):
        large[count] = f
        count = count + (size > half).astype(jnp.int32)

    def rest(step, carry):
        for u in range(UNROLL):
            place = step * UNROLL + u
            f = large[jnp.minimum(place, count - 1)]
            group = f // 8
            left = lefts[group]
            if not local:

                @pl.when(place < count)
                def _():
                    for copy in quarters(remote, blocks, sems, f, slice(1, 3)):
                        copy.wait()

            above = dot_nt(left[:, half:], blocks[f, :half, half:])
            below = dot_nt(left, blocks[f, half:, :])
            above = above[:8] + above[8:]
            below = below[:8] + below[8:]
            mine = jnp.logical_and(sub == f % 8, place < count)
            for k in range(chunk_half):
                piece = slice(k * LANES, (k + 1) * LANES)
                found[k, group] += jnp.where(mine, above[:, piece], 0.0)
                found[chunk_half + k, group] += jnp.where(mine, below[:, piece], 0.0)
        return carry

    lax.fori_loop(0, (count + UNROLL - 1) // UNROLL, rest, 0)
    parts = [
        jnp.where(live[k], found[k].reshape(faults, LANES), 0.0) for k in range(chunks)
    ]
    parts.append(jnp.zeros((faults, LANES), F32))
    for b in range(7):
        step = 1 << b
        rolled = [pltpu.roll(part, step, 1) for part in parts]
        moved = [
            jnp.where(lane >= step, rolled[k], rolled[k - 1] if k else 0.0)
            for k in range(chunks + 1)
        ]
        parts = [jnp.where(bits[b], new, old) for new, old in zip(moved, parts)]
    count = faults * (chunks + 1)
    for k in range(chunks + 1):
        stack[k * faults : (k + 1) * faults, :] = parts[k]
    depth = stack.shape[0]
    if depth > count:
        stack[count:depth, :] = jnp.zeros((depth - count, LANES), F32)
    place = lax.broadcasted_iota(jnp.int32, (1, depth), 1)
    chunk = jnp.zeros((1, depth), jnp.int32)
    for k in range(1, chunks + 1):
        chunk = chunk + (place >= k * faults).astype(jnp.int32)
    local = place - chunk * faults
    target = jnp.full((1, depth), -1, jnp.int32)
    for f, (tile, _, _) in enumerate(scalars):
        target = jnp.where(local == f, tile + chunk, target)
    target = jnp.where(place < count, target, -1)
    chosen = (lax.broadcasted_iota(jnp.int32, (rows, depth), 0) == target).astype(BF16)
    high, low = split(stack[...])
    return jnp.dot(chosen, high, preferred_element_type=F32) + jnp.dot(
        chosen, low, preferred_element_type=F32
    )


def set_field(field, value):
    tiles = value.shape[0]
    field[0:tiles, :] = value
    field[tiles:, :] = jnp.zeros((field.shape[0] - tiles, LANES), F32)


def owner(index, each, count):
    found = jnp.zeros(index.shape, jnp.int32)
    for c in range(1, count):
        found = found + (index >= c * each).astype(jnp.int32)
    return found


def first_kernel(shape, *refs):
    (blocks, far_tiles, send, near_blocks, near_tiles, spots, target) = refs[5:12]
    (sizes, rhs, friction, tile_row, tile_col) = refs[12:17]
    (sems, tiles_sem, block_sems, field, *work) = refs[17:]
    work = work + [near_blocks, block_sems]
    row_count, col_count = shape
    tiles = rhs.shape[2] // LANES
    height = send.shape[0]
    pairs = list(zip(refs[:5], refs[12:17]))
    copies = [pltpu.make_async_copy(a, b, sems.at[i]) for i, (a, b) in enumerate(pairs)]
    for copy in copies:
        copy.start()
    whole = pltpu.make_async_copy(far_tiles.at[0, 0], near_tiles, tiles_sem)
    copies[0].wait()

    def value_to_field():
        whole.start()
        copies[1].wait()
        set_field(field, load_rows(rhs, tiles))
        for copy in copies[3:]:
            copy.wait()
        column = tile_col[0]
        source = owner(column, tiles, row_count)
        spots[...] = (source ^ lax.axis_index("row")) * height + column - source * tiles
        row = tile_row[0]
        source = owner(row, tiles, col_count)
        place = source ^ lax.axis_index("col")
        place = (place & 1) * (col_count // 2) + (place >> 1)
        target[...] = place * height + row - source * tiles

    direction = precondition(sizes, blocks, field, work, value_to_field)[0:tiles]
    copies[2].wait()
    whole.wait()
    value = field[0:tiles, :]
    scaled = load_rows(friction, tiles) * direction
    send[...] = jnp.zeros_like(send)
    send[0:tiles, :] = direction
    send[tiles : tiles + 1, :] = lane_row([total(value * value), total(value * scaled)])


def gathered(parts, tiles):
    whole = parts[0][...]
    for part in parts[1:]:
        whole = whole + part[...]
    return whole[0:tiles], whole[tiles : tiles + 1]


def second_kernel(sizes, rhs, friction, blocks, sent, *refs):
    parts, (send, image_out, basis_out, field, *work) = refs[:-11], refs[-11:]
    tiles = rhs.shape[2] // LANES
    start = load_rows(rhs, tiles)
    diagonal = load_rows(friction, tiles)
    product, sums = gathered(parts, tiles)
    norm2 = pick(sums, 0)
    image = diagonal * sent[0:tiles, :] + product
    scale = lax.rsqrt(norm2)
    value = (image - pick(sums, 1) / norm2 * start) * scale
    image_out[...] = image
    basis_out[0:tiles, :] = value
    basis_out[tiles:, :] = jnp.broadcast_to(norm2, (basis_out.shape[0] - tiles, LANES))
    set_field(field, value)
    direction = precondition(sizes, blocks, field, work)[0:tiles]
    scaled = diagonal * direction
    send[...] = jnp.zeros_like(send)
    send[0:tiles, :] = direction
    send[tiles : tiles + 1, :] = lane_row(
        [
            total(value * value),
            total(start * value) * scale,
            total(start * scaled) * scale,
            total(value * scaled),
        ]
    )


def third_kernel(sizes, rhs, friction, blocks, sent, basis, *refs):
    parts, (send, image_out, field, *work) = refs[:-10], refs[-10:]
    tiles = rhs.shape[2] // LANES
    start = load_rows(rhs, tiles)
    diagonal = load_rows(friction, tiles)
    product, sums = gathered(parts, tiles)
    image = diagonal * sent[0:tiles, :] + product
    value = basis[0:tiles, :]
    scale = lax.rsqrt(basis[tiles : tiles + 1, 0:1])
    norm2, cross, along_start, along = [pick(sums, k) for k in range(4)]
    left = norm2 - cross * cross
    usable = left > 1e-5 * norm2
    along = jnp.where(usable, (along - cross * along_start) / jnp.where(usable, left, 1.0), 0.0)
    along_start = along_start - cross * along
    value = (image - along * value - (along_start * scale) * start) * lax.rsqrt(
        jnp.maximum(norm2, 1e-30)
    )
    image_out[...] = image
    set_field(field, value)
    direction = precondition(sizes, blocks, field, work)[0:tiles]
    send[...] = jnp.zeros_like(send)
    send[0:tiles, :] = direction


def fourth_kernel(rhs, friction, sent, image0, image1, *refs):
    parts, (image_out, sums_out) = refs[:-2], refs[-2:]
    tiles = rhs.shape[2] // LANES
    start = load_rows(rhs, tiles)
    product, _ = gathered(parts, tiles)
    image = load_rows(friction, tiles) * sent[0:tiles, :] + product
    image_out[...] = image
    images = [image0[...], image1[...], image]
    values = [total(images[i] * images[j]) for i in range(3) for j in range(i + 1)]
    values += [total(start * one) for one in images]
    sums_out[...] = jnp.broadcast_to(lane_row(values), sums_out.shape)


def last_kernel(sums, rhs, image0, image1, image2, sent0, sent1, sent2, update, residual):
    tiles = rhs.shape[2] // LANES
    row = jnp.sum(sums[...], axis=0, keepdims=True)
    entries = [pick(row, k) for k in range(9)]
    scale = [lax.rsqrt(jnp.maximum(entries[k], 1e-30)) for k in (0, 2, 5)]
    gram = {}
    place = 0
    for i in range(3):
        for j in range(i + 1):
            gram[i, j] = entries[place] * scale[i] * scale[j]
            place += 1
    goal = [entries[6 + i] * scale[i] for i in range(3)]
    low10 = gram[1, 0]
    low20 = gram[2, 0]
    pivot1 = 1.0 - low10 * low10
    keep1 = pivot1 > 1e-6
    inverse1 = jnp.where(keep1, 1.0 / jnp.where(keep1, pivot1, 1.0), 0.0)
    cross = gram[2, 1] - low20 * low10
    low21 = cross * inverse1
    pivot2 = 1.0 - low20 * low20 - cross * low21
    keep2 = pivot2 > 1e-6
    inverse2 = jnp.where(keep2, 1.0 / jnp.where(keep2, pivot2, 1.0), 0.0)
    part1 = goal[1] - low10 * goal[0]
    part2 = goal[2] - low20 * goal[0] - low21 * part1
    weight2 = part2 * inverse2
    weight1 = part1 * inverse1 - low21 * weight2
    weight0 = goal[0] - low10 * weight1 - low20 * weight2
    weights = [weight0 * scale[0], weight1 * scale[1], weight2 * scale[2]]
    start = load_rows(rhs, tiles)
    best = (
        weights[0] * sent0[0:tiles, :]
        + weights[1] * sent1[0:tiles, :]
        + weights[2] * sent2[0:tiles, :]
    )
    rest = start - weights[0] * image0[...] - weights[1] * image1[...] - weights[2] * image2[...]
    for k in range(tiles):
        update[0, :, pl.ds(k * LANES, LANES)] = best[k : k + 1]
        residual[0, :, pl.ds(k * LANES, LANES)] = rest[k : k + 1]


def tiles_kernel(tail, counts, spots, rows, scale, blocks, *refs):
    sent, (keep, give, field, found, products) = refs[:-5], refs[-5:]
    slots = blocks.shape[0]
    far, height = keep.shape[0], keep.shape[1]
    groups = slots // 16
    for k, one in enumerate(sent):
        field[k * height : (k + 1) * height, :] = one[...]
    for t in range(slots):
        found[t : t + 1, :] = field[pl.ds(spots[0, t], 1), :]
    sub = lax.broadcasted_iota(jnp.int32, (8, LANES), 0)
    blank = jnp.zeros((8, LANES), F32)
    for group in range(groups):
        base = group * 16
        top = jnp.concatenate([found[base : base + 8, :], blank], axis=1)
        bottom = jnp.concatenate([blank, found[base + 8 : base + 16, :]], axis=1)
        left = jnp.concatenate([top, bottom], axis=0).astype(BF16)
        first, second = blank, blank
        for p in range(4):
            a, b = base + 2 * p, base + 2 * p + 1
            right = jnp.concatenate(
                [
                    jnp.concatenate([blocks[a], blocks[a + 8]], axis=1),
                    jnp.concatenate([blocks[b], blocks[b + 8]], axis=1),
                ],
                axis=0,
            )
            result = dot_nt(left, right)
            for spot, half in ((2 * p, slice(0, LANES)), (2 * p + 1, slice(LANES, 2 * LANES))):
                first = jnp.where(sub == spot, result[:8, half], first)
                second = jnp.where(sub == spot, result[8:, half], second)
        products[base : base + 8, :] = first
        products[base + 8 : base + 16, :] = second
    high, low = split(products[...])
    target = rows[...]
    slot = lax.broadcasted_iota(jnp.int32, target.shape, 1)
    weight = jnp.where(slot < counts[0, 0], scale[0], 0.0)
    chosen = jnp.where(
        lax.broadcasted_iota(jnp.int32, (2 * far * height, slots), 0) == target, weight, 0.0
    )
    chosen_high, chosen_low = split(chosen)
    value = (
        jnp.dot(chosen_high, high, preferred_element_type=F32)
        + jnp.dot(chosen_low, high, preferred_element_type=F32)
        + jnp.dot(chosen_high, low, preferred_element_type=F32)
    )
    keep[...] = value[: far * height].reshape(far, height, LANES)
    give[...] = value[far * height :].reshape(far, height, LANES)
    last = height - 8
    sums = sent[0][last:height, :]
    for one in sent[1:]:
        sums = sums + one[last:height, :]
    sums = jnp.where(lax.broadcasted_iota(jnp.int32, (8, LANES), 0) == tail, sums, 0.0)
    for k in range(far):
        keep[k, last:height, :] += sums
        give[k, last:height, :] += sums


def scratch(shape, dtype=F32):
    return pltpu.VMEM(shape, dtype)


def local(
    rhs,
    friction,
    kernel_tiles,
    tile_scale,
    tile_row,
    tile_col,
    tile_counts,
    precond_blocks,
    fault_sizes,
):
    length = rhs.shape[2]
    slots = kernel_tiles.shape[2]
    faults, width = precond_blocks.shape[2], precond_blocks.shape[3]
    tiles = length // LANES
    height = (tiles + 8) // 8 * 8
    chunks = width // LANES
    row_count = lax.axis_size("row")
    col_count = lax.axis_size("col")
    far = col_count // 2
    rows = (tiles + chunks + 8) // 8 * 8
    depth = (faults * (chunks + 1) + LANES - 1) // LANES * LANES

    grid = jax.ShapeDtypeStruct((height, LANES), F32)
    plain = jax.ShapeDtypeStruct((tiles, LANES), F32)
    half_grid = jax.ShapeDtypeStruct((far, height, LANES), F32)
    work = [
        scratch((rows, LANES)),
        scratch((chunks + 1, faults, LANES)),
        scratch((faults, LANES), jnp.int32),
        scratch((faults, LANES), jnp.int32),
        scratch((depth, LANES)),
        scratch((faults // 8, 16, width), BF16),
        scratch((chunks, faults // 8, 8, LANES)),
        pltpu.SMEM((faults + 1,), jnp.int32),
    ]

    def exchange(value, axis, distance):
        size = lax.axis_size(axis)
        return lax.ppermute(value, axis, [(i, i ^ distance) for i in range(size)])

    inputs = (fault_sizes, rhs, friction, tile_row, tile_col, precond_blocks, kernel_tiles)
    places = jax.ShapeDtypeStruct((1, slots), jnp.int32)
    sent0, near_blocks, near_tiles, spots, target = pl.pallas_call(
        functools.partial(first_kernel, (row_count, col_count)),
        out_shape=[
            grid,
            pltpu.VMEM((faults, width, width), BF16),
            pltpu.VMEM((slots, LANES, LANES), BF16),
            places,
            places,
        ],
        in_specs=[HBM] * 7,
        out_specs=[VMEM] * 5,
        scratch_shapes=[
            pltpu.SMEM(fault_sizes.shape, jnp.int32),
            scratch(rhs.shape),
            scratch(friction.shape),
            scratch(tile_row.shape, jnp.int32),
            scratch(tile_col.shape, jnp.int32),
            pltpu.SemaphoreType.DMA((5,)),
            pltpu.SemaphoreType.DMA,
            pltpu.SemaphoreType.DMA((3, faults)),
        ]
        + work,
        compiler_params=PARAMS,
        name="first",
    )(*[pltpu.with_memory_space_constraint(a, pltpu.HBM) for a in inputs])

    def apply_kernel(sent):
        got = [sent] + [exchange(sent, "row", d) for d in range(1, row_count)]
        keep, give = pl.pallas_call(
            functools.partial(tiles_kernel, tiles % 8),
            out_shape=[half_grid, half_grid],
            in_specs=[SMEM, SMEM, VMEM, VMEM, VMEM] + [VMEM] * row_count,
            out_specs=[VMEM] * 2,
            scratch_shapes=[
                scratch((row_count * height, LANES)),
                scratch((slots, LANES)),
                scratch((slots, LANES)),
            ],
            compiler_params=PARAMS,
            name="tiles",
        )(tile_counts, spots, target, tile_scale, near_tiles, *got)
        both = keep + exchange(give, "col", 1)
        return [both[0]] + [exchange(both[d], "col", 2 * d) for d in range(1, far)]

    parts0 = apply_kernel(sent0)
    sent1, image0, basis = pl.pallas_call(
        second_kernel,
        out_shape=[grid, plain, grid],
        in_specs=[SMEM, VMEM, VMEM, VMEM] + [VMEM] * (1 + far),
        out_specs=[VMEM] * 3,
        scratch_shapes=work,
        compiler_params=PARAMS,
        name="second",
    )(fault_sizes, rhs, friction, near_blocks, sent0, *parts0)
    parts1 = apply_kernel(sent1)
    sent2, image1 = pl.pallas_call(
        third_kernel,
        out_shape=[grid, plain],
        in_specs=[SMEM, VMEM, VMEM, VMEM] + [VMEM] * (2 + far),
        out_specs=[VMEM] * 2,
        scratch_shapes=work,
        compiler_params=PARAMS,
        name="third",
    )(fault_sizes, rhs, friction, near_blocks, sent1, basis, *parts1)
    parts2 = apply_kernel(sent2)
    devices = row_count * col_count
    image2, sums = pl.pallas_call(
        fourth_kernel,
        out_shape=[plain, jax.ShapeDtypeStruct((devices, LANES), F32)],
        in_specs=[VMEM] * (5 + far),
        out_specs=[VMEM] * 2,
        compiler_params=PARAMS,
        name="fourth",
    )(rhs, friction, sent2, image0, image1, *parts2)
    sums = lax.all_to_all(sums, ("row", "col"), 0, 0, tiled=True)
    whole = jax.ShapeDtypeStruct((1, 1, length), F32)
    return pl.pallas_call(
        last_kernel,
        out_shape=[whole, whole],
        in_specs=[VMEM] * 8,
        out_specs=[VMEM] * 2,
        compiler_params=PARAMS,
        name="last",
    )(sums, rhs, image0, image1, image2, sent0, sent1, sent2)


def solution(mesh):
    return jax.shard_map(
        local,
        mesh=mesh,
        in_specs=(
            P("row", "col", None),
            P("row", "col", None),
            P("row", "col", None, None, None),
            P("row", "col", None),
            P("row", "col", None),
            P("row", "col", None),
            P("row", "col"),
            P("row", "col", None, None, None),
            P("row", "col", None),
        ),
        out_specs=(P("row", "col", None), P("row", "col", None)),
        check_vma=False,
    )
```

```python
import functools

import jax
import jax.numpy as jnp
from jax import lax
from jax.experimental import pallas as pl
from jax.experimental.pallas import tpu as pltpu
from jax.sharding import PartitionSpec as P

LANES = 128
UNROLL = 3
F32 = jnp.float32
BF16 = jnp.bfloat16
VMEM = pl.BlockSpec(memory_space=pltpu.VMEM)
SMEM = pl.BlockSpec(memory_space=pltpu.SMEM)
HBM = pl.BlockSpec(memory_space=pltpu.HBM)
PARAMS = pltpu.CompilerParams(vmem_limit_bytes=6 << 20)


def dot_nt(left, right):
    return lax.dot_general(left, right, (((1,), (1,)), ((), ())), preferred_element_type=F32)


def split(value):
    high = value.astype(BF16)
    low = (value - high.astype(F32)).astype(BF16)
    return high, low


def total(value):
    return jnp.sum(jnp.sum(value, axis=0, keepdims=True), axis=1, keepdims=True)


def lane_row(values):
    lane = lax.broadcasted_iota(jnp.int32, (1, LANES), 1)
    row = jnp.zeros((1, LANES), F32)
    for place, value in enumerate(values):
        row = jnp.where(lane == place, value, row)
    return row


def pick(row, place):
    lane = lax.broadcasted_iota(jnp.int32, (1, LANES), 1)
    return jnp.sum(jnp.where(lane == place, row, 0.0), axis=1, keepdims=True)


def load_rows(ref, count):
    return jnp.concatenate(
        [ref[0, :, pl.ds(k * LANES, LANES)] for k in range(count)], axis=0
    )


def fault_scalars(sizes, faults):
    start = jnp.int32(0)
    scalars = []
    for f in range(faults):
        scalars.append((start // LANES, start % LANES, sizes[0, 0, f]))
        start = start + sizes[0, 0, f]
    return scalars


def quarters(remote, blocks, sems, f, which):
    half = blocks.shape[1] // 2
    near, far = pl.ds(0, half), pl.ds(half, half)
    return [
        pltpu.make_async_copy(
            remote.at[(0, 0, f) + part], blocks.at[(f,) + part], sems.at[place, f]
        )
        for place, part in list(enumerate([(near, near), (near, far), (far,)]))[which]
    ]


def fetch(scalars, remote, blocks, sems):
    half = blocks.shape[1] // 2
    for f in range(len(scalars)):
        quarters(remote, blocks, sems, f, slice(0, 1))[0].start()
    for f, (_, _, size) in enumerate(scalars):

        @pl.when(size > half)
        def _():
            for copy in quarters(remote, blocks, sems, f, slice(1, 3)):
                copy.start()


def precondition(sizes, remote, field, work, begin=None):
    windows, shifts, lens, stack, lefts, found, large = work[:7]
    local = len(work) == 7
    blocks, sems = (remote, None) if local else work[7:]
    faults = blocks.shape[0]
    chunks = blocks.shape[1] // LANES
    rows = field.shape[0]
    scalars = fault_scalars(sizes, faults)
    if not local:
        fetch(scalars, remote, blocks, sems)
    if begin is not None:
        begin()
    lane = lax.broadcasted_iota(jnp.int32, (faults, LANES), 1)
    for f, (tile, shift, size) in enumerate(scalars):
        shifts[f : f + 1, :] = jnp.full((1, LANES), shift, jnp.int32)
        lens[f : f + 1, :] = jnp.full((1, LANES), size, jnp.int32)
        for k in range(chunks + 1):
            windows[k, f : f + 1, :] = field[pl.ds(tile + k, 1), :]
    shift = shifts[...]
    size = lens[...]
    bits = [((shift >> b) & 1) == 1 for b in range(7)]
    live = [lane + k * LANES < size for k in range(chunks)]
    parts = [windows[k] for k in range(chunks + 1)]
    for b in range(7):
        step = 1 << b
        rolled = [pltpu.roll(part, LANES - step, 1) for part in parts]
        moved = [
            jnp.where(lane < LANES - step, rolled[k], rolled[min(k + 1, chunks)])
            for k in range(chunks + 1)
        ]
        parts = [jnp.where(bits[b], new, old) for new, old in zip(moved, parts)]
    parts = [jnp.where(live[k], parts[k], 0.0) for k in range(chunks)]
    sub = lax.broadcasted_iota(jnp.int32, (8, LANES), 0)
    half = blocks.shape[1] // 2
    chunk_half = chunks // 2
    for group in range(faults // 8):
        pieces = []
        for k in range(chunks):
            high, low = split(parts[k][group * 8 : group * 8 + 8])
            pieces.append(jnp.concatenate([high, low], axis=0))
        left = jnp.concatenate(pieces, axis=1)
        lefts[group] = left
        sums = [jnp.zeros((8, LANES), F32) for _ in range(chunk_half)]
        for place in range(8):
            f = group * 8 + place
            if not local:
                quarters(remote, blocks, sems, f, slice(0, 1))[0].wait()
            result = dot_nt(left[:, :half], blocks[f, :half, :half])
            result = result[:8] + result[8:]
            for k in range(chunk_half):
                sums[k] = jnp.where(sub == place, result[:, k * LANES : (k + 1) * LANES], sums[k])
        for k in range(chunks):
            found[k, group] = sums[k] if k < chunk_half else jnp.zeros((8, LANES), F32)
    count = jnp.int32(0)
    for f, (_, _, size) in enumerate(scalars):
        large[count] = f
        count = count + (size > half).astype(jnp.int32)

    def rest(step, carry):
        for u in range(UNROLL):
            place = step * UNROLL + u
            f = large[jnp.minimum(place, count - 1)]
            group = f // 8
            left = lefts[group]
            if not local:

                @pl.when(place < count)
                def _():
                    for copy in quarters(remote, blocks, sems, f, slice(1, 3)):
                        copy.wait()

            above = dot_nt(left[:, half:], blocks[f, :half, half:])
            below = dot_nt(left, blocks[f, half:, :])
            above = above[:8] + above[8:]
            below = below[:8] + below[8:]
            mine = jnp.logical_and(sub == f % 8, place < count)
            for k in range(chunk_half):
                piece = slice(k * LANES, (k + 1) * LANES)
                found[k, group] += jnp.where(mine, above[:, piece], 0.0)
                found[chunk_half + k, group] += jnp.where(mine, below[:, piece], 0.0)
        return carry

    lax.fori_loop(0, (count + UNROLL - 1) // UNROLL, rest, 0)
    parts = [
        jnp.where(live[k], found[k].reshape(faults, LANES), 0.0) for k in range(chunks)
    ]
    parts.append(jnp.zeros((faults, LANES), F32))
    for b in range(7):
        step = 1 << b
        rolled = [pltpu.roll(part, step, 1) for part in parts]
        moved = [
            jnp.where(lane >= step, rolled[k], rolled[k - 1] if k else 0.0)
            for k in range(chunks + 1)
        ]
        parts = [jnp.where(bits[b], new, old) for new, old in zip(moved, parts)]
    count = faults * (chunks + 1)
    for k in range(chunks + 1):
        stack[k * faults : (k + 1) * faults, :] = parts[k]
    depth = stack.shape[0]
    if depth > count:
        stack[count:depth, :] = jnp.zeros((depth - count, LANES), F32)
    place = lax.broadcasted_iota(jnp.int32, (1, depth), 1)
    chunk = jnp.zeros((1, depth), jnp.int32)
    for k in range(1, chunks + 1):
        chunk = chunk + (place >= k * faults).astype(jnp.int32)
    local = place - chunk * faults
    target = jnp.full((1, depth), -1, jnp.int32)
    for f, (tile, _, _) in enumerate(scalars):
        target = jnp.where(local == f, tile + chunk, target)
    target = jnp.where(place < count, target, -1)
    chosen = (lax.broadcasted_iota(jnp.int32, (rows, depth), 0) == target).astype(BF16)
    high, low = split(stack[...])
    return jnp.dot(chosen, high, preferred_element_type=F32) + jnp.dot(
        chosen, low, preferred_element_type=F32
    )


def set_field(field, value):
    tiles = value.shape[0]
    field[0:tiles, :] = value
    field[tiles:, :] = jnp.zeros((field.shape[0] - tiles, LANES), F32)


def owner(index, each, count):
    found = jnp.zeros(index.shape, jnp.int32)
    for c in range(1, count):
        found = found + (index >= c * each).astype(jnp.int32)
    return found


def first_kernel(shape, *refs):
    (blocks, send, near_blocks, spots, target) = refs[5:10]
    (sizes, rhs, friction, tile_row, tile_col) = refs[10:15]
    (sems, block_sems, field, *work) = refs[15:]
    work = work + [near_blocks, block_sems]
    row_count, col_count = shape
    tiles = rhs.shape[2] // LANES
    height = send.shape[0]
    pairs = list(zip(refs[:5], refs[10:15]))
    copies = [pltpu.make_async_copy(a, b, sems.at[i]) for i, (a, b) in enumerate(pairs)]
    for copy in copies:
        copy.start()
    copies[0].wait()

    def value_to_field():
        copies[1].wait()
        set_field(field, load_rows(rhs, tiles))
        for copy in copies[3:]:
            copy.wait()
        column = tile_col[0]
        source = owner(column, tiles, row_count)
        spots[...] = (source ^ lax.axis_index("row")) * height + column - source * tiles
        row = tile_row[0]
        source = owner(row, tiles, col_count)
        place = source ^ lax.axis_index("col")
        place = (place & 1) * (col_count // 2) + (place >> 1)
        target[...] = place * height + row - source * tiles

    direction = precondition(sizes, blocks, field, work, value_to_field)[0:tiles]
    copies[2].wait()
    value = field[0:tiles, :]
    scaled = load_rows(friction, tiles) * direction
    send[...] = jnp.zeros_like(send)
    send[0:tiles, :] = direction
    send[tiles : tiles + 1, :] = lane_row([total(value * value), total(value * scaled)])


def gathered(parts, tiles):
    whole = parts[0][...]
    for part in parts[1:]:
        whole = whole + part[...]
    return whole[0:tiles], whole[tiles : tiles + 1]


def second_kernel(sizes, rhs, friction, blocks, sent, *refs):
    parts, (send, image_out, basis_out, field, *work) = refs[:-11], refs[-11:]
    tiles = rhs.shape[2] // LANES
    start = load_rows(rhs, tiles)
    diagonal = load_rows(friction, tiles)
    product, sums = gathered(parts, tiles)
    norm2 = pick(sums, 0)
    image = diagonal * sent[0:tiles, :] + product
    scale = lax.rsqrt(norm2)
    value = (image - pick(sums, 1) / norm2 * start) * scale
    image_out[...] = image
    basis_out[0:tiles, :] = value
    basis_out[tiles:, :] = jnp.broadcast_to(norm2, (basis_out.shape[0] - tiles, LANES))
    set_field(field, value)
    direction = precondition(sizes, blocks, field, work)[0:tiles]
    scaled = diagonal * direction
    send[...] = jnp.zeros_like(send)
    send[0:tiles, :] = direction
    send[tiles : tiles + 1, :] = lane_row(
        [
            total(value * value),
            total(start * value) * scale,
            total(start * scaled) * scale,
            total(value * scaled),
        ]
    )


def third_kernel(sizes, rhs, friction, blocks, sent, basis, *refs):
    parts, (send, image_out, field, *work) = refs[:-10], refs[-10:]
    tiles = rhs.shape[2] // LANES
    start = load_rows(rhs, tiles)
    diagonal = load_rows(friction, tiles)
    product, sums = gathered(parts, tiles)
    image = diagonal * sent[0:tiles, :] + product
    value = basis[0:tiles, :]
    scale = lax.rsqrt(basis[tiles : tiles + 1, 0:1])
    norm2, cross, along_start, along = [pick(sums, k) for k in range(4)]
    left = norm2 - cross * cross
    usable = left > 1e-5 * norm2
    along = jnp.where(usable, (along - cross * along_start) / jnp.where(usable, left, 1.0), 0.0)
    along_start = along_start - cross * along
    value = (image - along * value - (along_start * scale) * start) * lax.rsqrt(
        jnp.maximum(norm2, 1e-30)
    )
    image_out[...] = image
    set_field(field, value)
    direction = precondition(sizes, blocks, field, work)[0:tiles]
    send[...] = jnp.zeros_like(send)
    send[0:tiles, :] = direction


def fourth_kernel(rhs, friction, sent, image0, image1, *refs):
    parts, (image_out, sums_out) = refs[:-2], refs[-2:]
    tiles = rhs.shape[2] // LANES
    start = load_rows(rhs, tiles)
    product, _ = gathered(parts, tiles)
    image = load_rows(friction, tiles) * sent[0:tiles, :] + product
    image_out[...] = image
    images = [image0[...], image1[...], image]
    values = [total(images[i] * images[j]) for i in range(3) for j in range(i + 1)]
    values += [total(start * one) for one in images]
    sums_out[...] = jnp.broadcast_to(lane_row(values), sums_out.shape)


def last_kernel(sums, rhs, image0, image1, image2, sent0, sent1, sent2, update, residual):
    tiles = rhs.shape[2] // LANES
    row = jnp.sum(sums[...], axis=0, keepdims=True)
    entries = [pick(row, k) for k in range(9)]
    scale = [lax.rsqrt(jnp.maximum(entries[k], 1e-30)) for k in (0, 2, 5)]
    gram = {}
    place = 0
    for i in range(3):
        for j in range(i + 1):
            gram[i, j] = entries[place] * scale[i] * scale[j]
            place += 1
    goal = [entries[6 + i] * scale[i] for i in range(3)]
    low10 = gram[1, 0]
    low20 = gram[2, 0]
    pivot1 = 1.0 - low10 * low10
    keep1 = pivot1 > 1e-6
    inverse1 = jnp.where(keep1, 1.0 / jnp.where(keep1, pivot1, 1.0), 0.0)
    cross = gram[2, 1] - low20 * low10
    low21 = cross * inverse1
    pivot2 = 1.0 - low20 * low20 - cross * low21
    keep2 = pivot2 > 1e-6
    inverse2 = jnp.where(keep2, 1.0 / jnp.where(keep2, pivot2, 1.0), 0.0)
    part1 = goal[1] - low10 * goal[0]
    part2 = goal[2] - low20 * goal[0] - low21 * part1
    weight2 = part2 * inverse2
    weight1 = part1 * inverse1 - low21 * weight2
    weight0 = goal[0] - low10 * weight1 - low20 * weight2
    weights = [weight0 * scale[0], weight1 * scale[1], weight2 * scale[2]]
    start = load_rows(rhs, tiles)
    best = (
        weights[0] * sent0[0:tiles, :]
        + weights[1] * sent1[0:tiles, :]
        + weights[2] * sent2[0:tiles, :]
    )
    rest = start - weights[0] * image0[...] - weights[1] * image1[...] - weights[2] * image2[...]
    for k in range(tiles):
        update[0, :, pl.ds(k * LANES, LANES)] = best[k : k + 1]
        residual[0, :, pl.ds(k * LANES, LANES)] = rest[k : k + 1]


def tiles_kernel(tail, counts, spots, rows, scale, blocks, *refs):
    sent, (keep, give, field, found, products) = refs[:-5], refs[-5:]
    slots = blocks.shape[0]
    far, height = keep.shape[0], keep.shape[1]
    groups = slots // 16
    for k, one in enumerate(sent):
        field[k * height : (k + 1) * height, :] = one[...]
    for t in range(slots):
        found[t : t + 1, :] = field[pl.ds(spots[0, t], 1), :]
    sub = lax.broadcasted_iota(jnp.int32, (8, LANES), 0)
    blank = jnp.zeros((8, LANES), F32)
    for group in range(groups):
        base = group * 16
        top = jnp.concatenate([found[base : base + 8, :], blank], axis=1)
        bottom = jnp.concatenate([blank, found[base + 8 : base + 16, :]], axis=1)
        left = jnp.concatenate([top, bottom], axis=0).astype(BF16)
        first, second = blank, blank
        for p in range(4):
            a, b = base + 2 * p, base + 2 * p + 1
            right = jnp.concatenate(
                [
                    jnp.concatenate([blocks[a], blocks[a + 8]], axis=1),
                    jnp.concatenate([blocks[b], blocks[b + 8]], axis=1),
                ],
                axis=0,
            )
            result = dot_nt(left, right)
            for spot, half in ((2 * p, slice(0, LANES)), (2 * p + 1, slice(LANES, 2 * LANES))):
                first = jnp.where(sub == spot, result[:8, half], first)
                second = jnp.where(sub == spot, result[8:, half], second)
        products[base : base + 8, :] = first
        products[base + 8 : base + 16, :] = second
    high, low = split(products[...])
    target = rows[...]
    slot = lax.broadcasted_iota(jnp.int32, target.shape, 1)
    weight = jnp.where(slot < counts[0, 0], scale[0], 0.0)
    chosen = jnp.where(
        lax.broadcasted_iota(jnp.int32, (2 * far * height, slots), 0) == target, weight, 0.0
    )
    chosen_high, chosen_low = split(chosen)
    value = (
        jnp.dot(chosen_high, high, preferred_element_type=F32)
        + jnp.dot(chosen_low, high, preferred_element_type=F32)
        + jnp.dot(chosen_high, low, preferred_element_type=F32)
    )
    keep[...] = value[: far * height].reshape(far, height, LANES)
    give[...] = value[far * height :].reshape(far, height, LANES)
    last = height - 8
    sums = sent[0][last:height, :]
    for one in sent[1:]:
        sums = sums + one[last:height, :]
    sums = jnp.where(lax.broadcasted_iota(jnp.int32, (8, LANES), 0) == tail, sums, 0.0)
    for k in range(far):
        keep[k, last:height, :] += sums
        give[k, last:height, :] += sums


def scratch(shape, dtype=F32):
    return pltpu.VMEM(shape, dtype)


def local(
    rhs,
    friction,
    kernel_tiles,
    tile_scale,
    tile_row,
    tile_col,
    tile_counts,
    precond_blocks,
    fault_sizes,
):
    length = rhs.shape[2]
    slots = kernel_tiles.shape[2]
    faults, width = precond_blocks.shape[2], precond_blocks.shape[3]
    tiles = length // LANES
    height = (tiles + 8) // 8 * 8
    chunks = width // LANES
    row_count = lax.axis_size("row")
    col_count = lax.axis_size("col")
    far = col_count // 2
    rows = (tiles + chunks + 8) // 8 * 8
    depth = (faults * (chunks + 1) + LANES - 1) // LANES * LANES

    grid = jax.ShapeDtypeStruct((height, LANES), F32)
    plain = jax.ShapeDtypeStruct((tiles, LANES), F32)
    half_grid = jax.ShapeDtypeStruct((far, height, LANES), F32)
    work = [
        scratch((rows, LANES)),
        scratch((chunks + 1, faults, LANES)),
        scratch((faults, LANES), jnp.int32),
        scratch((faults, LANES), jnp.int32),
        scratch((depth, LANES)),
        scratch((faults // 8, 16, width), BF16),
        scratch((chunks, faults // 8, 8, LANES)),
        pltpu.SMEM((faults + 1,), jnp.int32),
    ]

    def exchange(value, axis, distance):
        size = lax.axis_size(axis)
        return lax.ppermute(value, axis, [(i, i ^ distance) for i in range(size)])

    near_tiles = kernel_tiles.reshape(slots, LANES, LANES)
    inputs = (fault_sizes, rhs, friction, tile_row, tile_col, precond_blocks)
    places = jax.ShapeDtypeStruct((1, slots), jnp.int32)
    sent0, near_blocks, spots, target = pl.pallas_call(
        functools.partial(first_kernel, (row_count, col_count)),
        out_shape=[
            grid,
            pltpu.VMEM((faults, width, width), BF16),
            places,
            places,
        ],
        in_specs=[HBM] * 6,
        out_specs=[VMEM] * 4,
        scratch_shapes=[
            pltpu.SMEM(fault_sizes.shape, jnp.int32),
            scratch(rhs.shape),
            scratch(friction.shape),
            scratch(tile_row.shape, jnp.int32),
            scratch(tile_col.shape, jnp.int32),
            pltpu.SemaphoreType.DMA((5,)),
            pltpu.SemaphoreType.DMA((3, faults)),
        ]
        + work,
        compiler_params=PARAMS,
        name="first",
    )(*[pltpu.with_memory_space_constraint(a, pltpu.HBM) for a in inputs])

    def apply_kernel(sent):
        got = [sent] + [exchange(sent, "row", d) for d in range(1, row_count)]
        keep, give = pl.pallas_call(
            functools.partial(tiles_kernel, tiles % 8),
            out_shape=[half_grid, half_grid],
            in_specs=[SMEM, SMEM, VMEM, VMEM, VMEM] + [VMEM] * row_count,
            out_specs=[VMEM] * 2,
            scratch_shapes=[
                scratch((row_count * height, LANES)),
                scratch((slots, LANES)),
                scratch((slots, LANES)),
            ],
            compiler_params=PARAMS,
            name="tiles",
        )(tile_counts, spots, target, tile_scale, near_tiles, *got)
        both = keep + exchange(give, "col", 1)
        return [both[0]] + [exchange(both[d], "col", 2 * d) for d in range(1, far)]

    parts0 = apply_kernel(sent0)
    sent1, image0, basis = pl.pallas_call(
        second_kernel,
        out_shape=[grid, plain, grid],
        in_specs=[SMEM, VMEM, VMEM, VMEM] + [VMEM] * (1 + far),
        out_specs=[VMEM] * 3,
        scratch_shapes=work,
        compiler_params=PARAMS,
        name="second",
    )(fault_sizes, rhs, friction, near_blocks, sent0, *parts0)
    parts1 = apply_kernel(sent1)
    sent2, image1 = pl.pallas_call(
        third_kernel,
        out_shape=[grid, plain],
        in_specs=[SMEM, VMEM, VMEM, VMEM] + [VMEM] * (2 + far),
        out_specs=[VMEM] * 2,
        scratch_shapes=work,
        compiler_params=PARAMS,
        name="third",
    )(fault_sizes, rhs, friction, near_blocks, sent1, basis, *parts1)
    parts2 = apply_kernel(sent2)
    devices = row_count * col_count
    image2, sums = pl.pallas_call(
        fourth_kernel,
        out_shape=[plain, jax.ShapeDtypeStruct((devices, LANES), F32)],
        in_specs=[VMEM] * (5 + far),
        out_specs=[VMEM] * 2,
        compiler_params=PARAMS,
        name="fourth",
    )(rhs, friction, sent2, image0, image1, *parts2)
    sums = lax.all_to_all(sums, ("row", "col"), 0, 0, tiled=True)
    whole = jax.ShapeDtypeStruct((1, 1, length), F32)
    return pl.pallas_call(
        last_kernel,
        out_shape=[whole, whole],
        in_specs=[VMEM] * 8,
        out_specs=[VMEM] * 2,
        compiler_params=PARAMS,
        name="last",
    )(sums, rhs, image0, image1, image2, sent0, sent1, sent2)


def solution(mesh):
    return jax.shard_map(
        local,
        mesh=mesh,
        in_specs=(
            P("row", "col", None),
            P("row", "col", None),
            P("row", "col", None, None, None),
            P("row", "col", None),
            P("row", "col", None),
            P("row", "col", None),
            P("row", "col"),
            P("row", "col", None, None, None),
            P("row", "col", None),
        ),
        out_specs=(P("row", "col", None), P("row", "col", None)),
        check_vma=False,
    )
```

```python
import functools

import jax
import jax.numpy as jnp
from jax import lax
from jax.experimental import pallas as pl
from jax.experimental.pallas import tpu as pltpu
from jax.sharding import PartitionSpec as P

LANES = 128
UNROLL = 3
F32 = jnp.float32
BF16 = jnp.bfloat16
VMEM = pl.BlockSpec(memory_space=pltpu.VMEM)
SMEM = pl.BlockSpec(memory_space=pltpu.SMEM)
HBM = pl.BlockSpec(memory_space=pltpu.HBM)
PARAMS = pltpu.CompilerParams(vmem_limit_bytes=6 << 20)


def dot_nt(left, right):
    return lax.dot_general(left, right, (((1,), (1,)), ((), ())), preferred_element_type=F32)


def split(value):
    high = value.astype(BF16)
    low = (value - high.astype(F32)).astype(BF16)
    return high, low


def total(value):
    return jnp.sum(jnp.sum(value, axis=0, keepdims=True), axis=1, keepdims=True)


def lane_row(values):
    lane = lax.broadcasted_iota(jnp.int32, (1, LANES), 1)
    row = jnp.zeros((1, LANES), F32)
    for place, value in enumerate(values):
        row = jnp.where(lane == place, value, row)
    return row


def pick(row, place):
    lane = lax.broadcasted_iota(jnp.int32, (1, LANES), 1)
    return jnp.sum(jnp.where(lane == place, row, 0.0), axis=1, keepdims=True)


def load_rows(ref, count):
    return jnp.concatenate(
        [ref[0, :, pl.ds(k * LANES, LANES)] for k in range(count)], axis=0
    )


def fault_scalars(sizes, faults):
    start = jnp.int32(0)
    scalars = []
    for f in range(faults):
        scalars.append((start // LANES, start % LANES, sizes[0, 0, f]))
        start = start + sizes[0, 0, f]
    return scalars


def quarters(remote, blocks, sems, f, which):
    half = blocks.shape[1] // 2
    near, far = pl.ds(0, half), pl.ds(half, half)
    return [
        pltpu.make_async_copy(
            remote.at[(0, 0, f) + part], blocks.at[(f,) + part], sems.at[place, f]
        )
        for place, part in list(enumerate([(near, near), (near, far), (far,)]))[which]
    ]


def fetch(scalars, remote, blocks, sems):
    half = blocks.shape[1] // 2
    for f in range(len(scalars)):
        quarters(remote, blocks, sems, f, slice(0, 1))[0].start()
    for f, (_, _, size) in enumerate(scalars):

        @pl.when(size > half)
        def _():
            for copy in quarters(remote, blocks, sems, f, slice(1, 3)):
                copy.start()


def make_plan(scalars, plan, column):
    chosen, chosen_t, shifts, lens = plan
    faults = len(scalars)
    depth, rows = chosen_t.shape
    chunks = depth // faults - 1
    column[...] = jnp.full(column.shape, -1, jnp.int32)
    place = lax.broadcasted_iota(jnp.int32, (1, depth), 1)
    target = jnp.full((1, depth), -1, jnp.int32)
    for f, (tile, shift, size) in enumerate(scalars):
        shifts[f : f + 1, :] = jnp.full((1, LANES), shift, jnp.int32)
        lens[f : f + 1, :] = jnp.full((1, LANES), size, jnp.int32)
        for k in range(chunks + 1):
            spot = k * faults + f
            column[spot : spot + 1, :] = jnp.full((1, LANES), tile + k, jnp.int32)
            target = jnp.where(place == spot, tile + k, target)
    chosen[...] = (lax.broadcasted_iota(jnp.int32, (rows, depth), 0) == target).astype(BF16)
    chosen_t[...] = (
        lax.broadcasted_iota(jnp.int32, (depth, rows), 1) == column[:, 0:1]
    ).astype(BF16)


def select(chosen, value):
    high, low = split(value)
    return jnp.dot(chosen, high, preferred_element_type=F32) + jnp.dot(
        chosen, low, preferred_element_type=F32
    )


def precondition(sizes, plan, field, blocks, work, remote=None, sems=None):
    chosen, chosen_t, shifts, lens = plan
    stack, lefts, found, large = work
    faults = blocks.shape[0]
    chunks = blocks.shape[1] // LANES
    local = remote is None
    lane = lax.broadcasted_iota(jnp.int32, (faults, LANES), 1)
    windows = select(chosen_t[...], field[...])
    shift = shifts[...]
    size = lens[...]
    bits = [((shift >> b) & 1) == 1 for b in range(7)]
    live = [lane + k * LANES < size for k in range(chunks)]
    parts = [windows[k * faults : (k + 1) * faults] for k in range(chunks + 1)]
    for b in range(7):
        step = 1 << b
        rolled = [pltpu.roll(part, LANES - step, 1) for part in parts]
        moved = [
            jnp.where(lane < LANES - step, rolled[k], rolled[min(k + 1, chunks)])
            for k in range(chunks + 1)
        ]
        parts = [jnp.where(bits[b], new, old) for new, old in zip(moved, parts)]
    parts = [jnp.where(live[k], parts[k], 0.0) for k in range(chunks)]
    sub = lax.broadcasted_iota(jnp.int32, (8, LANES), 0)
    half = blocks.shape[1] // 2
    chunk_half = chunks // 2
    for group in range(faults // 8):
        pieces = []
        for k in range(chunks):
            high, low = split(parts[k][group * 8 : group * 8 + 8])
            pieces.append(jnp.concatenate([high, low], axis=0))
        left = jnp.concatenate(pieces, axis=1)
        lefts[group] = left
        sums = [jnp.zeros((8, LANES), F32) for _ in range(chunk_half)]
        for place in range(8):
            f = group * 8 + place
            if not local:
                quarters(remote, blocks, sems, f, slice(0, 1))[0].wait()
            result = dot_nt(left[:, :half], blocks[f, :half, :half])
            result = result[:8] + result[8:]
            for k in range(chunk_half):
                sums[k] = jnp.where(sub == place, result[:, k * LANES : (k + 1) * LANES], sums[k])
        for k in range(chunks):
            found[k, group] = sums[k] if k < chunk_half else jnp.zeros((8, LANES), F32)
    count = jnp.int32(0)
    for f in range(faults):
        large[count] = f
        count = count + (sizes[0, 0, f] > half).astype(jnp.int32)

    def rest(step, carry):
        for u in range(UNROLL):
            place = step * UNROLL + u
            f = large[jnp.minimum(place, count - 1)]
            group = f // 8
            left = lefts[group]
            if not local:

                @pl.when(place < count)
                def _():
                    for copy in quarters(remote, blocks, sems, f, slice(1, 3)):
                        copy.wait()

            above = dot_nt(left[:, half:], blocks[f, :half, half:])
            below = dot_nt(left, blocks[f, half:, :])
            above = above[:8] + above[8:]
            below = below[:8] + below[8:]
            mine = jnp.logical_and(sub == f % 8, place < count)
            for k in range(chunk_half):
                piece = slice(k * LANES, (k + 1) * LANES)
                found[k, group] += jnp.where(mine, above[:, piece], 0.0)
                found[chunk_half + k, group] += jnp.where(mine, below[:, piece], 0.0)
        return carry

    lax.fori_loop(0, (count + UNROLL - 1) // UNROLL, rest, 0)
    parts = [
        jnp.where(live[k], found[k].reshape(faults, LANES), 0.0) for k in range(chunks)
    ]
    parts.append(jnp.zeros((faults, LANES), F32))
    for b in range(7):
        step = 1 << b
        rolled = [pltpu.roll(part, step, 1) for part in parts]
        moved = [
            jnp.where(lane >= step, rolled[k], rolled[k - 1] if k else 0.0)
            for k in range(chunks + 1)
        ]
        parts = [jnp.where(bits[b], new, old) for new, old in zip(moved, parts)]
    count = faults * (chunks + 1)
    for k in range(chunks + 1):
        stack[k * faults : (k + 1) * faults, :] = parts[k]
    depth = stack.shape[0]
    if depth > count:
        stack[count:depth, :] = jnp.zeros((depth - count, LANES), F32)
    return select(chosen[...], stack[...])


def set_field(field, value):
    tiles = value.shape[0]
    field[0:tiles, :] = value
    field[tiles:, :] = jnp.zeros((field.shape[0] - tiles, LANES), F32)


def owner(index, each, count):
    found = jnp.zeros(index.shape, jnp.int32)
    for c in range(1, count):
        found = found + (index >= c * each).astype(jnp.int32)
    return found


def first_kernel(far_sizes, far_rhs, far_friction, remote, send, blocks, *refs):
    plan, (sizes, rhs, friction, column, sems, block_sems, field, *work) = refs[:4], refs[4:]
    tiles = rhs.shape[2] // LANES
    pairs = [(far_sizes, sizes), (far_rhs, rhs), (far_friction, friction)]
    copies = [pltpu.make_async_copy(a, b, sems.at[i]) for i, (a, b) in enumerate(pairs)]
    for copy in copies:
        copy.start()
    copies[0].wait()
    scalars = fault_scalars(sizes, blocks.shape[0])
    fetch(scalars, remote, blocks, block_sems)
    make_plan(scalars, plan, column)
    copies[1].wait()
    set_field(field, load_rows(rhs, tiles))
    direction = precondition(sizes, plan, field, blocks, work, remote, block_sems)[0:tiles]
    copies[2].wait()
    value = field[0:tiles, :]
    scaled = load_rows(friction, tiles) * direction
    send[...] = jnp.zeros_like(send)
    send[0:tiles, :] = direction
    send[tiles : tiles + 1, :] = lane_row([total(value * value), total(value * scaled)])


def gathered(parts, tiles):
    whole = parts[0][...]
    for part in parts[1:]:
        whole = whole + part[...]
    return whole[0:tiles], whole[tiles : tiles + 1]


def second_kernel(sizes, rhs, friction, blocks, *refs):
    plan, sent, parts = refs[:4], refs[4], refs[5:-8]
    send, image_out, basis_out, field, *work = refs[-8:]
    tiles = rhs.shape[2] // LANES
    start = load_rows(rhs, tiles)
    diagonal = load_rows(friction, tiles)
    product, sums = gathered(parts, tiles)
    norm2 = pick(sums, 0)
    image = diagonal * sent[0:tiles, :] + product
    scale = lax.rsqrt(norm2)
    value = (image - pick(sums, 1) / norm2 * start) * scale
    image_out[...] = image
    basis_out[0:tiles, :] = value
    basis_out[tiles:, :] = jnp.broadcast_to(norm2, (basis_out.shape[0] - tiles, LANES))
    set_field(field, value)
    direction = precondition(sizes, plan, field, blocks, work)[0:tiles]
    scaled = diagonal * direction
    send[...] = jnp.zeros_like(send)
    send[0:tiles, :] = direction
    send[tiles : tiles + 1, :] = lane_row(
        [
            total(value * value),
            total(start * value) * scale,
            total(start * scaled) * scale,
            total(value * scaled),
        ]
    )


def third_kernel(sizes, rhs, friction, blocks, *refs):
    plan, sent, basis, parts = refs[:4], refs[4], refs[5], refs[6:-7]
    send, image_out, field, *work = refs[-7:]
    tiles = rhs.shape[2] // LANES
    start = load_rows(rhs, tiles)
    diagonal = load_rows(friction, tiles)
    product, sums = gathered(parts, tiles)
    image = diagonal * sent[0:tiles, :] + product
    value = basis[0:tiles, :]
    scale = lax.rsqrt(basis[tiles : tiles + 1, 0:1])
    norm2, cross, along_start, along = [pick(sums, k) for k in range(4)]
    left = norm2 - cross * cross
    usable = left > 1e-5 * norm2
    along = jnp.where(usable, (along - cross * along_start) / jnp.where(usable, left, 1.0), 0.0)
    along_start = along_start - cross * along
    value = (image - along * value - (along_start * scale) * start) * lax.rsqrt(
        jnp.maximum(norm2, 1e-30)
    )
    image_out[...] = image
    set_field(field, value)
    direction = precondition(sizes, plan, field, blocks, work)[0:tiles]
    send[...] = jnp.zeros_like(send)
    send[0:tiles, :] = direction


def fourth_kernel(rhs, friction, sent, image0, image1, *refs):
    parts, (image_out, sums_out) = refs[:-2], refs[-2:]
    tiles = rhs.shape[2] // LANES
    start = load_rows(rhs, tiles)
    product, _ = gathered(parts, tiles)
    image = load_rows(friction, tiles) * sent[0:tiles, :] + product
    image_out[...] = image
    images = [image0[...], image1[...], image]
    values = [total(images[i] * images[j]) for i in range(3) for j in range(i + 1)]
    values += [total(start * one) for one in images]
    sums_out[...] = jnp.broadcast_to(lane_row(values), sums_out.shape)


def last_kernel(sums, rhs, image0, image1, image2, sent0, sent1, sent2, update, residual):
    tiles = rhs.shape[2] // LANES
    row = jnp.sum(sums[...], axis=0, keepdims=True)
    entries = [pick(row, k) for k in range(9)]
    scale = [lax.rsqrt(jnp.maximum(entries[k], 1e-30)) for k in (0, 2, 5)]
    gram = {}
    place = 0
    for i in range(3):
        for j in range(i + 1):
            gram[i, j] = entries[place] * scale[i] * scale[j]
            place += 1
    goal = [entries[6 + i] * scale[i] for i in range(3)]
    low10 = gram[1, 0]
    low20 = gram[2, 0]
    pivot1 = 1.0 - low10 * low10
    keep1 = pivot1 > 1e-6
    inverse1 = jnp.where(keep1, 1.0 / jnp.where(keep1, pivot1, 1.0), 0.0)
    cross = gram[2, 1] - low20 * low10
    low21 = cross * inverse1
    pivot2 = 1.0 - low20 * low20 - cross * low21
    keep2 = pivot2 > 1e-6
    inverse2 = jnp.where(keep2, 1.0 / jnp.where(keep2, pivot2, 1.0), 0.0)
    part1 = goal[1] - low10 * goal[0]
    part2 = goal[2] - low20 * goal[0] - low21 * part1
    weight2 = part2 * inverse2
    weight1 = part1 * inverse1 - low21 * weight2
    weight0 = goal[0] - low10 * weight1 - low20 * weight2
    weights = [weight0 * scale[0], weight1 * scale[1], weight2 * scale[2]]
    start = load_rows(rhs, tiles)
    best = (
        weights[0] * sent0[0:tiles, :]
        + weights[1] * sent1[0:tiles, :]
        + weights[2] * sent2[0:tiles, :]
    )
    rest = start - weights[0] * image0[...] - weights[1] * image1[...] - weights[2] * image2[...]
    for k in range(tiles):
        update[0, :, pl.ds(k * LANES, LANES)] = best[k : k + 1]
        residual[0, :, pl.ds(k * LANES, LANES)] = rest[k : k + 1]


def prepare_kernel(shape, after, counts, tile_row, tile_col, scale, remote, blocks, *refs):
    gather, high, low, sems = refs
    tiles, height, row_count, col_count = shape
    slots = blocks.shape[0]
    pieces = sems.shape[0]
    copies = []
    for p in range(pieces):
        part = pl.ds(p * (slots // pieces), slots // pieces)
        copies.append(
            pltpu.make_async_copy(remote.at[0, 0, part], blocks.at[part], sems.at[p])
        )
        copies[-1].start()
    column = tile_col[0]
    source = owner(column, tiles, row_count)
    spots = (source ^ lax.axis_index("row")) * height + column - source * tiles
    ones = jnp.ones((LANES, LANES), BF16)
    for base in range(0, slots, LANES):
        mine = spots[:, base : base + LANES].astype(F32)
        square = lax.broadcasted_iota(jnp.int32, (LANES, LANES), 0)
        across = lax.broadcasted_iota(jnp.int32, (LANES, LANES), 1)
        square = jnp.where(square == across, mine, 0.0).astype(BF16)
        down = jnp.dot(square, ones, preferred_element_type=F32)[:, 0:1].astype(jnp.int32)
        wide = lax.broadcasted_iota(jnp.int32, (LANES, gather.shape[1]), 1)
        gather[base : base + LANES, :] = (wide == down).astype(BF16)
    row = tile_row[0]
    source = owner(row, tiles, col_count)
    place = source ^ lax.axis_index("col")
    place = (place & 1) * (col_count // 2) + (place >> 1)
    target = place * height + row - source * tiles
    slot = lax.broadcasted_iota(jnp.int32, target.shape, 1)
    weight = jnp.where(slot < counts[0, 0], scale[0], 0.0)
    chosen = jnp.where(lax.broadcasted_iota(jnp.int32, high.shape, 0) == target, weight, 0.0)
    high[...], low[...] = split(chosen)
    for copy in copies:
        copy.wait()


def tiles_kernel(tail, gather, chosen_high, chosen_low, blocks, *refs):
    sent, (keep, give, found, products) = refs[:-4], refs[-4:]
    slots = blocks.shape[0]
    far, height = keep.shape[0], keep.shape[1]
    groups = slots // 16
    field = jnp.concatenate([one[...] for one in sent], axis=0).astype(BF16)
    found[...] = jnp.dot(gather[...], field, preferred_element_type=F32)
    sub = lax.broadcasted_iota(jnp.int32, (8, LANES), 0)
    blank = jnp.zeros((8, LANES), F32)
    for group in range(groups):
        base = group * 16
        top = jnp.concatenate([found[base : base + 8, :], blank], axis=1)
        bottom = jnp.concatenate([blank, found[base + 8 : base + 16, :]], axis=1)
        left = jnp.concatenate([top, bottom], axis=0).astype(BF16)
        first, second = blank, blank
        for p in range(4):
            a, b = base + 2 * p, base + 2 * p + 1
            right = jnp.concatenate(
                [
                    jnp.concatenate([blocks[a], blocks[a + 8]], axis=1),
                    jnp.concatenate([blocks[b], blocks[b + 8]], axis=1),
                ],
                axis=0,
            )
            result = dot_nt(left, right)
            for spot, half in ((2 * p, slice(0, LANES)), (2 * p + 1, slice(LANES, 2 * LANES))):
                first = jnp.where(sub == spot, result[:8, half], first)
                second = jnp.where(sub == spot, result[8:, half], second)
        products[base : base + 8, :] = first
        products[base + 8 : base + 16, :] = second
    high, low = split(products[...])
    value = (
        jnp.dot(chosen_high[...], high, preferred_element_type=F32)
        + jnp.dot(chosen_low[...], high, preferred_element_type=F32)
        + jnp.dot(chosen_high[...], low, preferred_element_type=F32)
    )
    keep[...] = value[: far * height].reshape(far, height, LANES)
    give[...] = value[far * height :].reshape(far, height, LANES)
    last = height - 8
    sums = sent[0][last:height, :]
    for one in sent[1:]:
        sums = sums + one[last:height, :]
    sums = jnp.where(lax.broadcasted_iota(jnp.int32, (8, LANES), 0) == tail, sums, 0.0)
    for k in range(far):
        keep[k, last:height, :] += sums
        give[k, last:height, :] += sums


def scratch(shape, dtype=F32):
    return pltpu.VMEM(shape, dtype)


def local(
    rhs,
    friction,
    kernel_tiles,
    tile_scale,
    tile_row,
    tile_col,
    tile_counts,
    precond_blocks,
    fault_sizes,
):
    length = rhs.shape[2]
    slots = kernel_tiles.shape[2]
    faults, width = precond_blocks.shape[2], precond_blocks.shape[3]
    tiles = length // LANES
    height = (tiles + 8) // 8 * 8
    chunks = width // LANES
    row_count = lax.axis_size("row")
    col_count = lax.axis_size("col")
    far = col_count // 2
    rows = (tiles + chunks + 8) // 8 * 8
    depth = (faults * (chunks + 1) + LANES - 1) // LANES * LANES

    grid = jax.ShapeDtypeStruct((height, LANES), F32)
    plain = jax.ShapeDtypeStruct((tiles, LANES), F32)
    half_grid = jax.ShapeDtypeStruct((far, height, LANES), F32)
    work = [
        scratch((rows, LANES)),
        scratch((depth, LANES)),
        scratch((faults // 8, 16, width), BF16),
        scratch((chunks, faults // 8, 8, LANES)),
        pltpu.SMEM((faults + 1,), jnp.int32),
    ]

    def exchange(value, axis, distance):
        size = lax.axis_size(axis)
        return lax.ppermute(value, axis, [(i, i ^ distance) for i in range(size)])

    def pinned(value):
        return pltpu.with_memory_space_constraint(value, pltpu.HBM)

    sent0, near_blocks, *plan = pl.pallas_call(
        first_kernel,
        out_shape=[
            grid,
            pltpu.VMEM((faults, width, width), BF16),
            jax.ShapeDtypeStruct((rows, depth), BF16),
            jax.ShapeDtypeStruct((depth, rows), BF16),
            jax.ShapeDtypeStruct((faults, LANES), jnp.int32),
            jax.ShapeDtypeStruct((faults, LANES), jnp.int32),
        ],
        in_specs=[HBM] * 4,
        out_specs=[VMEM] * 6,
        scratch_shapes=[
            pltpu.SMEM(fault_sizes.shape, jnp.int32),
            scratch(rhs.shape),
            scratch(friction.shape),
            scratch((depth, LANES), jnp.int32),
            pltpu.SemaphoreType.DMA((3,)),
            pltpu.SemaphoreType.DMA((3, faults)),
        ]
        + work,
        compiler_params=PARAMS,
        name="first",
    )(pinned(fault_sizes), pinned(rhs), pinned(friction), pinned(precond_blocks))
    spread = (2 * far * height, slots)
    near_tiles, *selections = pl.pallas_call(
        functools.partial(prepare_kernel, (tiles, height, row_count, col_count)),
        out_shape=[
            pltpu.VMEM((slots, LANES, LANES), BF16),
            jax.ShapeDtypeStruct((slots, row_count * height), BF16),
            jax.ShapeDtypeStruct(spread, BF16),
            jax.ShapeDtypeStruct(spread, BF16),
        ],
        in_specs=[VMEM, SMEM, VMEM, VMEM, VMEM, HBM],
        out_specs=[VMEM] * 4,
        scratch_shapes=[pltpu.SemaphoreType.DMA((4,))],
        compiler_params=PARAMS,
        name="prepare",
    )(plan[3], tile_counts, tile_row, tile_col, tile_scale, pinned(kernel_tiles))

    def apply_kernel(sent):
        got = [sent] + [exchange(sent, "row", d) for d in range(1, row_count)]
        keep, give = pl.pallas_call(
            functools.partial(tiles_kernel, tiles % 8),
            out_shape=[half_grid, half_grid],
            in_specs=[VMEM] * (4 + row_count),
            out_specs=[VMEM] * 2,
            scratch_shapes=[
                scratch((slots, LANES)),
                scratch((slots, LANES)),
            ],
            compiler_params=PARAMS,
            name="tiles",
        )(*selections, near_tiles, *got)
        both = keep + exchange(give, "col", 1)
        return [both[0]] + [exchange(both[d], "col", 2 * d) for d in range(1, far)]

    parts0 = apply_kernel(sent0)
    sent1, image0, basis = pl.pallas_call(
        second_kernel,
        out_shape=[grid, plain, grid],
        in_specs=[SMEM, VMEM, VMEM, VMEM] + [VMEM] * (5 + far),
        out_specs=[VMEM] * 3,
        scratch_shapes=work,
        compiler_params=PARAMS,
        name="second",
    )(fault_sizes, rhs, friction, near_blocks, *plan, sent0, *parts0)
    parts1 = apply_kernel(sent1)
    sent2, image1 = pl.pallas_call(
        third_kernel,
        out_shape=[grid, plain],
        in_specs=[SMEM, VMEM, VMEM, VMEM] + [VMEM] * (6 + far),
        out_specs=[VMEM] * 2,
        scratch_shapes=work,
        compiler_params=PARAMS,
        name="third",
    )(fault_sizes, rhs, friction, near_blocks, *plan, sent1, basis, *parts1)
    parts2 = apply_kernel(sent2)
    devices = row_count * col_count
    image2, sums = pl.pallas_call(
        fourth_kernel,
        out_shape=[plain, jax.ShapeDtypeStruct((devices, LANES), F32)],
        in_specs=[VMEM] * (5 + far),
        out_specs=[VMEM] * 2,
        compiler_params=PARAMS,
        name="fourth",
    )(rhs, friction, sent2, image0, image1, *parts2)
    sums = lax.all_to_all(sums, ("row", "col"), 0, 0, tiled=True)
    whole = jax.ShapeDtypeStruct((1, 1, length), F32)
    return pl.pallas_call(
        last_kernel,
        out_shape=[whole, whole],
        in_specs=[VMEM] * 8,
        out_specs=[VMEM] * 2,
        compiler_params=PARAMS,
        name="last",
    )(sums, rhs, image0, image1, image2, sent0, sent1, sent2)


def solution(mesh):
    return jax.shard_map(
        local,
        mesh=mesh,
        in_specs=(
            P("row", "col", None),
            P("row", "col", None),
            P("row", "col", None, None, None),
            P("row", "col", None),
            P("row", "col", None),
            P("row", "col", None),
            P("row", "col"),
            P("row", "col", None, None, None),
            P("row", "col", None),
        ),
        out_specs=(P("row", "col", None), P("row", "col", None)),
        check_vma=False,
    )
```

```python
import functools

import jax
import jax.numpy as jnp
from jax import lax
from jax.experimental import pallas as pl
from jax.experimental.pallas import tpu as pltpu
from jax.sharding import PartitionSpec as P

LANES = 128
UNROLL = 3
F32 = jnp.float32
BF16 = jnp.bfloat16
VMEM = pl.BlockSpec(memory_space=pltpu.VMEM)
SMEM = pl.BlockSpec(memory_space=pltpu.SMEM)
HBM = pl.BlockSpec(memory_space=pltpu.HBM)
PARAMS = pltpu.CompilerParams(vmem_limit_bytes=6 << 20)


def dot_nt(left, right):
    return lax.dot_general(left, right, (((1,), (1,)), ((), ())), preferred_element_type=F32)


def split(value):
    high = value.astype(BF16)
    low = (value - high.astype(F32)).astype(BF16)
    return high, low


def total(value):
    return jnp.sum(jnp.sum(value, axis=0, keepdims=True), axis=1, keepdims=True)


def lane_row(values):
    lane = lax.broadcasted_iota(jnp.int32, (1, LANES), 1)
    row = jnp.zeros((1, LANES), F32)
    for place, value in enumerate(values):
        row = jnp.where(lane == place, value, row)
    return row


def pick(row, place):
    lane = lax.broadcasted_iota(jnp.int32, (1, LANES), 1)
    return jnp.sum(jnp.where(lane == place, row, 0.0), axis=1, keepdims=True)


def load_rows(ref, count):
    return jnp.concatenate(
        [ref[0, :, pl.ds(k * LANES, LANES)] for k in range(count)], axis=0
    )


def fault_scalars(sizes, faults):
    start = jnp.int32(0)
    scalars = []
    for f in range(faults):
        scalars.append((start // LANES, start % LANES, sizes[0, 0, f]))
        start = start + sizes[0, 0, f]
    return scalars


def leading(remote, blocks, sems, group):
    near = pl.ds(0, blocks.shape[1] // 2)
    part = (pl.ds(group * 8, 8), near, near)
    return pltpu.make_async_copy(remote.at[(0, 0) + part], blocks.at[part], sems.at[0, group])


def beyond(remote, blocks, sems, f):
    half = blocks.shape[1] // 2
    return [
        pltpu.make_async_copy(
            remote.at[(0, 0, f) + part], blocks.at[(f,) + part], sems.at[place, f]
        )
        for place, part in [(1, (pl.ds(0, half), pl.ds(half, half))), (2, (pl.ds(half, half),))]
    ]


def fetch(scalars, remote, blocks, sems):
    half = blocks.shape[1] // 2
    for group in range(len(scalars) // 8):
        leading(remote, blocks, sems, group).start()
    for f, (_, _, size) in enumerate(scalars):

        @pl.when(size > half)
        def _():
            for copy in beyond(remote, blocks, sems, f):
                copy.start()


def make_plan(scalars, plan, column):
    chosen, chosen_t, shifts, lens = plan
    faults = len(scalars)
    depth, rows = chosen_t.shape
    chunks = depth // faults - 1
    column[...] = jnp.full(column.shape, -1, jnp.int32)
    place = lax.broadcasted_iota(jnp.int32, (1, depth), 1)
    target = jnp.full((1, depth), -1, jnp.int32)
    for f, (tile, shift, size) in enumerate(scalars):
        shifts[f : f + 1, :] = jnp.full((1, LANES), shift, jnp.int32)
        lens[f : f + 1, :] = jnp.full((1, LANES), size, jnp.int32)
        for k in range(chunks + 1):
            spot = k * faults + f
            column[spot : spot + 1, :] = jnp.full((1, LANES), tile + k, jnp.int32)
            target = jnp.where(place == spot, tile + k, target)
    chosen[...] = (lax.broadcasted_iota(jnp.int32, (rows, depth), 0) == target).astype(BF16)
    chosen_t[...] = (
        lax.broadcasted_iota(jnp.int32, (depth, rows), 1) == column[:, 0:1]
    ).astype(BF16)


def select(chosen, value):
    high, low = split(value)
    return jnp.dot(chosen, high, preferred_element_type=F32) + jnp.dot(
        chosen, low, preferred_element_type=F32
    )


def precondition(sizes, plan, field, blocks, work, remote=None, sems=None):
    chosen, chosen_t, shifts, lens = plan
    stack, lefts, found, large = work
    faults = blocks.shape[0]
    chunks = blocks.shape[1] // LANES
    local = remote is None
    lane = lax.broadcasted_iota(jnp.int32, (faults, LANES), 1)
    windows = select(chosen_t[...], field[...])
    shift = shifts[...]
    size = lens[...]
    bits = [((shift >> b) & 1) == 1 for b in range(7)]
    live = [lane + k * LANES < size for k in range(chunks)]
    parts = [windows[k * faults : (k + 1) * faults] for k in range(chunks + 1)]
    for b in range(7):
        step = 1 << b
        rolled = [pltpu.roll(part, LANES - step, 1) for part in parts]
        moved = [
            jnp.where(lane < LANES - step, rolled[k], rolled[min(k + 1, chunks)])
            for k in range(chunks + 1)
        ]
        parts = [jnp.where(bits[b], new, old) for new, old in zip(moved, parts)]
    parts = [jnp.where(live[k], parts[k], 0.0) for k in range(chunks)]
    sub = lax.broadcasted_iota(jnp.int32, (8, LANES), 0)
    half = blocks.shape[1] // 2
    chunk_half = chunks // 2
    for group in range(faults // 8):
        pieces = []
        for k in range(chunks):
            high, low = split(parts[k][group * 8 : group * 8 + 8])
            pieces.append(jnp.concatenate([high, low], axis=0))
        left = jnp.concatenate(pieces, axis=1)
        lefts[group] = left
        sums = [jnp.zeros((8, LANES), F32) for _ in range(chunk_half)]
        for place in range(8):
            f = group * 8 + place
            if not local and place == 0:
                leading(remote, blocks, sems, group).wait()
            result = dot_nt(left[:, :half], blocks[f, :half, :half])
            result = result[:8] + result[8:]
            for k in range(chunk_half):
                sums[k] = jnp.where(sub == place, result[:, k * LANES : (k + 1) * LANES], sums[k])
        for k in range(chunks):
            found[k, group] = sums[k] if k < chunk_half else jnp.zeros((8, LANES), F32)
    count = jnp.int32(0)
    for f in range(faults):
        large[count] = f
        count = count + (sizes[0, 0, f] > half).astype(jnp.int32)

    def rest(step, carry):
        for u in range(UNROLL):
            place = step * UNROLL + u
            f = large[jnp.minimum(place, count - 1)]
            group = f // 8
            left = lefts[group]
            if not local:

                @pl.when(place < count)
                def _():
                    for copy in beyond(remote, blocks, sems, f):
                        copy.wait()

            above = dot_nt(left[:, half:], blocks[f, :half, half:])
            below = dot_nt(left, blocks[f, half:, :])
            above = above[:8] + above[8:]
            below = below[:8] + below[8:]
            mine = jnp.logical_and(sub == f % 8, place < count)
            for k in range(chunk_half):
                piece = slice(k * LANES, (k + 1) * LANES)
                found[k, group] += jnp.where(mine, above[:, piece], 0.0)
                found[chunk_half + k, group] += jnp.where(mine, below[:, piece], 0.0)
        return carry

    lax.fori_loop(0, (count + UNROLL - 1) // UNROLL, rest, 0)
    parts = [
        jnp.where(live[k], found[k].reshape(faults, LANES), 0.0) for k in range(chunks)
    ]
    parts.append(jnp.zeros((faults, LANES), F32))
    for b in range(7):
        step = 1 << b
        rolled = [pltpu.roll(part, step, 1) for part in parts]
        moved = [
            jnp.where(lane >= step, rolled[k], rolled[k - 1] if k else 0.0)
            for k in range(chunks + 1)
        ]
        parts = [jnp.where(bits[b], new, old) for new, old in zip(moved, parts)]
    count = faults * (chunks + 1)
    for k in range(chunks + 1):
        stack[k * faults : (k + 1) * faults, :] = parts[k]
    depth = stack.shape[0]
    if depth > count:
        stack[count:depth, :] = jnp.zeros((depth - count, LANES), F32)
    return select(chosen[...], stack[...])


def set_field(field, value):
    tiles = value.shape[0]
    field[0:tiles, :] = value
    field[tiles:, :] = jnp.zeros((field.shape[0] - tiles, LANES), F32)


def owner(index, each, count):
    found = jnp.zeros(index.shape, jnp.int32)
    for c in range(1, count):
        found = found + (index >= c * each).astype(jnp.int32)
    return found


def first_kernel(far_sizes, far_rhs, far_friction, remote, send, blocks, *refs):
    plan, (sizes, rhs, friction, column, sems, block_sems, field, *work) = refs[:4], refs[4:]
    tiles = rhs.shape[2] // LANES
    pairs = [(far_sizes, sizes), (far_rhs, rhs), (far_friction, friction)]
    copies = [pltpu.make_async_copy(a, b, sems.at[i]) for i, (a, b) in enumerate(pairs)]
    for copy in copies:
        copy.start()
    copies[0].wait()
    scalars = fault_scalars(sizes, blocks.shape[0])
    fetch(scalars, remote, blocks, block_sems)
    make_plan(scalars, plan, column)
    copies[1].wait()
    set_field(field, load_rows(rhs, tiles))
    direction = precondition(sizes, plan, field, blocks, work, remote, block_sems)[0:tiles]
    copies[2].wait()
    value = field[0:tiles, :]
    scaled = load_rows(friction, tiles) * direction
    send[...] = jnp.zeros_like(send)
    send[0:tiles, :] = direction
    send[tiles : tiles + 1, :] = lane_row([total(value * value), total(value * scaled)])


def gathered(parts, tiles):
    whole = parts[0][...]
    for part in parts[1:]:
        whole = whole + part[...]
    return whole[0:tiles], whole[tiles : tiles + 1]


def second_kernel(sizes, rhs, friction, blocks, *refs):
    plan, sent, parts = refs[:4], refs[4], refs[5:-8]
    send, image_out, basis_out, field, *work = refs[-8:]
    tiles = rhs.shape[2] // LANES
    start = load_rows(rhs, tiles)
    diagonal = load_rows(friction, tiles)
    product, sums = gathered(parts, tiles)
    norm2 = pick(sums, 0)
    image = diagonal * sent[0:tiles, :] + product
    scale = lax.rsqrt(norm2)
    value = (image - pick(sums, 1) / norm2 * start) * scale
    image_out[...] = image
    basis_out[0:tiles, :] = value
    basis_out[tiles:, :] = jnp.broadcast_to(norm2, (basis_out.shape[0] - tiles, LANES))
    set_field(field, value)
    direction = precondition(sizes, plan, field, blocks, work)[0:tiles]
    scaled = diagonal * direction
    send[...] = jnp.zeros_like(send)
    send[0:tiles, :] = direction
    send[tiles : tiles + 1, :] = lane_row(
        [
            total(value * value),
            total(start * value) * scale,
            total(start * scaled) * scale,
            total(value * scaled),
        ]
    )


def third_kernel(sizes, rhs, friction, blocks, *refs):
    plan, sent, basis, parts = refs[:4], refs[4], refs[5], refs[6:-7]
    send, image_out, field, *work = refs[-7:]
    tiles = rhs.shape[2] // LANES
    start = load_rows(rhs, tiles)
    diagonal = load_rows(friction, tiles)
    product, sums = gathered(parts, tiles)
    image = diagonal * sent[0:tiles, :] + product
    value = basis[0:tiles, :]
    scale = lax.rsqrt(basis[tiles : tiles + 1, 0:1])
    norm2, cross, along_start, along = [pick(sums, k) for k in range(4)]
    left = norm2 - cross * cross
    usable = left > 1e-5 * norm2
    along = jnp.where(usable, (along - cross * along_start) / jnp.where(usable, left, 1.0), 0.0)
    along_start = along_start - cross * along
    value = (image - along * value - (along_start * scale) * start) * lax.rsqrt(
        jnp.maximum(norm2, 1e-30)
    )
    image_out[...] = image
    set_field(field, value)
    direction = precondition(sizes, plan, field, blocks, work)[0:tiles]
    send[...] = jnp.zeros_like(send)
    send[0:tiles, :] = direction


def fourth_kernel(rhs, friction, sent, image0, image1, *refs):
    parts, (image_out, sums_out) = refs[:-2], refs[-2:]
    tiles = rhs.shape[2] // LANES
    start = load_rows(rhs, tiles)
    product, _ = gathered(parts, tiles)
    image = load_rows(friction, tiles) * sent[0:tiles, :] + product
    image_out[...] = image
    images = [image0[...], image1[...], image]
    values = [total(images[i] * images[j]) for i in range(3) for j in range(i + 1)]
    values += [total(start * one) for one in images]
    sums_out[...] = jnp.broadcast_to(lane_row(values), sums_out.shape)


def last_kernel(sums, rhs, image0, image1, image2, sent0, sent1, sent2, update, residual):
    tiles = rhs.shape[2] // LANES
    row = jnp.sum(sums[...], axis=0, keepdims=True)
    entries = [pick(row, k) for k in range(9)]
    scale = [lax.rsqrt(jnp.maximum(entries[k], 1e-30)) for k in (0, 2, 5)]
    gram = {}
    place = 0
    for i in range(3):
        for j in range(i + 1):
            gram[i, j] = entries[place] * scale[i] * scale[j]
            place += 1
    goal = [entries[6 + i] * scale[i] for i in range(3)]
    low10 = gram[1, 0]
    low20 = gram[2, 0]
    pivot1 = 1.0 - low10 * low10
    keep1 = pivot1 > 1e-6
    inverse1 = jnp.where(keep1, 1.0 / jnp.where(keep1, pivot1, 1.0), 0.0)
    cross = gram[2, 1] - low20 * low10
    low21 = cross * inverse1
    pivot2 = 1.0 - low20 * low20 - cross * low21
    keep2 = pivot2 > 1e-6
    inverse2 = jnp.where(keep2, 1.0 / jnp.where(keep2, pivot2, 1.0), 0.0)
    part1 = goal[1] - low10 * goal[0]
    part2 = goal[2] - low20 * goal[0] - low21 * part1
    weight2 = part2 * inverse2
    weight1 = part1 * inverse1 - low21 * weight2
    weight0 = goal[0] - low10 * weight1 - low20 * weight2
    weights = [weight0 * scale[0], weight1 * scale[1], weight2 * scale[2]]
    start = load_rows(rhs, tiles)
    best = (
        weights[0] * sent0[0:tiles, :]
        + weights[1] * sent1[0:tiles, :]
        + weights[2] * sent2[0:tiles, :]
    )
    rest = start - weights[0] * image0[...] - weights[1] * image1[...] - weights[2] * image2[...]
    for k in range(tiles):
        update[0, :, pl.ds(k * LANES, LANES)] = best[k : k + 1]
        residual[0, :, pl.ds(k * LANES, LANES)] = rest[k : k + 1]


def prepare_kernel(shape, after, counts, tile_row, tile_col, scale, remote, blocks, *refs):
    gather, high, low, sems = refs
    tiles, height, row_count, col_count = shape
    slots = blocks.shape[0]
    pieces = sems.shape[0]
    copies = []
    for p in range(pieces):
        part = pl.ds(p * (slots // pieces), slots // pieces)
        copies.append(
            pltpu.make_async_copy(remote.at[0, 0, part], blocks.at[part], sems.at[p])
        )
        copies[-1].start()
    column = tile_col[0]
    source = owner(column, tiles, row_count)
    spots = (source ^ lax.axis_index("row")) * height + column - source * tiles
    ones = jnp.ones((LANES, LANES), BF16)
    for base in range(0, slots, LANES):
        mine = spots[:, base : base + LANES].astype(F32)
        square = lax.broadcasted_iota(jnp.int32, (LANES, LANES), 0)
        across = lax.broadcasted_iota(jnp.int32, (LANES, LANES), 1)
        square = jnp.where(square == across, mine, 0.0).astype(BF16)
        down = jnp.dot(square, ones, preferred_element_type=F32)[:, 0:1].astype(jnp.int32)
        wide = lax.broadcasted_iota(jnp.int32, (LANES, gather.shape[1]), 1)
        gather[base : base + LANES, :] = (wide == down).astype(BF16)
    row = tile_row[0]
    source = owner(row, tiles, col_count)
    place = source ^ lax.axis_index("col")
    place = (place & 1) * (col_count // 2) + (place >> 1)
    target = place * height + row - source * tiles
    slot = lax.broadcasted_iota(jnp.int32, target.shape, 1)
    weight = jnp.where(slot < counts[0, 0], scale[0], 0.0)
    chosen = jnp.where(lax.broadcasted_iota(jnp.int32, high.shape, 0) == target, weight, 0.0)
    high[...], low[...] = split(chosen)
    for copy in copies:
        copy.wait()


def tiles_kernel(tail, gather, chosen_high, chosen_low, blocks, *refs):
    sent, (keep, give, found, products) = refs[:-4], refs[-4:]
    slots = blocks.shape[0]
    far, height = keep.shape[0], keep.shape[1]
    groups = slots // 16
    field = jnp.concatenate([one[...] for one in sent], axis=0).astype(BF16)
    found[...] = jnp.dot(gather[...], field, preferred_element_type=F32)
    sub = lax.broadcasted_iota(jnp.int32, (8, LANES), 0)
    blank = jnp.zeros((8, LANES), F32)
    for group in range(groups):
        base = group * 16
        top = jnp.concatenate([found[base : base + 8, :], blank], axis=1)
        bottom = jnp.concatenate([blank, found[base + 8 : base + 16, :]], axis=1)
        left = jnp.concatenate([top, bottom], axis=0).astype(BF16)
        first, second = blank, blank
        for p in range(4):
            a, b = base + 2 * p, base + 2 * p + 1
            right = jnp.concatenate(
                [
                    jnp.concatenate([blocks[a], blocks[a + 8]], axis=1),
                    jnp.concatenate([blocks[b], blocks[b + 8]], axis=1),
                ],
                axis=0,
            )
            result = dot_nt(left, right)
            for spot, half in ((2 * p, slice(0, LANES)), (2 * p + 1, slice(LANES, 2 * LANES))):
                first = jnp.where(sub == spot, result[:8, half], first)
                second = jnp.where(sub == spot, result[8:, half], second)
        products[base : base + 8, :] = first
        products[base + 8 : base + 16, :] = second
    high, low = split(products[...])
    value = (
        jnp.dot(chosen_high[...], high, preferred_element_type=F32)
        + jnp.dot(chosen_low[...], high, preferred_element_type=F32)
        + jnp.dot(chosen_high[...], low, preferred_element_type=F32)
    )
    keep[...] = value[: far * height].reshape(far, height, LANES)
    give[...] = value[far * height :].reshape(far, height, LANES)
    last = height - 8
    sums = sent[0][last:height, :]
    for one in sent[1:]:
        sums = sums + one[last:height, :]
    sums = jnp.where(lax.broadcasted_iota(jnp.int32, (8, LANES), 0) == tail, sums, 0.0)
    for k in range(far):
        keep[k, last:height, :] += sums
        give[k, last:height, :] += sums


def scratch(shape, dtype=F32):
    return pltpu.VMEM(shape, dtype)


def local(
    rhs,
    friction,
    kernel_tiles,
    tile_scale,
    tile_row,
    tile_col,
    tile_counts,
    precond_blocks,
    fault_sizes,
):
    length = rhs.shape[2]
    slots = kernel_tiles.shape[2]
    faults, width = precond_blocks.shape[2], precond_blocks.shape[3]
    tiles = length // LANES
    height = (tiles + 8) // 8 * 8
    chunks = width // LANES
    row_count = lax.axis_size("row")
    col_count = lax.axis_size("col")
    far = col_count // 2
    rows = (tiles + chunks + 8) // 8 * 8
    depth = (faults * (chunks + 1) + LANES - 1) // LANES * LANES

    grid = jax.ShapeDtypeStruct((height, LANES), F32)
    plain = jax.ShapeDtypeStruct((tiles, LANES), F32)
    half_grid = jax.ShapeDtypeStruct((far, height, LANES), F32)
    work = [
        scratch((rows, LANES)),
        scratch((depth, LANES)),
        scratch((faults // 8, 16, width), BF16),
        scratch((chunks, faults // 8, 8, LANES)),
        pltpu.SMEM((faults + 1,), jnp.int32),
    ]

    def exchange(value, axis, distance):
        size = lax.axis_size(axis)
        return lax.ppermute(value, axis, [(i, i ^ distance) for i in range(size)])

    def pinned(value):
        return pltpu.with_memory_space_constraint(value, pltpu.HBM)

    sent0, near_blocks, *plan = pl.pallas_call(
        first_kernel,
        out_shape=[
            grid,
            pltpu.VMEM((faults, width, width), BF16),
            jax.ShapeDtypeStruct((rows, depth), BF16),
            jax.ShapeDtypeStruct((depth, rows), BF16),
            jax.ShapeDtypeStruct((faults, LANES), jnp.int32),
            jax.ShapeDtypeStruct((faults, LANES), jnp.int32),
        ],
        in_specs=[HBM] * 4,
        out_specs=[VMEM] * 6,
        scratch_shapes=[
            pltpu.SMEM(fault_sizes.shape, jnp.int32),
            scratch(rhs.shape),
            scratch(friction.shape),
            scratch((depth, LANES), jnp.int32),
            pltpu.SemaphoreType.DMA((3,)),
            pltpu.SemaphoreType.DMA((3, faults)),
        ]
        + work,
        compiler_params=PARAMS,
        name="first",
    )(pinned(fault_sizes), pinned(rhs), pinned(friction), pinned(precond_blocks))
    spread = (2 * far * height, slots)
    near_tiles, *selections = pl.pallas_call(
        functools.partial(prepare_kernel, (tiles, height, row_count, col_count)),
        out_shape=[
            pltpu.VMEM((slots, LANES, LANES), BF16),
            jax.ShapeDtypeStruct((slots, row_count * height), BF16),
            jax.ShapeDtypeStruct(spread, BF16),
            jax.ShapeDtypeStruct(spread, BF16),
        ],
        in_specs=[VMEM, SMEM, VMEM, VMEM, VMEM, HBM],
        out_specs=[VMEM] * 4,
        scratch_shapes=[pltpu.SemaphoreType.DMA((4,))],
        compiler_params=PARAMS,
        name="prepare",
    )(plan[3], tile_counts, tile_row, tile_col, tile_scale, pinned(kernel_tiles))

    def apply_kernel(sent):
        got = [sent] + [exchange(sent, "row", d) for d in range(1, row_count)]
        keep, give = pl.pallas_call(
            functools.partial(tiles_kernel, tiles % 8),
            out_shape=[half_grid, half_grid],
            in_specs=[VMEM] * (4 + row_count),
            out_specs=[VMEM] * 2,
            scratch_shapes=[
                scratch((slots, LANES)),
                scratch((slots, LANES)),
            ],
            compiler_params=PARAMS,
            name="tiles",
        )(*selections, near_tiles, *got)
        both = keep + exchange(give, "col", 1)
        return [both[0]] + [exchange(both[d], "col", 2 * d) for d in range(1, far)]

    parts0 = apply_kernel(sent0)
    sent1, image0, basis = pl.pallas_call(
        second_kernel,
        out_shape=[grid, plain, grid],
        in_specs=[SMEM, VMEM, VMEM, VMEM] + [VMEM] * (5 + far),
        out_specs=[VMEM] * 3,
        scratch_shapes=work,
        compiler_params=PARAMS,
        name="second",
    )(fault_sizes, rhs, friction, near_blocks, *plan, sent0, *parts0)
    parts1 = apply_kernel(sent1)
    sent2, image1 = pl.pallas_call(
        third_kernel,
        out_shape=[grid, plain],
        in_specs=[SMEM, VMEM, VMEM, VMEM] + [VMEM] * (6 + far),
        out_specs=[VMEM] * 2,
        scratch_shapes=work,
        compiler_params=PARAMS,
        name="third",
    )(fault_sizes, rhs, friction, near_blocks, *plan, sent1, basis, *parts1)
    parts2 = apply_kernel(sent2)
    devices = row_count * col_count
    image2, sums = pl.pallas_call(
        fourth_kernel,
        out_shape=[plain, jax.ShapeDtypeStruct((devices, LANES), F32)],
        in_specs=[VMEM] * (5 + far),
        out_specs=[VMEM] * 2,
        compiler_params=PARAMS,
        name="fourth",
    )(rhs, friction, sent2, image0, image1, *parts2)
    sums = lax.all_to_all(sums, ("row", "col"), 0, 0, tiled=True)
    whole = jax.ShapeDtypeStruct((1, 1, length), F32)
    return pl.pallas_call(
        last_kernel,
        out_shape=[whole, whole],
        in_specs=[VMEM] * 8,
        out_specs=[VMEM] * 2,
        compiler_params=PARAMS,
        name="last",
    )(sums, rhs, image0, image1, image2, sent0, sent1, sent2)


def solution(mesh):
    return jax.shard_map(
        local,
        mesh=mesh,
        in_specs=(
            P("row", "col", None),
            P("row", "col", None),
            P("row", "col", None, None, None),
            P("row", "col", None),
            P("row", "col", None),
            P("row", "col", None),
            P("row", "col"),
            P("row", "col", None, None, None),
            P("row", "col", None),
        ),
        out_specs=(P("row", "col", None), P("row", "col", None)),
        check_vma=False,
    )
```

```python
import functools

import jax
import jax.numpy as jnp
from jax import lax
from jax.experimental import pallas as pl
from jax.experimental.pallas import tpu as pltpu
from jax.sharding import PartitionSpec as P

LANES = 128
UNROLL = 4
F32 = jnp.float32
BF16 = jnp.bfloat16
VMEM = pl.BlockSpec(memory_space=pltpu.VMEM)
SMEM = pl.BlockSpec(memory_space=pltpu.SMEM)
HBM = pl.BlockSpec(memory_space=pltpu.HBM)
PARAMS = pltpu.CompilerParams(vmem_limit_bytes=6 << 20)


def dot_nt(left, right):
    return lax.dot_general(left, right, (((1,), (1,)), ((), ())), preferred_element_type=F32)


def split(value):
    high = value.astype(BF16)
    low = (value - high.astype(F32)).astype(BF16)
    return high, low


def total(value):
    return jnp.sum(jnp.sum(value, axis=0, keepdims=True), axis=1, keepdims=True)


def lane_row(values):
    lane = lax.broadcasted_iota(jnp.int32, (1, LANES), 1)
    row = jnp.zeros((1, LANES), F32)
    for place, value in enumerate(values):
        row = jnp.where(lane == place, value, row)
    return row


def pick(row, place):
    lane = lax.broadcasted_iota(jnp.int32, (1, LANES), 1)
    return jnp.sum(jnp.where(lane == place, row, 0.0), axis=1, keepdims=True)


def load_rows(ref, count):
    return jnp.concatenate(
        [ref[0, :, pl.ds(k * LANES, LANES)] for k in range(count)], axis=0
    )


def fault_scalars(sizes, faults):
    start = jnp.int32(0)
    scalars = []
    for f in range(faults):
        scalars.append((start // LANES, start % LANES, sizes[0, 0, f]))
        start = start + sizes[0, 0, f]
    return scalars


def leading(remote, blocks, sems, group):
    near = pl.ds(0, blocks.shape[1] // 2)
    part = (pl.ds(group * 8, 8), near, near)
    return pltpu.make_async_copy(remote.at[(0, 0) + part], blocks.at[part], sems.at[0, group])


def beyond(remote, blocks, sems, f):
    half = blocks.shape[1] // 2
    return [
        pltpu.make_async_copy(
            remote.at[(0, 0, f) + part], blocks.at[(f,) + part], sems.at[place, f]
        )
        for place, part in [(1, (pl.ds(0, half), pl.ds(half, half))), (2, (pl.ds(half, half),))]
    ]


def fetch(scalars, remote, blocks, sems):
    half = blocks.shape[1] // 2
    for group in range(len(scalars) // 8):
        leading(remote, blocks, sems, group).start()
    for f, (_, _, size) in enumerate(scalars):

        @pl.when(size > half)
        def _():
            for copy in beyond(remote, blocks, sems, f):
                copy.start()


def make_plan(scalars, plan, column):
    chosen, chosen_t, shifts, lens = plan
    faults = len(scalars)
    depth, rows = chosen_t.shape
    chunks = depth // faults - 1
    column[...] = jnp.full(column.shape, -1, jnp.int32)
    place = lax.broadcasted_iota(jnp.int32, (1, depth), 1)
    target = jnp.full((1, depth), -1, jnp.int32)
    for f, (tile, shift, size) in enumerate(scalars):
        shifts[f : f + 1, :] = jnp.full((1, LANES), shift, jnp.int32)
        lens[f : f + 1, :] = jnp.full((1, LANES), size, jnp.int32)
        for k in range(chunks + 1):
            spot = k * faults + f
            column[spot : spot + 1, :] = jnp.full((1, LANES), tile + k, jnp.int32)
            target = jnp.where(place == spot, tile + k, target)
    chosen[...] = (lax.broadcasted_iota(jnp.int32, (rows, depth), 0) == target).astype(BF16)
    chosen_t[...] = (
        lax.broadcasted_iota(jnp.int32, (depth, rows), 1) == column[:, 0:1]
    ).astype(BF16)


def select(chosen, value):
    high, low = split(value)
    return jnp.dot(chosen, high, preferred_element_type=F32) + jnp.dot(
        chosen, low, preferred_element_type=F32
    )


def precondition(sizes, plan, field, blocks, work, remote=None, sems=None):
    chosen, chosen_t, shifts, lens = plan
    stack, lefts, found, large = work
    faults = blocks.shape[0]
    chunks = blocks.shape[1] // LANES
    local = remote is None
    lane = lax.broadcasted_iota(jnp.int32, (faults, LANES), 1)
    windows = select(chosen_t[...], field[...])
    shift = shifts[...]
    size = lens[...]
    bits = [((shift >> b) & 1) == 1 for b in range(7)]
    live = [lane + k * LANES < size for k in range(chunks)]
    parts = [windows[k * faults : (k + 1) * faults] for k in range(chunks + 1)]
    for b in range(7):
        step = 1 << b
        rolled = [pltpu.roll(part, LANES - step, 1) for part in parts]
        moved = [
            jnp.where(lane < LANES - step, rolled[k], rolled[min(k + 1, chunks)])
            for k in range(chunks + 1)
        ]
        parts = [jnp.where(bits[b], new, old) for new, old in zip(moved, parts)]
    parts = [jnp.where(live[k], parts[k], 0.0) for k in range(chunks)]
    sub = lax.broadcasted_iota(jnp.int32, (8, LANES), 0)
    half = blocks.shape[1] // 2
    chunk_half = chunks // 2
    for group in range(faults // 8):
        pieces = []
        for k in range(chunks):
            high, low = split(parts[k][group * 8 : group * 8 + 8])
            pieces.append(jnp.concatenate([high, low], axis=0))
        left = jnp.concatenate(pieces, axis=1)
        lefts[group] = left
        sums = [jnp.zeros((8, LANES), F32) for _ in range(chunk_half)]
        for place in range(8):
            f = group * 8 + place
            if not local and place == 0:
                leading(remote, blocks, sems, group).wait()
            result = dot_nt(left[:, :half], blocks[f, :half, :half])
            result = result[:8] + result[8:]
            for k in range(chunk_half):
                sums[k] = jnp.where(sub == place, result[:, k * LANES : (k + 1) * LANES], sums[k])
        for k in range(chunks):
            found[k, group] = sums[k] if k < chunk_half else jnp.zeros((8, LANES), F32)
    count = jnp.int32(0)
    for f in range(faults):
        large[count] = f
        count = count + (sizes[0, 0, f] > half).astype(jnp.int32)

    def rest(step, carry):
        for u in range(UNROLL):
            place = step * UNROLL + u
            f = large[jnp.minimum(place, count - 1)]
            group = f // 8
            left = lefts[group]
            if not local:

                @pl.when(place < count)
                def _():
                    for copy in beyond(remote, blocks, sems, f):
                        copy.wait()

            above = dot_nt(left[:, half:], blocks[f, :half, half:])
            below = dot_nt(left, blocks[f, half:, :])
            above = above[:8] + above[8:]
            below = below[:8] + below[8:]
            mine = jnp.logical_and(sub == f % 8, place < count)
            for k in range(chunk_half):
                piece = slice(k * LANES, (k + 1) * LANES)
                found[k, group] += jnp.where(mine, above[:, piece], 0.0)
                found[chunk_half + k, group] += jnp.where(mine, below[:, piece], 0.0)
        return carry

    lax.fori_loop(0, (count + UNROLL - 1) // UNROLL, rest, 0)
    parts = [
        jnp.where(live[k], found[k].reshape(faults, LANES), 0.0) for k in range(chunks)
    ]
    parts.append(jnp.zeros((faults, LANES), F32))
    for b in range(7):
        step = 1 << b
        rolled = [pltpu.roll(part, step, 1) for part in parts]
        moved = [
            jnp.where(lane >= step, rolled[k], rolled[k - 1] if k else 0.0)
            for k in range(chunks + 1)
        ]
        parts = [jnp.where(bits[b], new, old) for new, old in zip(moved, parts)]
    count = faults * (chunks + 1)
    for k in range(chunks + 1):
        stack[k * faults : (k + 1) * faults, :] = parts[k]
    depth = stack.shape[0]
    if depth > count:
        stack[count:depth, :] = jnp.zeros((depth - count, LANES), F32)
    return select(chosen[...], stack[...])


def set_field(field, value):
    tiles = value.shape[0]
    field[0:tiles, :] = value
    field[tiles:, :] = jnp.zeros((field.shape[0] - tiles, LANES), F32)


def owner(index, each, count):
    found = jnp.zeros(index.shape, jnp.int32)
    for c in range(1, count):
        found = found + (index >= c * each).astype(jnp.int32)
    return found


def first_kernel(far_sizes, far_rhs, far_friction, remote, send, blocks, *refs):
    plan, (sizes, rhs, friction, column, sems, block_sems, field, *work) = refs[:4], refs[4:]
    tiles = rhs.shape[2] // LANES
    pairs = [(far_sizes, sizes), (far_rhs, rhs), (far_friction, friction)]
    copies = [pltpu.make_async_copy(a, b, sems.at[i]) for i, (a, b) in enumerate(pairs)]
    for copy in copies:
        copy.start()
    copies[0].wait()
    scalars = fault_scalars(sizes, blocks.shape[0])
    fetch(scalars, remote, blocks, block_sems)
    make_plan(scalars, plan, column)
    copies[1].wait()
    set_field(field, load_rows(rhs, tiles))
    direction = precondition(sizes, plan, field, blocks, work, remote, block_sems)[0:tiles]
    copies[2].wait()
    value = field[0:tiles, :]
    scaled = load_rows(friction, tiles) * direction
    send[...] = jnp.zeros_like(send)
    send[0:tiles, :] = direction
    send[tiles : tiles + 1, :] = lane_row([total(value * value), total(value * scaled)])


def gathered(parts, tiles):
    whole = parts[0][...]
    for part in parts[1:]:
        whole = whole + part[...]
    return whole[0:tiles], whole[tiles : tiles + 1]


def second_kernel(sizes, rhs, friction, blocks, *refs):
    plan, sent, parts = refs[:4], refs[4], refs[5:-8]
    send, image_out, basis_out, field, *work = refs[-8:]
    tiles = rhs.shape[2] // LANES
    start = load_rows(rhs, tiles)
    diagonal = load_rows(friction, tiles)
    product, sums = gathered(parts, tiles)
    norm2 = pick(sums, 0)
    image = diagonal * sent[0:tiles, :] + product
    scale = lax.rsqrt(norm2)
    value = (image - pick(sums, 1) / norm2 * start) * scale
    image_out[...] = image
    basis_out[0:tiles, :] = value
    basis_out[tiles:, :] = jnp.broadcast_to(norm2, (basis_out.shape[0] - tiles, LANES))
    set_field(field, value)
    direction = precondition(sizes, plan, field, blocks, work)[0:tiles]
    scaled = diagonal * direction
    send[...] = jnp.zeros_like(send)
    send[0:tiles, :] = direction
    send[tiles : tiles + 1, :] = lane_row(
        [
            total(value * value),
            total(start * value) * scale,
            total(start * scaled) * scale,
            total(value * scaled),
        ]
    )


def third_kernel(sizes, rhs, friction, blocks, *refs):
    plan, sent, basis, parts = refs[:4], refs[4], refs[5], refs[6:-7]
    send, image_out, field, *work = refs[-7:]
    tiles = rhs.shape[2] // LANES
    start = load_rows(rhs, tiles)
    diagonal = load_rows(friction, tiles)
    product, sums = gathered(parts, tiles)
    image = diagonal * sent[0:tiles, :] + product
    value = basis[0:tiles, :]
    scale = lax.rsqrt(basis[tiles : tiles + 1, 0:1])
    norm2, cross, along_start, along = [pick(sums, k) for k in range(4)]
    left = norm2 - cross * cross
    usable = left > 1e-5 * norm2
    along = jnp.where(usable, (along - cross * along_start) / jnp.where(usable, left, 1.0), 0.0)
    along_start = along_start - cross * along
    value = (image - along * value - (along_start * scale) * start) * lax.rsqrt(
        jnp.maximum(norm2, 1e-30)
    )
    image_out[...] = image
    set_field(field, value)
    direction = precondition(sizes, plan, field, blocks, work)[0:tiles]
    send[...] = jnp.zeros_like(send)
    send[0:tiles, :] = direction


def fourth_kernel(rhs, friction, sent, image0, image1, *refs):
    parts, (image_out, sums_out) = refs[:-2], refs[-2:]
    tiles = rhs.shape[2] // LANES
    start = load_rows(rhs, tiles)
    product, _ = gathered(parts, tiles)
    image = load_rows(friction, tiles) * sent[0:tiles, :] + product
    image_out[...] = image
    images = [image0[...], image1[...], image]
    values = [total(images[i] * images[j]) for i in range(3) for j in range(i + 1)]
    values += [total(start * one) for one in images]
    sums_out[...] = jnp.broadcast_to(lane_row(values), sums_out.shape)


def last_kernel(sums, rhs, image0, image1, image2, sent0, sent1, sent2, update, residual):
    tiles = rhs.shape[2] // LANES
    row = jnp.sum(sums[...], axis=0, keepdims=True)
    entries = [pick(row, k) for k in range(9)]
    scale = [lax.rsqrt(jnp.maximum(entries[k], 1e-30)) for k in (0, 2, 5)]
    gram = {}
    place = 0
    for i in range(3):
        for j in range(i + 1):
            gram[i, j] = entries[place] * scale[i] * scale[j]
            place += 1
    goal = [entries[6 + i] * scale[i] for i in range(3)]
    low10 = gram[1, 0]
    low20 = gram[2, 0]
    pivot1 = 1.0 - low10 * low10
    keep1 = pivot1 > 1e-6
    inverse1 = jnp.where(keep1, 1.0 / jnp.where(keep1, pivot1, 1.0), 0.0)
    cross = gram[2, 1] - low20 * low10
    low21 = cross * inverse1
    pivot2 = 1.0 - low20 * low20 - cross * low21
    keep2 = pivot2 > 1e-6
    inverse2 = jnp.where(keep2, 1.0 / jnp.where(keep2, pivot2, 1.0), 0.0)
    part1 = goal[1] - low10 * goal[0]
    part2 = goal[2] - low20 * goal[0] - low21 * part1
    weight2 = part2 * inverse2
    weight1 = part1 * inverse1 - low21 * weight2
    weight0 = goal[0] - low10 * weight1 - low20 * weight2
    weights = [weight0 * scale[0], weight1 * scale[1], weight2 * scale[2]]
    start = load_rows(rhs, tiles)
    best = (
        weights[0] * sent0[0:tiles, :]
        + weights[1] * sent1[0:tiles, :]
        + weights[2] * sent2[0:tiles, :]
    )
    rest = start - weights[0] * image0[...] - weights[1] * image1[...] - weights[2] * image2[...]
    for k in range(tiles):
        update[0, :, pl.ds(k * LANES, LANES)] = best[k : k + 1]
        residual[0, :, pl.ds(k * LANES, LANES)] = rest[k : k + 1]


def prepare_kernel(shape, after, counts, tile_row, tile_col, scale, remote, blocks, *refs):
    gather, high, low, sems = refs
    tiles, height, row_count, col_count = shape
    slots = blocks.shape[0]
    pieces = sems.shape[0]
    copies = []
    for p in range(pieces):
        part = pl.ds(p * (slots // pieces), slots // pieces)
        copies.append(
            pltpu.make_async_copy(remote.at[0, 0, part], blocks.at[part], sems.at[p])
        )
        copies[-1].start()
    column = tile_col[0]
    source = owner(column, tiles, row_count)
    spots = (source ^ lax.axis_index("row")) * height + column - source * tiles
    ones = jnp.ones((LANES, LANES), BF16)
    for base in range(0, slots, LANES):
        mine = spots[:, base : base + LANES].astype(F32)
        square = lax.broadcasted_iota(jnp.int32, (LANES, LANES), 0)
        across = lax.broadcasted_iota(jnp.int32, (LANES, LANES), 1)
        square = jnp.where(square == across, mine, 0.0).astype(BF16)
        down = jnp.dot(square, ones, preferred_element_type=F32)[:, 0:1].astype(jnp.int32)
        wide = lax.broadcasted_iota(jnp.int32, (LANES, gather.shape[1]), 1)
        gather[base : base + LANES, :] = (wide == down).astype(BF16)
    row = tile_row[0]
    source = owner(row, tiles, col_count)
    place = source ^ lax.axis_index("col")
    place = (place & 1) * (col_count // 2) + (place >> 1)
    target = place * height + row - source * tiles
    slot = lax.broadcasted_iota(jnp.int32, target.shape, 1)
    weight = jnp.where(slot < counts[0, 0], scale[0], 0.0)
    chosen = jnp.where(lax.broadcasted_iota(jnp.int32, high.shape, 0) == target, weight, 0.0)
    high[...], low[...] = split(chosen)
    for copy in copies:
        copy.wait()


def tiles_kernel(tail, gather, chosen_high, chosen_low, blocks, *refs):
    sent, (keep, give, found, products) = refs[:-4], refs[-4:]
    slots = blocks.shape[0]
    far, height = keep.shape[0], keep.shape[1]
    groups = slots // 16
    field = jnp.concatenate([one[...] for one in sent], axis=0).astype(BF16)
    found[...] = jnp.dot(gather[...], field, preferred_element_type=F32)
    sub = lax.broadcasted_iota(jnp.int32, (8, LANES), 0)
    blank = jnp.zeros((8, LANES), F32)
    for group in range(groups):
        base = group * 16
        top = jnp.concatenate([found[base : base + 8, :], blank], axis=1)
        bottom = jnp.concatenate([blank, found[base + 8 : base + 16, :]], axis=1)
        left = jnp.concatenate([top, bottom], axis=0).astype(BF16)
        first, second = blank, blank
        for p in range(4):
            a, b = base + 2 * p, base + 2 * p + 1
            right = jnp.concatenate(
                [
                    jnp.concatenate([blocks[a], blocks[a + 8]], axis=1),
                    jnp.concatenate([blocks[b], blocks[b + 8]], axis=1),
                ],
                axis=0,
            )
            result = dot_nt(left, right)
            for spot, half in ((2 * p, slice(0, LANES)), (2 * p + 1, slice(LANES, 2 * LANES))):
                first = jnp.where(sub == spot, result[:8, half], first)
                second = jnp.where(sub == spot, result[8:, half], second)
        products[base : base + 8, :] = first
        products[base + 8 : base + 16, :] = second
    high, low = split(products[...])
    value = (
        jnp.dot(chosen_high[...], high, preferred_element_type=F32)
        + jnp.dot(chosen_low[...], high, preferred_element_type=F32)
        + jnp.dot(chosen_high[...], low, preferred_element_type=F32)
    )
    keep[...] = value[: far * height].reshape(far, height, LANES)
    give[...] = value[far * height :].reshape(far, height, LANES)
    last = height - 8
    sums = sent[0][last:height, :]
    for one in sent[1:]:
        sums = sums + one[last:height, :]
    sums = jnp.where(lax.broadcasted_iota(jnp.int32, (8, LANES), 0) == tail, sums, 0.0)
    for k in range(far):
        keep[k, last:height, :] += sums
        give[k, last:height, :] += sums


def scratch(shape, dtype=F32):
    return pltpu.VMEM(shape, dtype)


def local(
    rhs,
    friction,
    kernel_tiles,
    tile_scale,
    tile_row,
    tile_col,
    tile_counts,
    precond_blocks,
    fault_sizes,
):
    length = rhs.shape[2]
    slots = kernel_tiles.shape[2]
    faults, width = precond_blocks.shape[2], precond_blocks.shape[3]
    tiles = length // LANES
    height = (tiles + 8) // 8 * 8
    chunks = width // LANES
    row_count = lax.axis_size("row")
    col_count = lax.axis_size("col")
    far = col_count // 2
    rows = (tiles + chunks + 8) // 8 * 8
    depth = (faults * (chunks + 1) + LANES - 1) // LANES * LANES

    grid = jax.ShapeDtypeStruct((height, LANES), F32)
    plain = jax.ShapeDtypeStruct((tiles, LANES), F32)
    half_grid = jax.ShapeDtypeStruct((far, height, LANES), F32)
    work = [
        scratch((rows, LANES)),
        scratch((depth, LANES)),
        scratch((faults // 8, 16, width), BF16),
        scratch((chunks, faults // 8, 8, LANES)),
        pltpu.SMEM((faults + 1,), jnp.int32),
    ]

    def exchange(value, axis, distance):
        size = lax.axis_size(axis)
        return lax.ppermute(value, axis, [(i, i ^ distance) for i in range(size)])

    def pinned(value):
        return pltpu.with_memory_space_constraint(value, pltpu.HBM)

    sent0, near_blocks, *plan = pl.pallas_call(
        first_kernel,
        out_shape=[
            grid,
            pltpu.VMEM((faults, width, width), BF16),
            jax.ShapeDtypeStruct((rows, depth), BF16),
            jax.ShapeDtypeStruct((depth, rows), BF16),
            jax.ShapeDtypeStruct((faults, LANES), jnp.int32),
            jax.ShapeDtypeStruct((faults, LANES), jnp.int32),
        ],
        in_specs=[HBM] * 4,
        out_specs=[VMEM] * 6,
        scratch_shapes=[
            pltpu.SMEM(fault_sizes.shape, jnp.int32),
            scratch(rhs.shape),
            scratch(friction.shape),
            scratch((depth, LANES), jnp.int32),
            pltpu.SemaphoreType.DMA((3,)),
            pltpu.SemaphoreType.DMA((3, faults)),
        ]
        + work,
        compiler_params=PARAMS,
        name="first",
    )(pinned(fault_sizes), pinned(rhs), pinned(friction), pinned(precond_blocks))
    spread = (2 * far * height, slots)
    near_tiles, *selections = pl.pallas_call(
        functools.partial(prepare_kernel, (tiles, height, row_count, col_count)),
        out_shape=[
            pltpu.VMEM((slots, LANES, LANES), BF16),
            jax.ShapeDtypeStruct((slots, row_count * height), BF16),
            jax.ShapeDtypeStruct(spread, BF16),
            jax.ShapeDtypeStruct(spread, BF16),
        ],
        in_specs=[VMEM, SMEM, VMEM, VMEM, VMEM, HBM],
        out_specs=[VMEM] * 4,
        scratch_shapes=[pltpu.SemaphoreType.DMA((4,))],
        compiler_params=PARAMS,
        name="prepare",
    )(plan[3], tile_counts, tile_row, tile_col, tile_scale, pinned(kernel_tiles))

    def apply_kernel(sent):
        got = [sent] + [exchange(sent, "row", d) for d in range(1, row_count)]
        keep, give = pl.pallas_call(
            functools.partial(tiles_kernel, tiles % 8),
            out_shape=[half_grid, half_grid],
            in_specs=[VMEM] * (4 + row_count),
            out_specs=[VMEM] * 2,
            scratch_shapes=[
                scratch((slots, LANES)),
                scratch((slots, LANES)),
            ],
            compiler_params=PARAMS,
            name="tiles",
        )(*selections, near_tiles, *got)
        both = keep + exchange(give, "col", 1)
        return [both[0]] + [exchange(both[d], "col", 2 * d) for d in range(1, far)]

    parts0 = apply_kernel(sent0)
    sent1, image0, basis = pl.pallas_call(
        second_kernel,
        out_shape=[grid, plain, grid],
        in_specs=[SMEM, VMEM, VMEM, VMEM] + [VMEM] * (5 + far),
        out_specs=[VMEM] * 3,
        scratch_shapes=work,
        compiler_params=PARAMS,
        name="second",
    )(fault_sizes, rhs, friction, near_blocks, *plan, sent0, *parts0)
    parts1 = apply_kernel(sent1)
    sent2, image1 = pl.pallas_call(
        third_kernel,
        out_shape=[grid, plain],
        in_specs=[SMEM, VMEM, VMEM, VMEM] + [VMEM] * (6 + far),
        out_specs=[VMEM] * 2,
        scratch_shapes=work,
        compiler_params=PARAMS,
        name="third",
    )(fault_sizes, rhs, friction, near_blocks, *plan, sent1, basis, *parts1)
    parts2 = apply_kernel(sent2)
    devices = row_count * col_count
    image2, sums = pl.pallas_call(
        fourth_kernel,
        out_shape=[plain, jax.ShapeDtypeStruct((devices, LANES), F32)],
        in_specs=[VMEM] * (5 + far),
        out_specs=[VMEM] * 2,
        compiler_params=PARAMS,
        name="fourth",
    )(rhs, friction, sent2, image0, image1, *parts2)
    sums = lax.all_to_all(sums, ("row", "col"), 0, 0, tiled=True)
    whole = jax.ShapeDtypeStruct((1, 1, length), F32)
    return pl.pallas_call(
        last_kernel,
        out_shape=[whole, whole],
        in_specs=[VMEM] * 8,
        out_specs=[VMEM] * 2,
        compiler_params=PARAMS,
        name="last",
    )(sums, rhs, image0, image1, image2, sent0, sent1, sent2)


def solution(mesh):
    return jax.shard_map(
        local,
        mesh=mesh,
        in_specs=(
            P("row", "col", None),
            P("row", "col", None),
            P("row", "col", None, None, None),
            P("row", "col", None),
            P("row", "col", None),
            P("row", "col", None),
            P("row", "col"),
            P("row", "col", None, None, None),
            P("row", "col", None),
        ),
        out_specs=(P("row", "col", None), P("row", "col", None)),
        check_vma=False,
    )
```

```python
import functools

import jax
import jax.numpy as jnp
from jax import lax
from jax.experimental import pallas as pl
from jax.experimental.pallas import tpu as pltpu
from jax.sharding import PartitionSpec as P

LANES = 128
UNROLL = 4
F32 = jnp.float32
BF16 = jnp.bfloat16
VMEM = pl.BlockSpec(memory_space=pltpu.VMEM)
SMEM = pl.BlockSpec(memory_space=pltpu.SMEM)
HBM = pl.BlockSpec(memory_space=pltpu.HBM)
PARAMS = pltpu.CompilerParams(vmem_limit_bytes=6 << 20)


def dot_nt(left, right):
    return lax.dot_general(left, right, (((1,), (1,)), ((), ())), preferred_element_type=F32)


def split(value):
    high = value.astype(BF16)
    low = (value - high.astype(F32)).astype(BF16)
    return high, low


def total(value):
    return jnp.sum(jnp.sum(value, axis=0, keepdims=True), axis=1, keepdims=True)


def lane_row(values):
    lane = lax.broadcasted_iota(jnp.int32, (1, LANES), 1)
    row = jnp.zeros((1, LANES), F32)
    for place, value in enumerate(values):
        row = jnp.where(lane == place, value, row)
    return row


def pick(row, place):
    lane = lax.broadcasted_iota(jnp.int32, (1, LANES), 1)
    return jnp.sum(jnp.where(lane == place, row, 0.0), axis=1, keepdims=True)


def load_rows(ref, count):
    return jnp.concatenate(
        [ref[0, :, pl.ds(k * LANES, LANES)] for k in range(count)], axis=0
    )


def fault_scalars(sizes, faults):
    start = jnp.int32(0)
    scalars = []
    for f in range(faults):
        scalars.append((start // LANES, start % LANES, sizes[0, 0, f]))
        start = start + sizes[0, 0, f]
    return scalars


def leading(remote, blocks, sems, group):
    near = pl.ds(0, blocks.shape[1] // 2)
    part = (pl.ds(group * 8, 8), near, near)
    return pltpu.make_async_copy(remote.at[(0, 0) + part], blocks.at[part], sems.at[0, group])


def beyond(remote, blocks, sems, f):
    half = blocks.shape[1] // 2
    return [
        pltpu.make_async_copy(
            remote.at[(0, 0, f) + part], blocks.at[(f,) + part], sems.at[place, f]
        )
        for place, part in [(1, (pl.ds(0, half), pl.ds(half, half))), (2, (pl.ds(half, half),))]
    ]


def fetch(scalars, remote, blocks, sems):
    half = blocks.shape[1] // 2
    for f, (_, _, size) in enumerate(scalars):

        @pl.when(size > half)
        def _():
            for copy in beyond(remote, blocks, sems, f):
                copy.start()


def make_plan(scalars, plan, column):
    chosen, chosen_t, shifts, lens = plan
    faults = len(scalars)
    depth, rows = chosen_t.shape
    chunks = depth // faults - 1
    column[...] = jnp.full(column.shape, -1, jnp.int32)
    place = lax.broadcasted_iota(jnp.int32, (1, depth), 1)
    target = jnp.full((1, depth), -1, jnp.int32)
    for f, (tile, shift, size) in enumerate(scalars):
        shifts[f : f + 1, :] = jnp.full((1, LANES), shift, jnp.int32)
        lens[f : f + 1, :] = jnp.full((1, LANES), size, jnp.int32)
        for k in range(chunks + 1):
            spot = k * faults + f
            column[spot : spot + 1, :] = jnp.full((1, LANES), tile + k, jnp.int32)
            target = jnp.where(place == spot, tile + k, target)
    chosen[...] = (lax.broadcasted_iota(jnp.int32, (rows, depth), 0) == target).astype(BF16)
    chosen_t[...] = (
        lax.broadcasted_iota(jnp.int32, (depth, rows), 1) == column[:, 0:1]
    ).astype(BF16)


def select(chosen, value):
    high, low = split(value)
    return jnp.dot(chosen, high, preferred_element_type=F32) + jnp.dot(
        chosen, low, preferred_element_type=F32
    )


def precondition(sizes, plan, field, blocks, work, remote=None, sems=None):
    chosen, chosen_t, shifts, lens = plan
    stack, lefts, found, large = work
    faults = blocks.shape[0]
    chunks = blocks.shape[1] // LANES
    local = remote is None
    lane = lax.broadcasted_iota(jnp.int32, (faults, LANES), 1)
    windows = select(chosen_t[...], field[...])
    shift = shifts[...]
    size = lens[...]
    bits = [((shift >> b) & 1) == 1 for b in range(7)]
    live = [lane + k * LANES < size for k in range(chunks)]
    parts = [windows[k * faults : (k + 1) * faults] for k in range(chunks + 1)]
    for b in range(7):
        step = 1 << b
        rolled = [pltpu.roll(part, LANES - step, 1) for part in parts]
        moved = [
            jnp.where(lane < LANES - step, rolled[k], rolled[min(k + 1, chunks)])
            for k in range(chunks + 1)
        ]
        parts = [jnp.where(bits[b], new, old) for new, old in zip(moved, parts)]
    parts = [jnp.where(live[k], parts[k], 0.0) for k in range(chunks)]
    sub = lax.broadcasted_iota(jnp.int32, (8, LANES), 0)
    half = blocks.shape[1] // 2
    chunk_half = chunks // 2
    for group in range(faults // 8):
        pieces = []
        for k in range(chunks):
            high, low = split(parts[k][group * 8 : group * 8 + 8])
            pieces.append(jnp.concatenate([high, low], axis=0))
        left = jnp.concatenate(pieces, axis=1)
        lefts[group] = left
        sums = [jnp.zeros((8, LANES), F32) for _ in range(chunk_half)]
        for place in range(8):
            f = group * 8 + place
            if not local and place == 0:
                leading(remote, blocks, sems, group).wait()
            result = dot_nt(left[:, :half], blocks[f, :half, :half])
            result = result[:8] + result[8:]
            for k in range(chunk_half):
                sums[k] = jnp.where(sub == place, result[:, k * LANES : (k + 1) * LANES], sums[k])
        for k in range(chunks):
            found[k, group] = sums[k] if k < chunk_half else jnp.zeros((8, LANES), F32)
    count = jnp.int32(0)
    for f in range(faults):
        large[count] = f
        count = count + (sizes[0, 0, f] > half).astype(jnp.int32)

    def rest(step, carry):
        for u in range(UNROLL):
            place = step * UNROLL + u
            f = large[jnp.minimum(place, count - 1)]
            group = f // 8
            left = lefts[group]
            if not local:

                @pl.when(place < count)
                def _():
                    for copy in beyond(remote, blocks, sems, f):
                        copy.wait()

            above = dot_nt(left[:, half:], blocks[f, :half, half:])
            below = dot_nt(left, blocks[f, half:, :])
            above = above[:8] + above[8:]
            below = below[:8] + below[8:]
            mine = jnp.logical_and(sub == f % 8, place < count)
            for k in range(chunk_half):
                piece = slice(k * LANES, (k + 1) * LANES)
                found[k, group] += jnp.where(mine, above[:, piece], 0.0)
                found[chunk_half + k, group] += jnp.where(mine, below[:, piece], 0.0)
        return carry

    lax.fori_loop(0, (count + UNROLL - 1) // UNROLL, rest, 0)
    parts = [
        jnp.where(live[k], found[k].reshape(faults, LANES), 0.0) for k in range(chunks)
    ]
    parts.append(jnp.zeros((faults, LANES), F32))
    for b in range(7):
        step = 1 << b
        rolled = [pltpu.roll(part, step, 1) for part in parts]
        moved = [
            jnp.where(lane >= step, rolled[k], rolled[k - 1] if k else 0.0)
            for k in range(chunks + 1)
        ]
        parts = [jnp.where(bits[b], new, old) for new, old in zip(moved, parts)]
    count = faults * (chunks + 1)
    for k in range(chunks + 1):
        stack[k * faults : (k + 1) * faults, :] = parts[k]
    depth = stack.shape[0]
    if depth > count:
        stack[count:depth, :] = jnp.zeros((depth - count, LANES), F32)
    return select(chosen[...], stack[...])


def set_field(field, value):
    tiles = value.shape[0]
    field[0:tiles, :] = value
    field[tiles:, :] = jnp.zeros((field.shape[0] - tiles, LANES), F32)


def owner(index, each, count):
    found = jnp.zeros(index.shape, jnp.int32)
    for c in range(1, count):
        found = found + (index >= c * each).astype(jnp.int32)
    return found


def first_kernel(far_sizes, far_rhs, far_friction, remote, send, blocks, *refs):
    plan, (sizes, rhs, friction, column, sems, block_sems, field, *work) = refs[:4], refs[4:]
    tiles = rhs.shape[2] // LANES
    pairs = [(far_sizes, sizes), (far_rhs, rhs), (far_friction, friction)]
    copies = [pltpu.make_async_copy(a, b, sems.at[i]) for i, (a, b) in enumerate(pairs)]
    for copy in copies:
        copy.start()
    for group in range(blocks.shape[0] // 8):
        leading(remote, blocks, block_sems, group).start()
    copies[0].wait()
    scalars = fault_scalars(sizes, blocks.shape[0])
    fetch(scalars, remote, blocks, block_sems)
    make_plan(scalars, plan, column)
    copies[1].wait()
    set_field(field, load_rows(rhs, tiles))
    direction = precondition(sizes, plan, field, blocks, work, remote, block_sems)[0:tiles]
    copies[2].wait()
    value = field[0:tiles, :]
    scaled = load_rows(friction, tiles) * direction
    send[...] = jnp.zeros_like(send)
    send[0:tiles, :] = direction
    send[tiles : tiles + 1, :] = lane_row([total(value * value), total(value * scaled)])


def gathered(parts, tiles):
    whole = parts[0][...]
    for part in parts[1:]:
        whole = whole + part[...]
    return whole[0:tiles], whole[tiles : tiles + 1]


def second_kernel(sizes, rhs, friction, blocks, *refs):
    plan, sent, parts = refs[:4], refs[4], refs[5:-8]
    send, image_out, basis_out, field, *work = refs[-8:]
    tiles = rhs.shape[2] // LANES
    start = load_rows(rhs, tiles)
    diagonal = load_rows(friction, tiles)
    product, sums = gathered(parts, tiles)
    norm2 = pick(sums, 0)
    image = diagonal * sent[0:tiles, :] + product
    scale = lax.rsqrt(norm2)
    value = (image - pick(sums, 1) / norm2 * start) * scale
    image_out[...] = image
    basis_out[0:tiles, :] = value
    basis_out[tiles:, :] = jnp.broadcast_to(norm2, (basis_out.shape[0] - tiles, LANES))
    set_field(field, value)
    direction = precondition(sizes, plan, field, blocks, work)[0:tiles]
    scaled = diagonal * direction
    send[...] = jnp.zeros_like(send)
    send[0:tiles, :] = direction
    send[tiles : tiles + 1, :] = lane_row(
        [
            total(value * value),
            total(start * value) * scale,
            total(start * scaled) * scale,
            total(value * scaled),
        ]
    )


def third_kernel(sizes, rhs, friction, blocks, *refs):
    plan, sent, basis, parts = refs[:4], refs[4], refs[5], refs[6:-7]
    send, image_out, field, *work = refs[-7:]
    tiles = rhs.shape[2] // LANES
    start = load_rows(rhs, tiles)
    diagonal = load_rows(friction, tiles)
    product, sums = gathered(parts, tiles)
    image = diagonal * sent[0:tiles, :] + product
    value = basis[0:tiles, :]
    scale = lax.rsqrt(basis[tiles : tiles + 1, 0:1])
    norm2, cross, along_start, along = [pick(sums, k) for k in range(4)]
    left = norm2 - cross * cross
    usable = left > 1e-5 * norm2
    along = jnp.where(usable, (along - cross * along_start) / jnp.where(usable, left, 1.0), 0.0)
    along_start = along_start - cross * along
    value = (image - along * value - (along_start * scale) * start) * lax.rsqrt(
        jnp.maximum(norm2, 1e-30)
    )
    image_out[...] = image
    set_field(field, value)
    direction = precondition(sizes, plan, field, blocks, work)[0:tiles]
    send[...] = jnp.zeros_like(send)
    send[0:tiles, :] = direction


def fourth_kernel(rhs, friction, sent, image0, image1, *refs):
    parts, (image_out, sums_out) = refs[:-2], refs[-2:]
    tiles = rhs.shape[2] // LANES
    start = load_rows(rhs, tiles)
    product, _ = gathered(parts, tiles)
    image = load_rows(friction, tiles) * sent[0:tiles, :] + product
    image_out[...] = image
    images = [image0[...], image1[...], image]
    values = [total(images[i] * images[j]) for i in range(3) for j in range(i + 1)]
    values += [total(start * one) for one in images]
    sums_out[...] = jnp.broadcast_to(lane_row(values), sums_out.shape)


def last_kernel(sums, rhs, image0, image1, image2, sent0, sent1, sent2, update, residual):
    tiles = rhs.shape[2] // LANES
    row = jnp.sum(sums[...], axis=0, keepdims=True)
    entries = [pick(row, k) for k in range(9)]
    scale = [lax.rsqrt(jnp.maximum(entries[k], 1e-30)) for k in (0, 2, 5)]
    gram = {}
    place = 0
    for i in range(3):
        for j in range(i + 1):
            gram[i, j] = entries[place] * scale[i] * scale[j]
            place += 1
    goal = [entries[6 + i] * scale[i] for i in range(3)]
    low10 = gram[1, 0]
    low20 = gram[2, 0]
    pivot1 = 1.0 - low10 * low10
    keep1 = pivot1 > 1e-6
    inverse1 = jnp.where(keep1, 1.0 / jnp.where(keep1, pivot1, 1.0), 0.0)
    cross = gram[2, 1] - low20 * low10
    low21 = cross * inverse1
    pivot2 = 1.0 - low20 * low20 - cross * low21
    keep2 = pivot2 > 1e-6
    inverse2 = jnp.where(keep2, 1.0 / jnp.where(keep2, pivot2, 1.0), 0.0)
    part1 = goal[1] - low10 * goal[0]
    part2 = goal[2] - low20 * goal[0] - low21 * part1
    weight2 = part2 * inverse2
    weight1 = part1 * inverse1 - low21 * weight2
    weight0 = goal[0] - low10 * weight1 - low20 * weight2
    weights = [weight0 * scale[0], weight1 * scale[1], weight2 * scale[2]]
    start = load_rows(rhs, tiles)
    best = (
        weights[0] * sent0[0:tiles, :]
        + weights[1] * sent1[0:tiles, :]
        + weights[2] * sent2[0:tiles, :]
    )
    rest = start - weights[0] * image0[...] - weights[1] * image1[...] - weights[2] * image2[...]
    for k in range(tiles):
        update[0, :, pl.ds(k * LANES, LANES)] = best[k : k + 1]
        residual[0, :, pl.ds(k * LANES, LANES)] = rest[k : k + 1]


def prepare_kernel(shape, after, counts, tile_row, tile_col, scale, remote, blocks, *refs):
    gather, high, low, sems = refs
    tiles, height, row_count, col_count = shape
    slots = blocks.shape[0]
    pieces = sems.shape[0]
    copies = []
    for p in range(pieces):
        part = pl.ds(p * (slots // pieces), slots // pieces)
        copies.append(
            pltpu.make_async_copy(remote.at[0, 0, part], blocks.at[part], sems.at[p])
        )
        copies[-1].start()
    column = tile_col[0]
    source = owner(column, tiles, row_count)
    spots = (source ^ lax.axis_index("row")) * height + column - source * tiles
    ones = jnp.ones((LANES, LANES), BF16)
    for base in range(0, slots, LANES):
        mine = spots[:, base : base + LANES].astype(F32)
        square = lax.broadcasted_iota(jnp.int32, (LANES, LANES), 0)
        across = lax.broadcasted_iota(jnp.int32, (LANES, LANES), 1)
        square = jnp.where(square == across, mine, 0.0).astype(BF16)
        down = jnp.dot(square, ones, preferred_element_type=F32)[:, 0:1].astype(jnp.int32)
        wide = lax.broadcasted_iota(jnp.int32, (LANES, gather.shape[1]), 1)
        gather[base : base + LANES, :] = (wide == down).astype(BF16)
    row = tile_row[0]
    source = owner(row, tiles, col_count)
    place = source ^ lax.axis_index("col")
    place = (place & 1) * (col_count // 2) + (place >> 1)
    target = place * height + row - source * tiles
    slot = lax.broadcasted_iota(jnp.int32, target.shape, 1)
    weight = jnp.where(slot < counts[0, 0], scale[0], 0.0)
    chosen = jnp.where(lax.broadcasted_iota(jnp.int32, high.shape, 0) == target, weight, 0.0)
    high[...], low[...] = split(chosen)
    for copy in copies:
        copy.wait()


def tiles_kernel(tail, gather, chosen_high, chosen_low, blocks, *refs):
    sent, (keep, give, found, products) = refs[:-4], refs[-4:]
    slots = blocks.shape[0]
    far, height = keep.shape[0], keep.shape[1]
    groups = slots // 16
    field = jnp.concatenate([one[...] for one in sent], axis=0).astype(BF16)
    found[...] = jnp.dot(gather[...], field, preferred_element_type=F32)
    sub = lax.broadcasted_iota(jnp.int32, (8, LANES), 0)
    blank = jnp.zeros((8, LANES), F32)
    for group in range(groups):
        base = group * 16
        top = jnp.concatenate([found[base : base + 8, :], blank], axis=1)
        bottom = jnp.concatenate([blank, found[base + 8 : base + 16, :]], axis=1)
        left = jnp.concatenate([top, bottom], axis=0).astype(BF16)
        first, second = blank, blank
        for p in range(4):
            a, b = base + 2 * p, base + 2 * p + 1
            right = jnp.concatenate(
                [
                    jnp.concatenate([blocks[a], blocks[a + 8]], axis=1),
                    jnp.concatenate([blocks[b], blocks[b + 8]], axis=1),
                ],
                axis=0,
            )
            result = dot_nt(left, right)
            for spot, half in ((2 * p, slice(0, LANES)), (2 * p + 1, slice(LANES, 2 * LANES))):
                first = jnp.where(sub == spot, result[:8, half], first)
                second = jnp.where(sub == spot, result[8:, half], second)
        products[base : base + 8, :] = first
        products[base + 8 : base + 16, :] = second
    high, low = split(products[...])
    value = (
        jnp.dot(chosen_high[...], high, preferred_element_type=F32)
        + jnp.dot(chosen_low[...], high, preferred_element_type=F32)
        + jnp.dot(chosen_high[...], low, preferred_element_type=F32)
    )
    keep[...] = value[: far * height].reshape(far, height, LANES)
    give[...] = value[far * height :].reshape(far, height, LANES)
    last = height - 8
    sums = sent[0][last:height, :]
    for one in sent[1:]:
        sums = sums + one[last:height, :]
    sums = jnp.where(lax.broadcasted_iota(jnp.int32, (8, LANES), 0) == tail, sums, 0.0)
    for k in range(far):
        keep[k, last:height, :] += sums
        give[k, last:height, :] += sums


def scratch(shape, dtype=F32):
    return pltpu.VMEM(shape, dtype)


def local(
    rhs,
    friction,
    kernel_tiles,
    tile_scale,
    tile_row,
    tile_col,
    tile_counts,
    precond_blocks,
    fault_sizes,
):
    length = rhs.shape[2]
    slots = kernel_tiles.shape[2]
    faults, width = precond_blocks.shape[2], precond_blocks.shape[3]
    tiles = length // LANES
    height = (tiles + 8) // 8 * 8
    chunks = width // LANES
    row_count = lax.axis_size("row")
    col_count = lax.axis_size("col")
    far = col_count // 2
    rows = (tiles + chunks + 8) // 8 * 8
    depth = (faults * (chunks + 1) + LANES - 1) // LANES * LANES

    grid = jax.ShapeDtypeStruct((height, LANES), F32)
    plain = jax.ShapeDtypeStruct((tiles, LANES), F32)
    half_grid = jax.ShapeDtypeStruct((far, height, LANES), F32)
    work = [
        scratch((rows, LANES)),
        scratch((depth, LANES)),
        scratch((faults // 8, 16, width), BF16),
        scratch((chunks, faults // 8, 8, LANES)),
        pltpu.SMEM((faults + 1,), jnp.int32),
    ]

    def exchange(value, axis, distance):
        size = lax.axis_size(axis)
        return lax.ppermute(value, axis, [(i, i ^ distance) for i in range(size)])

    def pinned(value):
        return pltpu.with_memory_space_constraint(value, pltpu.HBM)

    sent0, near_blocks, *plan = pl.pallas_call(
        first_kernel,
        out_shape=[
            grid,
            pltpu.VMEM((faults, width, width), BF16),
            jax.ShapeDtypeStruct((rows, depth), BF16),
            jax.ShapeDtypeStruct((depth, rows), BF16),
            jax.ShapeDtypeStruct((faults, LANES), jnp.int32),
            jax.ShapeDtypeStruct((faults, LANES), jnp.int32),
        ],
        in_specs=[HBM] * 4,
        out_specs=[VMEM] * 6,
        scratch_shapes=[
            pltpu.SMEM(fault_sizes.shape, jnp.int32),
            scratch(rhs.shape),
            scratch(friction.shape),
            scratch((depth, LANES), jnp.int32),
            pltpu.SemaphoreType.DMA((3,)),
            pltpu.SemaphoreType.DMA((3, faults)),
        ]
        + work,
        compiler_params=PARAMS,
        name="first",
    )(pinned(fault_sizes), pinned(rhs), pinned(friction), pinned(precond_blocks))
    spread = (2 * far * height, slots)
    near_tiles, *selections = pl.pallas_call(
        functools.partial(prepare_kernel, (tiles, height, row_count, col_count)),
        out_shape=[
            pltpu.VMEM((slots, LANES, LANES), BF16),
            jax.ShapeDtypeStruct((slots, row_count * height), BF16),
            jax.ShapeDtypeStruct(spread, BF16),
            jax.ShapeDtypeStruct(spread, BF16),
        ],
        in_specs=[VMEM, SMEM, VMEM, VMEM, VMEM, HBM],
        out_specs=[VMEM] * 4,
        scratch_shapes=[pltpu.SemaphoreType.DMA((4,))],
        compiler_params=PARAMS,
        name="prepare",
    )(plan[3], tile_counts, tile_row, tile_col, tile_scale, pinned(kernel_tiles))

    def apply_kernel(sent):
        got = [sent] + [exchange(sent, "row", d) for d in range(1, row_count)]
        keep, give = pl.pallas_call(
            functools.partial(tiles_kernel, tiles % 8),
            out_shape=[half_grid, half_grid],
            in_specs=[VMEM] * (4 + row_count),
            out_specs=[VMEM] * 2,
            scratch_shapes=[
                scratch((slots, LANES)),
                scratch((slots, LANES)),
            ],
            compiler_params=PARAMS,
            name="tiles",
        )(*selections, near_tiles, *got)
        both = keep + exchange(give, "col", 1)
        return [both[0]] + [exchange(both[d], "col", 2 * d) for d in range(1, far)]

    parts0 = apply_kernel(sent0)
    sent1, image0, basis = pl.pallas_call(
        second_kernel,
        out_shape=[grid, plain, grid],
        in_specs=[SMEM, VMEM, VMEM, VMEM] + [VMEM] * (5 + far),
        out_specs=[VMEM] * 3,
        scratch_shapes=work,
        compiler_params=PARAMS,
        name="second",
    )(fault_sizes, rhs, friction, near_blocks, *plan, sent0, *parts0)
    parts1 = apply_kernel(sent1)
    sent2, image1 = pl.pallas_call(
        third_kernel,
        out_shape=[grid, plain],
        in_specs=[SMEM, VMEM, VMEM, VMEM] + [VMEM] * (6 + far),
        out_specs=[VMEM] * 2,
        scratch_shapes=work,
        compiler_params=PARAMS,
        name="third",
    )(fault_sizes, rhs, friction, near_blocks, *plan, sent1, basis, *parts1)
    parts2 = apply_kernel(sent2)
    devices = row_count * col_count
    image2, sums = pl.pallas_call(
        fourth_kernel,
        out_shape=[plain, jax.ShapeDtypeStruct((devices, LANES), F32)],
        in_specs=[VMEM] * (5 + far),
        out_specs=[VMEM] * 2,
        compiler_params=PARAMS,
        name="fourth",
    )(rhs, friction, sent2, image0, image1, *parts2)
    sums = lax.all_to_all(sums, ("row", "col"), 0, 0, tiled=True)
    whole = jax.ShapeDtypeStruct((1, 1, length), F32)
    return pl.pallas_call(
        last_kernel,
        out_shape=[whole, whole],
        in_specs=[VMEM] * 8,
        out_specs=[VMEM] * 2,
        compiler_params=PARAMS,
        name="last",
    )(sums, rhs, image0, image1, image2, sent0, sent1, sent2)


def solution(mesh):
    return jax.shard_map(
        local,
        mesh=mesh,
        in_specs=(
            P("row", "col", None),
            P("row", "col", None),
            P("row", "col", None, None, None),
            P("row", "col", None),
            P("row", "col", None),
            P("row", "col", None),
            P("row", "col"),
            P("row", "col", None, None, None),
            P("row", "col", None),
        ),
        out_specs=(P("row", "col", None), P("row", "col", None)),
        check_vma=False,
    )
```
